128 devices in a mesh: expert: 4 (over z), seq: 4 (over y), tensor: 8 (over x, core).
Axes of the slice: x: 4, y: 4, z: 4, core: 2. Of those that a mesh axis runs over, the one named last changes fastest.
Arguments:
- tokens: bfloat16 [3072, 7168], P(('expert', 'seq')), may hold values from -6 to 6
- grad_out: bfloat16 [3072, 7168], P(('expert', 'seq')), may hold values from -6 to 6
- expert_ids: int32 [3072, 2], P(('expert', 'seq')), may hold values from 0 to 3, all different within a row; in each aligned block of 192 rows (0 to 191, 192 to 383, ...) at most 128 rows name the same one
- route_weights: bfloat16 [3072, 2], P(('expert', 'seq')), may hold values from 0.099609375 to 1
- gate_weight: bfloat16 [4, 7168, 2048], P('expert', 'seq', 'tensor'), may hold values from -0.0625 to 0.0625
- up_weight: bfloat16 [4, 7168, 2048], P('expert', 'seq', 'tensor'), may hold values from -0.0625 to 0.0625
- down_weight: bfloat16 [4, 7168, 2048], P('expert', 'seq', 'tensor'), may hold values from -0.125 to 0.125
Outputs:
- grad_tokens: bfloat16 [3072, 7168], P(('expert', 'seq'), 'tensor')
- grad_route: float32 [3072, 2], P(('expert', 'seq'))
- grad_gate: float32 [4, 7168, 2048], P('expert', 'seq', 'tensor')
- grad_up: float32 [4, 7168, 2048], P('expert', 'seq', 'tensor')
- grad_down: float32 [4, 7168, 2048], P('expert', 'seq', 'tensor')
The draws below stay inside these ranges and needn't reach their ends.
Inputs may be any that keep to these rules, and one draw needn't show every extreme that they name: `expert_ids`: the two ids of a row differ. Within each aligned block of 192 rows (the tokens of one group of the expert and seq axes) no expert is named by more than 128 rows, and in some block an expert is named by exactly 128 rows.
All inputs are finite; a program needn't handle non-finite values.
Results may differ from the reference program's by a relative error of at most 0.019.
Values may be sent and summed in bfloat16 or wider, within the bound.
A program may use at most 192 MiB of HBM per device.

```python
import math
import jax
import jax.numpy as jnp
import numpy as np
from jax import lax

D = 7168
FF = 2048
TOK_DEV = 192
EXPERTS = 4
CAP = 128
TOKENS = 3072
N_TENSOR = 8


def levels(rng, shape, pieces, least, high):
    def one(position, parts):
        steps = jax.random.uniform(jax.random.fold_in(jax.random.fold_in(rng, 6), position), (parts,), jnp.float32, least / len(pieces), high / len(pieces))
        return jnp.repeat(jnp.exp(steps), shape[position] // parts).reshape((-1,) + (1,) * (len(shape) - position - 1))

    loudness = one(*pieces[0])
    for cut in pieces[1:]:
        loudness = loudness * one(*cut)
    return loudness


def routed_block(rng, own, number, rows, amount, top, limit, skew):
    order = jax.random.permutation(rng, amount)
    heavy_load, ordinary = portions_of(amount, rows * top, limit, skew, True), portions_of(amount, rows * top, limit, skew, False)
    places = jnp.arange(amount)

    def named(sizes, turn):
        used = int((sizes > 0).sum())
        fixed = max(1, used // 4)
        moved = fixed + (places - fixed + turn * (used - fixed)) % max(1, amount - fixed)
        return jnp.zeros((amount,), jnp.int32).at[order[jnp.where(places < fixed, places, moved)]].set(jnp.asarray(sizes, jnp.int32))

    sizes = jnp.where(number % 4 == 0, named(heavy_load, number // 4), named(ordinary, number - number // 4 - 1))
    mixed = jax.random.permutation(jax.random.fold_in(own, 3), amount)
    donor, receiver = mixed[0:amount // 2 * 2:2], mixed[1:amount // 2 * 2:2]
    margin = jnp.minimum(sizes[donor] - 1, limit - sizes[receiver]) // 2
    margin = jnp.where((donor == order[0]) | (receiver == order[0]) | (sizes[receiver] == 0), 0, jnp.maximum(margin, 0))
    moved = jax.random.randint(jax.random.fold_in(own, 4), (amount // 2,), 0, 1 << 20) % (margin + 1)
    sizes = sizes.at[donor].add(-moved).at[receiver].add(moved)
    items = jnp.searchsorted(jnp.cumsum(sizes), jnp.arange(rows * top), side="right").astype(jnp.int32)
    grid = items.reshape(top, rows).T
    grid = grid[jax.random.permutation(jax.random.fold_in(own, 1), rows)]
    turn = jax.random.randint(jax.random.fold_in(own, 2), (rows, 1), 0, top)
    return jnp.take_along_axis(grid, (jnp.arange(top)[None, :] + turn) % top, axis=1)


def portions_of(count, total, limit, lean, full):
    portions = [(1 << 20) // math.isqrt(grade ** lean) + 1 for grade in range(1, count + 1)]
    largest = limit if full else min(limit, max(-(-total // count), total * portions[0] // sum(portions)))
    least = 1 if total - largest >= count - 1 else 0
    given, spare = [largest] + [least] * (count - 1), total - largest - least * (count - 1)
    while spare > 0:
        candidates = [i for i in range(1, count) if given[i] < largest] or [i for i in range(1, count) if given[i] < limit]
        pool, left = sum([portions[i] for i in candidates]), spare
        for i in candidates:
            extra = min(limit - given[i], max(1, left * portions[i] // pool), spare)
            given[i] = given[i] + extra
            spare = spare - extra
    return np.array(given)


def bell_draw(rng, extent, deviation, bound, split=(), kind=jnp.bfloat16):
    level = levels(rng, extent, split, -0.22, 0.18) if split else 1.0
    array = jax.random.normal(rng, extent, jnp.float32) * deviation * level
    return jnp.minimum(jnp.maximum(array, -bound), bound).astype(kind)


def setup_inputs(seed: int = 0) -> dict:
    seeds = jax.random.split(jax.random.key(seed), 8)
    tokens = bell_draw(seeds[0], (TOKENS, D), 1.0, 6.0, ((0, 16),))
    grad_out = bell_draw(seeds[1], (TOKENS, D), 1.0, 6.0, ((0, 16),))
    expert_ids_keys = jax.random.split(jax.random.fold_in(seeds[2], 1), TOKENS // TOK_DEV)
    expert_ids_turns = jax.random.permutation(jax.random.fold_in(seeds[2], 3), TOKENS // TOK_DEV)
    expert_ids = jax.vmap(lambda own, number: routed_block(jax.random.fold_in(seeds[2], 2), own, number, TOK_DEV, EXPERTS, 2, CAP, 2))(expert_ids_keys, expert_ids_turns).reshape((TOKENS, 2))
    route_weights = jnp.clip(jnp.exp(math.log(1.0) - 2.306499 * jax.random.uniform(seeds[3], (TOKENS, 2), jnp.float32) ** levels(seeds[3], (TOKENS, 2), ((0, 16),), -0.2, 0.2)), 0.099609375, 1.0).astype(jnp.bfloat16)
    gate_weight = bell_draw(seeds[4], (EXPERTS, D, FF), D ** -0.5, 0.0625, ((0, 4), (1, 4), (2, 8)))
    up_weight = bell_draw(seeds[5], (EXPERTS, D, FF), D ** -0.5, 0.0625, ((0, 4), (1, 4), (2, 8)))
    down_weight = bell_draw(seeds[6], (EXPERTS, D, FF), FF ** -0.5, 0.125, ((0, 4), (1, 4), (2, 8)))
    return dict(tokens=tokens, grad_out=grad_out, expert_ids=expert_ids, route_weights=route_weights, gate_weight=gate_weight, up_weight=up_weight, down_weight=down_weight)


def contract_rows(left, right):
    return lax.dot_general(left, right, (((0,), (0,)), ((), ())), preferred_element_type=jnp.float32)


def contract_units(left, right):
    return lax.dot_general(left, right, (((1,), (1,)), ((), ())), preferred_element_type=jnp.float32)


def reference(tokens, grad_out, expert_ids, route_weights, gate_weight, up_weight, down_weight):
    most_rows = (TOKENS // TOK_DEV) * CAP
    group_width = FF // N_TENSOR
    flat_ids = expert_ids.reshape(-1)
    flat_prob = route_weights.reshape(-1).astype(jnp.float32)
    route_terms = jnp.zeros((2 * TOKENS, D), jnp.float32)
    route_scores = jnp.zeros((2 * TOKENS,), jnp.float32)
    gate_grads = []
    up_grads = []
    down_grads = []
    for expert in range(EXPERTS):
        chosen = flat_ids == expert
        picked = jnp.nonzero(chosen, size=most_rows, fill_value=0)[0].astype(jnp.int32)
        chosen_total = jnp.sum(chosen.astype(jnp.int32))
        present = jnp.arange(most_rows, dtype=jnp.int32) < chosen_total
        token_rows = picked // 2
        in_rows = tokens[token_rows] * present[:, None].astype(tokens.dtype)
        out_rows = grad_out[token_rows] * present[:, None].astype(grad_out.dtype)
        prob_rows = (flat_prob[picked] * present.astype(jnp.float32))[:, None]
        gate_mat = gate_weight[expert]
        up_mat = up_weight[expert]
        down_mat = down_weight[expert]
        pre_gate = jnp.dot(in_rows, gate_mat, preferred_element_type=jnp.float32)
        pre_up = jnp.dot(in_rows, up_mat, preferred_element_type=jnp.float32)
        sigmoid_gate = jax.nn.sigmoid(pre_gate)
        silu_gate = pre_gate * sigmoid_gate
        hidden = silu_gate * pre_up
        hidden_low = hidden.astype(jnp.bfloat16)
        back_proj = jnp.dot(out_rows, down_mat, preferred_element_type=jnp.float32)
        scores = jnp.sum(hidden * back_proj, axis=1)
        scaled = (prob_rows * out_rows.astype(jnp.float32)).astype(jnp.bfloat16)
        hidden_grad = prob_rows * back_proj
        up_grad = (hidden_grad * silu_gate).astype(jnp.bfloat16)
        gate_grad = (hidden_grad * pre_up * sigmoid_gate * (1.0 + pre_gate * (1.0 - sigmoid_gate))).astype(jnp.bfloat16)
        gate_grads.append(contract_rows(in_rows, gate_grad))
        up_grads.append(contract_rows(in_rows, up_grad))
        down_grads.append(contract_rows(scaled, hidden_low))
        summed = jnp.zeros((most_rows, D), jnp.float32)
        for group_index in range(N_TENSOR):
            first = group_index * group_width
            piece_sum = contract_units(gate_grad[:, first:first + group_width], gate_mat[:, first:first + group_width])
            piece_sum = piece_sum + contract_units(up_grad[:, first:first + group_width], up_mat[:, first:first + group_width])
            summed = summed + lax.optimization_barrier(piece_sum.astype(jnp.bfloat16)).astype(jnp.float32)
        summed = summed * present[:, None].astype(jnp.float32)
        route_terms = route_terms.at[picked].add(summed)
        route_scores = route_scores.at[picked].add(scores * present.astype(jnp.float32))
    grad_tokens = jnp.sum(route_terms.reshape(TOKENS, 2, D), axis=1).astype(jnp.bfloat16)
    grad_route = route_scores.reshape(TOKENS, 2)
    return (grad_tokens, grad_route, jnp.stack(gate_grads), jnp.stack(up_grads), jnp.stack(down_grads))
```

```python
import jax
import jax.numpy as jnp
from jax import lax
from jax.sharding import PartitionSpec as P


def shards(tokens, grad_out, expert_ids, route_weights, gate_weight, up_weight, down_weight):
    expert_count = lax.axis_size("expert")
    seq_count = lax.axis_size("seq")
    tensor_count = lax.axis_size("tx") * lax.axis_size("core")
    core = lax.axis_index("core")
    local_count = gate_weight.shape[0]
    tok_rows = tokens.shape[0]
    model_width = tokens.shape[1]
    part_width = model_width // tensor_count
    per_peer = tok_rows // 6
    peer_count = expert_count * seq_count
    block_rows = local_count * per_peer
    slot_count = peer_count * block_rows
    flat_ids = expert_ids.reshape(-1)
    route_count = flat_ids.shape[0]
    onehot = (
        flat_ids[:, None] == jnp.arange(local_count * expert_count, dtype=jnp.int32)[None, :]
    ).astype(jnp.int32)
    before = jnp.cumsum(onehot, axis=0) - onehot
    ranking = jnp.sum(before * onehot, axis=1)
    local_expert = flat_ids % local_count
    dest_peer = flat_ids // local_count * seq_count + ranking % seq_count
    target = (dest_peer * local_count + local_expert) * per_peer + ranking // seq_count
    source = (
        jnp.full((slot_count,), -1, jnp.int32)
        .at[target]
        .set(jnp.arange(route_count, dtype=jnp.int32))
    )
    filled = source >= 0
    safe_source = jnp.maximum(source, 0)
    token_of = safe_source // 2
    keep = filled[:, None].astype(tokens.dtype)
    weight_send = (
        route_weights.reshape(-1)[safe_source] * filled.astype(route_weights.dtype)
    ).reshape(peer_count, block_rows)
    half = model_width // 2
    tokens_half = lax.dynamic_slice_in_dim(tokens, core * half, half, axis=1)
    grad_half = lax.dynamic_slice_in_dim(grad_out, core * half, half, axis=1)
    in_send = (tokens_half[token_of] * keep).reshape(peer_count, block_rows, half)
    out_send = (grad_half[token_of] * keep).reshape(peer_count, block_rows, half)
    in_mine, out_mine, weight_recv = (
        lax.all_to_all(in_send, ("expert", "seq"), split_axis=0, concat_axis=0, tiled=True),
        lax.all_to_all(out_send, ("expert", "seq"), split_axis=0, concat_axis=0, tiled=True),
        lax.all_to_all(weight_send, ("expert", "seq"), split_axis=0, concat_axis=0, tiled=True),
    )

    def join_halves(mine):
        other = lax.ppermute(mine, "core", [(0, 1), (1, 0)])
        first = jnp.where(core == 0, mine, other)
        second = jnp.where(core == 0, other, mine)
        return jnp.concatenate([first, second], axis=-1)

    in_recv = join_halves(in_mine)
    out_recv = join_halves(out_mine)

    def by_expert(values):
        shaped = values.reshape((peer_count, local_count, per_peer) + values.shape[2:])
        return jnp.swapaxes(shaped, 0, 1).reshape(
            (local_count, peer_count * per_peer) + values.shape[2:]
        )

    def by_peer(values):
        shaped = values.reshape((local_count, peer_count, per_peer) + values.shape[2:])
        return jnp.swapaxes(shaped, 0, 1).reshape((peer_count, block_rows) + values.shape[2:])

    in_rows = by_expert(in_recv)
    out_rows = by_expert(out_recv)
    prob = by_expert(weight_recv).astype(jnp.float32)[:, :, None]
    gate_full, up_full, down_full = (
        lax.all_gather(gate_weight, "seq", axis=1, tiled=True),
        lax.all_gather(up_weight, "seq", axis=1, tiled=True),
        lax.all_gather(down_weight, "seq", axis=1, tiled=True),
    )
    pre_gate = jnp.einsum("emd,edf->emf", in_rows, gate_full, preferred_element_type=jnp.float32)
    pre_up = jnp.einsum("emd,edf->emf", in_rows, up_full, preferred_element_type=jnp.float32)
    sigmoid_gate = jax.nn.sigmoid(pre_gate)
    silu_gate = pre_gate * sigmoid_gate
    hidden = silu_gate * pre_up
    hidden_low = hidden.astype(jnp.bfloat16)
    back_proj = jnp.einsum("emd,edf->emf", out_rows, down_full, preferred_element_type=jnp.float32)
    partial_scores = jnp.sum(hidden * back_proj, axis=2)
    scaled = (prob * out_rows.astype(jnp.float32)).astype(jnp.bfloat16)
    hidden_grad = prob * back_proj
    up_grad = (hidden_grad * silu_gate).astype(jnp.bfloat16)
    gate_grad = (
        hidden_grad * pre_up * sigmoid_gate * (1.0 + pre_gate * (1.0 - sigmoid_gate))
    ).astype(jnp.bfloat16)
    input_terms = jnp.einsum(
        "emf,edf->emd", gate_grad, gate_full, preferred_element_type=jnp.float32
    )
    input_terms = input_terms + jnp.einsum(
        "emf,edf->emd", up_grad, up_full, preferred_element_type=jnp.float32
    )
    route_scores = lax.psum(partial_scores, ("tx", "core"))
    input_shards = lax.psum_scatter(
        input_terms.astype(jnp.bfloat16), ("tx", "core"), scatter_dimension=2, tiled=True
    ).astype(jnp.float32)
    back_rows, back_scores = (
        lax.all_to_all(
            by_peer(input_shards).astype(jnp.bfloat16),
            ("expert", "seq"),
            split_axis=0,
            concat_axis=0,
            tiled=True,
        ).astype(jnp.float32),
        lax.all_to_all(
            by_peer(route_scores).astype(jnp.bfloat16),
            ("expert", "seq"),
            split_axis=0,
            concat_axis=0,
            tiled=True,
        ).astype(jnp.float32),
    )
    route_rows = back_rows.reshape(slot_count, part_width)[target].reshape(tok_rows, 2, part_width)
    grad_tokens = jnp.sum(route_rows, axis=1).astype(jnp.bfloat16)
    grad_route = back_scores.reshape(slot_count)[target].reshape(tok_rows, 2)
    gate_part = jnp.einsum("emd,emf->edf", in_rows, gate_grad, preferred_element_type=jnp.float32)
    up_part = jnp.einsum("emd,emf->edf", in_rows, up_grad, preferred_element_type=jnp.float32)
    down_part = jnp.einsum("emd,emf->edf", scaled, hidden_low, preferred_element_type=jnp.float32)
    grad_gate, grad_up, grad_down = (
        lax.psum_scatter(
            gate_part.astype(jnp.bfloat16), "seq", scatter_dimension=1, tiled=True
        ).astype(jnp.float32),
        lax.psum_scatter(
            up_part.astype(jnp.bfloat16), "seq", scatter_dimension=1, tiled=True
        ).astype(jnp.float32),
        lax.psum_scatter(
            down_part.astype(jnp.bfloat16), "seq", scatter_dimension=1, tiled=True
        ).astype(jnp.float32),
    )
    return (grad_tokens, grad_route, grad_gate, grad_up, grad_down)


def solution(mesh):
    shape = mesh.devices.shape
    mesh = jax.sharding.Mesh(
        mesh.devices.reshape(shape[0], shape[1], shape[2] // 2, 2), ("expert", "seq", "tx", "core")
    )
    tensor = ("tx", "core")
    placed = (
        P(("expert", "seq"), None),
        P(("expert", "seq"), None),
        P(("expert", "seq"), None),
        P(("expert", "seq"), None),
        P("expert", "seq", tensor),
        P("expert", "seq", tensor),
        P("expert", "seq", tensor),
    )
    return jax.shard_map(
        shards,
        mesh=mesh,
        in_specs=placed,
        out_specs=(
            P(("expert", "seq"), tensor),
            P(("expert", "seq"), None),
            P("expert", "seq", tensor),
            P("expert", "seq", tensor),
            P("expert", "seq", tensor),
        ),
        check_vma=False,
    )
```

```python
import jax
import jax.numpy as jnp
from jax import lax
from jax.sharding import PartitionSpec as P


def shards(tokens, grad_out, expert_ids, route_weights, gate_weight, up_weight, down_weight):
    expert_count = lax.axis_size("expert")
    seq_count = lax.axis_size("seq")
    tensor_count = lax.axis_size("tx") * lax.axis_size("core")
    core = lax.axis_index("core")
    local_count = gate_weight.shape[0]
    tok_rows = tokens.shape[0]
    model_width = tokens.shape[1]
    part_width = model_width // tensor_count
    per_peer = tok_rows // 6
    peer_count = expert_count * seq_count
    block_rows = local_count * per_peer
    slot_count = peer_count * block_rows
    flat_ids = expert_ids.reshape(-1)
    route_count = flat_ids.shape[0]
    onehot = (
        flat_ids[:, None] == jnp.arange(local_count * expert_count, dtype=jnp.int32)[None, :]
    ).astype(jnp.int32)
    before = jnp.cumsum(onehot, axis=0) - onehot
    ranking = jnp.sum(before * onehot, axis=1)
    local_expert = flat_ids % local_count
    dest_peer = flat_ids // local_count * seq_count + ranking % seq_count
    target = (dest_peer * local_count + local_expert) * per_peer + ranking // seq_count
    source = (
        jnp.full((slot_count,), -1, jnp.int32)
        .at[target]
        .set(jnp.arange(route_count, dtype=jnp.int32))
    )
    filled = source >= 0
    safe_source = jnp.maximum(source, 0)
    token_of = safe_source // 2
    keep = filled[:, None].astype(tokens.dtype)
    weight_send = (
        route_weights.reshape(-1)[safe_source] * filled.astype(route_weights.dtype)
    ).reshape(peer_count, block_rows)
    half = model_width // 2
    tokens_half = lax.dynamic_slice_in_dim(tokens, core * half, half, axis=1)
    grad_half = lax.dynamic_slice_in_dim(grad_out, core * half, half, axis=1)
    in_send = (tokens_half[token_of] * keep).reshape(peer_count, block_rows, half)
    out_send = (grad_half[token_of] * keep).reshape(peer_count, block_rows, half)
    in_mine, out_mine, weight_recv = (
        lax.all_to_all(in_send, ("expert", "seq"), split_axis=0, concat_axis=0, tiled=True),
        lax.all_to_all(out_send, ("expert", "seq"), split_axis=0, concat_axis=0, tiled=True),
        lax.all_to_all(weight_send, ("expert", "seq"), split_axis=0, concat_axis=0, tiled=True),
    )

    def join_halves(mine):
        both = jnp.broadcast_to(mine[None], (2,) + mine.shape)
        return lax.all_to_all(both, "core", split_axis=0, concat_axis=0, tiled=True)

    def by_expert(values):
        shaped = values.reshape((peer_count, local_count, per_peer) + values.shape[2:])
        return jnp.swapaxes(shaped, 0, 1).reshape(
            (local_count, peer_count * per_peer) + values.shape[2:]
        )

    def by_peer(values):
        shaped = values.reshape((local_count, peer_count, per_peer) + values.shape[2:])
        return jnp.swapaxes(shaped, 0, 1).reshape((peer_count, block_rows) + values.shape[2:])

    in_rows = jax.vmap(by_expert)(join_halves(in_mine))
    out_rows = jax.vmap(by_expert)(join_halves(out_mine))
    prob = by_expert(weight_recv).astype(jnp.float32)[:, :, None]
    gate_full, up_full, down_full = (
        lax.all_gather(gate_weight, "seq", axis=1, tiled=True),
        lax.all_gather(up_weight, "seq", axis=1, tiled=True),
        lax.all_gather(down_weight, "seq", axis=1, tiled=True),
    )
    hidden_count = gate_full.shape[2]
    gate_h, up_h, down_h = (
        w.reshape(local_count, 2, half, hidden_count) for w in (gate_full, up_full, down_full)
    )
    pre_gate = jnp.einsum("cemd,ecdf->emf", in_rows, gate_h, preferred_element_type=jnp.float32)
    pre_up = jnp.einsum("cemd,ecdf->emf", in_rows, up_h, preferred_element_type=jnp.float32)
    sigmoid_gate = jax.nn.sigmoid(pre_gate)
    silu_gate = pre_gate * sigmoid_gate
    hidden = silu_gate * pre_up
    hidden_low = hidden.astype(jnp.bfloat16)
    back_proj = jnp.einsum("cemd,ecdf->emf", out_rows, down_h, preferred_element_type=jnp.float32)
    partial_scores = jnp.sum(hidden * back_proj, axis=2)
    scaled = (prob[None] * out_rows.astype(jnp.float32)).astype(jnp.bfloat16)
    hidden_grad = prob * back_proj
    up_grad = (hidden_grad * silu_gate).astype(jnp.bfloat16)
    gate_grad = (
        hidden_grad * pre_up * sigmoid_gate * (1.0 + pre_gate * (1.0 - sigmoid_gate))
    ).astype(jnp.bfloat16)
    input_terms = jnp.einsum(
        "emf,ecdf->ecdm", gate_grad, gate_h, preferred_element_type=jnp.float32
    )
    input_terms = input_terms + jnp.einsum(
        "emf,ecdf->ecdm", up_grad, up_h, preferred_element_type=jnp.float32
    )
    rows_here = local_count * slot_count
    input_terms = jnp.swapaxes(
        input_terms.reshape(local_count, tensor_count, part_width, slot_count), 0, 1
    ).reshape(tensor_count, part_width, rows_here)
    score_pad = 16
    score_rows = jnp.zeros((tensor_count, score_pad, rows_here), jnp.float32)
    score_rows = score_rows.at[:, 0, :].set(partial_scores.reshape(1, rows_here))
    stacked = jnp.concatenate([input_terms, score_rows], axis=1).astype(jnp.bfloat16)
    reduced = lax.psum_scatter(
        stacked.reshape(tensor_count * (part_width + score_pad), rows_here),
        ("tx", "core"),
        scatter_dimension=0,
        tiled=True,
    )
    back_send = by_peer(
        jnp.swapaxes(reduced, 0, 1).reshape(local_count, slot_count, part_width + score_pad)
    )
    back_all = lax.all_to_all(
        back_send, ("expert", "seq"), split_axis=0, concat_axis=0, tiled=True
    ).astype(jnp.float32)
    back_all = back_all.reshape(slot_count, part_width + score_pad)[target]
    route_rows = back_all[:, :part_width].reshape(tok_rows, 2, part_width)
    grad_tokens = jnp.sum(route_rows, axis=1).astype(jnp.bfloat16)
    grad_route = back_all[:, part_width].reshape(tok_rows, 2)
    gate_part = jnp.einsum("cemd,emf->ecdf", in_rows, gate_grad, preferred_element_type=jnp.float32)
    up_part = jnp.einsum("cemd,emf->ecdf", in_rows, up_grad, preferred_element_type=jnp.float32)
    down_part = jnp.einsum("cemd,emf->ecdf", scaled, hidden_low, preferred_element_type=jnp.float32)
    grad_gate, grad_up, grad_down = (
        lax.psum_scatter(
            part.reshape(local_count, model_width, hidden_count).astype(jnp.bfloat16),
            "seq",
            scatter_dimension=1,
            tiled=True,
        ).astype(jnp.float32)
        for part in (gate_part, up_part, down_part)
    )
    return (grad_tokens, grad_route, grad_gate, grad_up, grad_down)


def solution(mesh):
    shape = mesh.devices.shape
    mesh = jax.sharding.Mesh(
        mesh.devices.reshape(shape[0], shape[1], shape[2] // 2, 2), ("expert", "seq", "tx", "core")
    )
    tensor = ("tx", "core")
    placed = (
        P(("expert", "seq"), None),
        P(("expert", "seq"), None),
        P(("expert", "seq"), None),
        P(("expert", "seq"), None),
        P("expert", "seq", tensor),
        P("expert", "seq", tensor),
        P("expert", "seq", tensor),
    )
    return jax.shard_map(
        shards,
        mesh=mesh,
        in_specs=placed,
        out_specs=(
            P(("expert", "seq"), tensor),
            P(("expert", "seq"), None),
            P("expert", "seq", tensor),
            P("expert", "seq", tensor),
            P("expert", "seq", tensor),
        ),
        check_vma=False,
    )
```

```python
import jax
import jax.numpy as jnp
from jax import lax
from jax.sharding import PartitionSpec as P


def shards(tokens, grad_out, expert_ids, route_weights, gate_weight, up_weight, down_weight):
    expert_count = lax.axis_size("expert")
    seq_count = lax.axis_size("seq")
    tensor_count = lax.axis_size("tx") * lax.axis_size("core")
    core = lax.axis_index("core")
    local_count = gate_weight.shape[0]
    tok_rows = tokens.shape[0]
    model_width = tokens.shape[1]
    part_width = model_width // tensor_count
    per_peer = tok_rows // 6
    peer_count = expert_count * seq_count
    block_rows = local_count * per_peer
    slot_count = peer_count * block_rows
    flat_ids = expert_ids.reshape(-1)
    route_count = flat_ids.shape[0]
    onehot = (
        flat_ids[:, None] == jnp.arange(local_count * expert_count, dtype=jnp.int32)[None, :]
    ).astype(jnp.int32)
    before = jnp.cumsum(onehot, axis=0) - onehot
    ranking = jnp.sum(before * onehot, axis=1)
    local_expert = flat_ids % local_count
    dest_peer = flat_ids // local_count * seq_count + ranking % seq_count
    target = (dest_peer * local_count + local_expert) * per_peer + ranking // seq_count
    source = (
        jnp.full((slot_count,), -1, jnp.int32)
        .at[target]
        .set(jnp.arange(route_count, dtype=jnp.int32))
    )
    filled = source >= 0
    safe_source = jnp.maximum(source, 0)
    token_of = safe_source // 2
    keep = filled[:, None].astype(tokens.dtype)
    weight_send = (
        route_weights.reshape(-1)[safe_source] * filled.astype(route_weights.dtype)
    ).reshape(peer_count, block_rows)
    half = model_width // 2
    tokens_half = lax.dynamic_slice_in_dim(tokens, core * half, half, axis=1)
    grad_half = lax.dynamic_slice_in_dim(grad_out, core * half, half, axis=1)
    in_send = (tokens_half[token_of] * keep).reshape(peer_count, block_rows, half)
    out_send = (grad_half[token_of] * keep).reshape(peer_count, block_rows, half)
    in_mine, out_mine, weight_recv = (
        lax.all_to_all(in_send, ("expert", "seq"), split_axis=0, concat_axis=0, tiled=True),
        lax.all_to_all(out_send, ("expert", "seq"), split_axis=0, concat_axis=0, tiled=True),
        lax.all_to_all(weight_send, ("expert", "seq"), split_axis=0, concat_axis=0, tiled=True),
    )

    def join_halves(mine):
        both = jnp.broadcast_to(mine[None], (2,) + mine.shape)
        return lax.all_to_all(both, "core", split_axis=0, concat_axis=0, tiled=True)

    def by_expert(values):
        shaped = values.reshape((peer_count, local_count, per_peer) + values.shape[2:])
        return jnp.swapaxes(shaped, 0, 1).reshape(
            (local_count, peer_count * per_peer) + values.shape[2:]
        )

    def by_peer(values):
        shaped = values.reshape((local_count, peer_count, per_peer) + values.shape[2:])
        return jnp.swapaxes(shaped, 0, 1).reshape((peer_count, block_rows) + values.shape[2:])

    in_rows = jax.vmap(by_expert)(join_halves(in_mine))
    out_rows = jax.vmap(by_expert)(join_halves(out_mine))
    prob = by_expert(weight_recv).astype(jnp.float32)[:, :, None]
    weights = lax.all_gather(
        jnp.stack([gate_weight, up_weight, down_weight]), "seq", axis=2, tiled=True
    )
    gate_full, up_full, down_full = weights[0], weights[1], weights[2]
    hidden_count = gate_full.shape[2]
    gate_h, up_h, down_h = (
        w.reshape(local_count, 2, half, hidden_count) for w in (gate_full, up_full, down_full)
    )
    pre_gate = jnp.einsum("cemd,ecdf->emf", in_rows, gate_h, preferred_element_type=jnp.float32)
    pre_up = jnp.einsum("cemd,ecdf->emf", in_rows, up_h, preferred_element_type=jnp.float32)
    sigmoid_gate = jax.nn.sigmoid(pre_gate)
    silu_gate = pre_gate * sigmoid_gate
    hidden = silu_gate * pre_up
    hidden_low = hidden.astype(jnp.bfloat16)
    back_proj = jnp.einsum("cemd,ecdf->emf", out_rows, down_h, preferred_element_type=jnp.float32)
    partial_scores = jnp.sum(hidden * back_proj, axis=2)
    scaled = (prob[None] * out_rows.astype(jnp.float32)).astype(jnp.bfloat16)
    hidden_grad = prob * back_proj
    up_grad = (hidden_grad * silu_gate).astype(jnp.bfloat16)
    gate_grad = (
        hidden_grad * pre_up * sigmoid_gate * (1.0 + pre_gate * (1.0 - sigmoid_gate))
    ).astype(jnp.bfloat16)
    gate_part = jnp.einsum("cemd,emf->ecdf", in_rows, gate_grad, preferred_element_type=jnp.float32)
    up_part = jnp.einsum("cemd,emf->ecdf", in_rows, up_grad, preferred_element_type=jnp.float32)
    down_part = jnp.einsum("cemd,emf->ecdf", scaled, hidden_low, preferred_element_type=jnp.float32)
    parts = jnp.stack([gate_part, up_part, down_part]).reshape(
        3, local_count, model_width, hidden_count
    ).astype(jnp.bfloat16)
    parts, gate_grad, up_grad = lax.optimization_barrier((parts, gate_grad, up_grad))
    reduced_parts = lax.psum_scatter(parts, "seq", scatter_dimension=2, tiled=True).astype(jnp.float32)
    grad_gate, grad_up, grad_down = reduced_parts[0], reduced_parts[1], reduced_parts[2]
    input_terms = jnp.einsum(
        "emf,ecdf->ecdm", gate_grad, gate_h, preferred_element_type=jnp.float32
    )
    input_terms = input_terms + jnp.einsum(
        "emf,ecdf->ecdm", up_grad, up_h, preferred_element_type=jnp.float32
    )
    rows_here = local_count * slot_count
    input_terms = jnp.swapaxes(
        input_terms.reshape(local_count, tensor_count, part_width, slot_count), 0, 1
    ).reshape(tensor_count, part_width, rows_here)
    score_pad = 16
    score_rows = jnp.zeros((tensor_count, score_pad, rows_here), jnp.float32)
    score_rows = score_rows.at[:, 0, :].set(partial_scores.reshape(1, rows_here))
    stacked = jnp.concatenate([input_terms, score_rows], axis=1).astype(jnp.bfloat16)
    tx_count = lax.axis_size("tx")
    stacked = stacked.reshape(tx_count, 2, part_width + score_pad, rows_here)
    pair = lax.all_to_all(stacked, "core", split_axis=1, concat_axis=1, tiled=True)
    pair = jnp.sum(pair.astype(jnp.float32), axis=1).astype(jnp.bfloat16)
    ring = lax.all_to_all(pair, "tx", split_axis=0, concat_axis=0, tiled=True)
    reduced = jnp.sum(ring.astype(jnp.float32), axis=0).astype(jnp.bfloat16)
    back_send = by_peer(
        jnp.swapaxes(reduced, 0, 1).reshape(local_count, slot_count, part_width + score_pad)
    )
    back_all = lax.all_to_all(
        back_send, ("expert", "seq"), split_axis=0, concat_axis=0, tiled=True
    ).astype(jnp.float32)
    back_all = back_all.reshape(slot_count, part_width + score_pad)[target]
    route_rows = back_all[:, :part_width].reshape(tok_rows, 2, part_width)
    grad_tokens = jnp.sum(route_rows, axis=1).astype(jnp.bfloat16)
    grad_route = back_all[:, part_width].reshape(tok_rows, 2)
    return (grad_tokens, grad_route, grad_gate, grad_up, grad_down)


def solution(mesh):
    shape = mesh.devices.shape
    mesh = jax.sharding.Mesh(
        mesh.devices.reshape(shape[0], shape[1], shape[2] // 2, 2), ("expert", "seq", "tx", "core")
    )
    tensor = ("tx", "core")
    placed = (
        P(("expert", "seq"), None),
        P(("expert", "seq"), None),
        P(("expert", "seq"), None),
        P(("expert", "seq"), None),
        P("expert", "seq", tensor),
        P("expert", "seq", tensor),
        P("expert", "seq", tensor),
    )
    return jax.shard_map(
        shards,
        mesh=mesh,
        in_specs=placed,
        out_specs=(
            P(("expert", "seq"), tensor),
            P(("expert", "seq"), None),
            P("expert", "seq", tensor),
            P("expert", "seq", tensor),
            P("expert", "seq", tensor),
        ),
        check_vma=False,
    )
```

```python
import jax
import jax.numpy as jnp
from jax import lax
from jax.sharding import PartitionSpec as P


def shards(tokens, grad_out, expert_ids, route_weights, gate_weight, up_weight, down_weight):
    expert_count = lax.axis_size("expert")
    seq_count = lax.axis_size("seq")
    tensor_count = lax.axis_size("tx") * lax.axis_size("core")
    core = lax.axis_index("core")
    local_count = gate_weight.shape[0]
    tok_rows = tokens.shape[0]
    model_width = tokens.shape[1]
    part_width = model_width // tensor_count
    per_peer = tok_rows // 6
    peer_count = expert_count * seq_count
    block_rows = local_count * per_peer
    slot_count = peer_count * block_rows
    flat_ids = expert_ids.reshape(-1)
    route_count = flat_ids.shape[0]
    onehot = (
        flat_ids[:, None] == jnp.arange(local_count * expert_count, dtype=jnp.int32)[None, :]
    ).astype(jnp.int32)
    before = jnp.cumsum(onehot, axis=0) - onehot
    ranking = jnp.sum(before * onehot, axis=1)
    local_expert = flat_ids % local_count
    dest_peer = flat_ids // local_count * seq_count + ranking % seq_count
    target = (dest_peer * local_count + local_expert) * per_peer + ranking // seq_count
    source = (
        jnp.full((slot_count,), -1, jnp.int32)
        .at[target]
        .set(jnp.arange(route_count, dtype=jnp.int32))
    )
    filled = source >= 0
    safe_source = jnp.maximum(source, 0)
    token_of = safe_source // 2
    weight_send = (
        route_weights.reshape(-1)[safe_source] * filled.astype(route_weights.dtype)
    ).reshape(peer_count, block_rows)
    half = model_width // 2
    tokens_half = lax.dynamic_slice_in_dim(tokens, core * half, half, axis=1)
    grad_half = lax.dynamic_slice_in_dim(grad_out, core * half, half, axis=1)
    rows_send = jnp.stack(
        [
            tokens_half[token_of].reshape(peer_count, block_rows, half),
            grad_half[token_of].reshape(peer_count, block_rows, half),
        ],
        axis=1,
    )
    rows_mine, weight_recv = (
        lax.all_to_all(rows_send, ("expert", "seq"), split_axis=0, concat_axis=0, tiled=True),
        lax.all_to_all(weight_send, ("expert", "seq"), split_axis=0, concat_axis=0, tiled=True),
    )

    def join_halves(mine):
        both = jnp.broadcast_to(mine[None], (2,) + mine.shape)
        return lax.all_to_all(both, "core", split_axis=0, concat_axis=0, tiled=True)

    def by_expert(values):
        shaped = values.reshape((peer_count, local_count, per_peer) + values.shape[2:])
        return jnp.swapaxes(shaped, 0, 1).reshape(
            (local_count, peer_count * per_peer) + values.shape[2:]
        )

    def by_peer(values):
        shaped = values.reshape((local_count, peer_count, per_peer) + values.shape[2:])
        return jnp.swapaxes(shaped, 0, 1).reshape((peer_count, block_rows) + values.shape[2:])

    rows_both = join_halves(rows_mine)
    in_rows = jax.vmap(by_expert)(rows_both[:, :, 0])
    out_rows = jax.vmap(by_expert)(rows_both[:, :, 1])
    prob = by_expert(weight_recv).astype(jnp.float32)[:, :, None]
    weights = lax.all_gather(
        jnp.stack([gate_weight, up_weight, down_weight]), "seq", axis=2, tiled=True
    )
    gate_full, up_full, down_full = weights[0], weights[1], weights[2]
    hidden_count = gate_full.shape[2]
    gate_h, up_h, down_h = (
        w.reshape(local_count, 2, half, hidden_count) for w in (gate_full, up_full, down_full)
    )
    pre_gate = jnp.einsum("cemd,ecdf->emf", in_rows, gate_h, preferred_element_type=jnp.float32)
    pre_up = jnp.einsum("cemd,ecdf->emf", in_rows, up_h, preferred_element_type=jnp.float32)
    sigmoid_gate = jax.nn.sigmoid(pre_gate)
    silu_gate = pre_gate * sigmoid_gate
    hidden = silu_gate * pre_up
    hidden_low = hidden.astype(jnp.bfloat16)
    back_proj = jnp.einsum("cemd,ecdf->emf", out_rows, down_h, preferred_element_type=jnp.float32)
    partial_scores = jnp.sum(hidden * back_proj, axis=2)
    scaled = (prob[None] * out_rows.astype(jnp.float32)).astype(jnp.bfloat16)
    hidden_grad = prob * back_proj
    up_grad = (hidden_grad * silu_gate).astype(jnp.bfloat16)
    gate_grad = (
        hidden_grad * pre_up * sigmoid_gate * (1.0 + pre_gate * (1.0 - sigmoid_gate))
    ).astype(jnp.bfloat16)
    gate_part = jnp.einsum("cemd,emf->ecdf", in_rows, gate_grad, preferred_element_type=jnp.float32)
    up_part = jnp.einsum("cemd,emf->ecdf", in_rows, up_grad, preferred_element_type=jnp.float32)
    down_part = jnp.einsum("cemd,emf->ecdf", scaled, hidden_low, preferred_element_type=jnp.float32)
    parts = jnp.stack([gate_part, up_part, down_part]).reshape(
        3, local_count, model_width, hidden_count
    ).astype(jnp.bfloat16)
    parts, gate_grad, up_grad = lax.optimization_barrier((parts, gate_grad, up_grad))
    reduced_parts = lax.psum_scatter(parts, "seq", scatter_dimension=2, tiled=True).astype(jnp.float32)
    grad_gate, grad_up, grad_down = reduced_parts[0], reduced_parts[1], reduced_parts[2]
    input_terms = jnp.einsum(
        "emf,ecdf->ecdm", gate_grad, gate_h, preferred_element_type=jnp.float32
    )
    input_terms = input_terms + jnp.einsum(
        "emf,ecdf->ecdm", up_grad, up_h, preferred_element_type=jnp.float32
    )
    rows_here = local_count * slot_count
    input_terms = jnp.swapaxes(
        input_terms.reshape(local_count, tensor_count, part_width, slot_count), 0, 1
    ).reshape(tensor_count, part_width, rows_here)
    score_pad = 16
    score_rows = jnp.zeros((tensor_count, score_pad, rows_here), jnp.float32)
    score_rows = score_rows.at[:, 0, :].set(partial_scores.reshape(1, rows_here))
    stacked = jnp.concatenate([input_terms, score_rows], axis=1).astype(jnp.bfloat16)
    tx_count = lax.axis_size("tx")
    stacked = stacked.reshape(tx_count, 2, part_width + score_pad, rows_here)
    pair = lax.all_to_all(stacked, "core", split_axis=1, concat_axis=1, tiled=True)
    pair = jnp.sum(pair.astype(jnp.float32), axis=1).astype(jnp.bfloat16)
    ring = lax.all_to_all(pair, "tx", split_axis=0, concat_axis=0, tiled=True)
    reduced = jnp.sum(ring.astype(jnp.float32), axis=0).astype(jnp.bfloat16)
    back_send = by_peer(
        jnp.swapaxes(reduced, 0, 1).reshape(local_count, slot_count, part_width + score_pad)
    )
    back_all = lax.all_to_all(
        back_send, ("expert", "seq"), split_axis=0, concat_axis=0, tiled=True
    ).astype(jnp.float32)
    back_all = back_all.reshape(slot_count, part_width + score_pad)[target]
    route_rows = back_all[:, :part_width].reshape(tok_rows, 2, part_width)
    grad_tokens = jnp.sum(route_rows, axis=1).astype(jnp.bfloat16)
    grad_route = back_all[:, part_width].reshape(tok_rows, 2)
    return (grad_tokens, grad_route, grad_gate, grad_up, grad_down)


def solution(mesh):
    shape = mesh.devices.shape
    mesh = jax.sharding.Mesh(
        mesh.devices.reshape(shape[0], shape[1], shape[2] // 2, 2), ("expert", "seq", "tx", "core")
    )
    tensor = ("tx", "core")
    placed = (
        P(("expert", "seq"), None),
        P(("expert", "seq"), None),
        P(("expert", "seq"), None),
        P(("expert", "seq"), None),
        P("expert", "seq", tensor),
        P("expert", "seq", tensor),
        P("expert", "seq", tensor),
    )
    return jax.shard_map(
        shards,
        mesh=mesh,
        in_specs=placed,
        out_specs=(
            P(("expert", "seq"), tensor),
            P(("expert", "seq"), None),
            P("expert", "seq", tensor),
            P("expert", "seq", tensor),
            P("expert", "seq", tensor),
        ),
        check_vma=False,
    )
```

```python
import functools

import jax
import jax.numpy as jnp
from jax import lax
from jax.experimental import pallas as pl
from jax.experimental.pallas import tpu as pltpu
from jax.sharding import PartitionSpec as P

MESH = pl.DeviceIdType.MESH


def exchange_kernel(n_seq, peers, send_ref, out_ref, send_sem, recv_sem, local_sem, fsend_sem, frecv_sem):
    e = lax.axis_index("expert")
    s = lax.axis_index("seq")
    x = lax.axis_index("tx")
    c = lax.axis_index("core")
    me = e * n_seq + s
    other = 1 - c
    partner = (e, s, x, other)

    def peer_of(k):
        q = lax.rem(me + k, peers)
        return q, (q // n_seq, q % n_seq, x, c)

    barrier = pltpu.get_barrier_semaphore()
    for k in range(1, peers):
        pl.semaphore_signal(barrier, inc=1, device_id=peer_of(k)[1], device_id_type=MESH)
    pl.semaphore_signal(barrier, inc=1, device_id=partner, device_id_type=MESH)
    pl.semaphore_wait(barrier, peers)

    local = pltpu.make_async_copy(send_ref.at[me], out_ref.at[c, me], local_sem.at[0])
    local.start()
    sends = []
    for k in range(1, peers):
        q, where = peer_of(k)
        copy = pltpu.make_async_remote_copy(
            src_ref=send_ref.at[q],
            dst_ref=out_ref.at[c, me],
            send_sem=send_sem.at[q],
            recv_sem=recv_sem.at[me],
            device_id=where,
            device_id_type=MESH,
        )
        copy.start()
        sends.append(copy)
    forwards = []
    for k in range(peers):
        p, where = peer_of(k)
        if k == 0:
            local.wait()
        else:
            pltpu.make_async_remote_copy(
                src_ref=send_ref.at[p],
                dst_ref=out_ref.at[c, p],
                send_sem=send_sem.at[p],
                recv_sem=recv_sem.at[p],
                device_id=where,
                device_id_type=MESH,
            ).wait_recv()
        forward = pltpu.make_async_remote_copy(
            src_ref=out_ref.at[c, p],
            dst_ref=out_ref.at[c, p],
            send_sem=fsend_sem.at[p],
            recv_sem=frecv_sem.at[p],
            device_id=partner,
            device_id_type=MESH,
        )
        forward.start()
        forwards.append(forward)
    for k in range(peers):
        p = peer_of(k)[0]
        pltpu.make_async_remote_copy(
            src_ref=out_ref.at[other, p],
            dst_ref=out_ref.at[other, p],
            send_sem=fsend_sem.at[p],
            recv_sem=frecv_sem.at[p],
            device_id=partner,
            device_id_type=MESH,
        ).wait_recv()
    for copy in sends:
        copy.wait_send()
    for forward in forwards:
        forward.wait_send()


def exchange_rows(rows_send, n_seq):
    peers = rows_send.shape[0]
    return pl.pallas_call(
        functools.partial(exchange_kernel, n_seq, peers),
        out_shape=jax.ShapeDtypeStruct((2,) + rows_send.shape, rows_send.dtype),
        in_specs=[pl.BlockSpec(memory_space=pl.ANY)],
        out_specs=pl.BlockSpec(memory_space=pl.ANY),
        scratch_shapes=[
            pltpu.SemaphoreType.DMA((peers,)),
            pltpu.SemaphoreType.DMA((peers,)),
            pltpu.SemaphoreType.DMA((1,)),
            pltpu.SemaphoreType.DMA((peers,)),
            pltpu.SemaphoreType.DMA((peers,)),
        ],
        compiler_params=pltpu.CompilerParams(collective_id=0, has_side_effects=True),
    )(rows_send)


def shards(tokens, grad_out, expert_ids, route_weights, gate_weight, up_weight, down_weight):
    expert_count = lax.axis_size("expert")
    seq_count = lax.axis_size("seq")
    tensor_count = lax.axis_size("tx") * lax.axis_size("core")
    core = lax.axis_index("core")
    local_count = gate_weight.shape[0]
    tok_rows = tokens.shape[0]
    model_width = tokens.shape[1]
    part_width = model_width // tensor_count
    per_peer = tok_rows // 6
    peer_count = expert_count * seq_count
    block_rows = local_count * per_peer
    slot_count = peer_count * block_rows
    flat_ids = expert_ids.reshape(-1)
    route_count = flat_ids.shape[0]
    onehot = (
        flat_ids[:, None] == jnp.arange(local_count * expert_count, dtype=jnp.int32)[None, :]
    ).astype(jnp.int32)
    before = jnp.cumsum(onehot, axis=0) - onehot
    ranking = jnp.sum(before * onehot, axis=1)
    local_expert = flat_ids % local_count
    dest_peer = flat_ids // local_count * seq_count + ranking % seq_count
    target = (dest_peer * local_count + local_expert) * per_peer + ranking // seq_count
    source = (
        jnp.full((slot_count,), -1, jnp.int32)
        .at[target]
        .set(jnp.arange(route_count, dtype=jnp.int32))
    )
    filled = source >= 0
    safe_source = jnp.maximum(source, 0)
    token_of = safe_source // 2
    weight_send = (
        route_weights.reshape(-1)[safe_source] * filled.astype(route_weights.dtype)
    ).reshape(peer_count, block_rows)
    half = model_width // 2
    tokens_half = lax.dynamic_slice_in_dim(tokens, core * half, half, axis=1)
    grad_half = lax.dynamic_slice_in_dim(grad_out, core * half, half, axis=1)
    rows_send = jnp.stack(
        [
            tokens_half[token_of].reshape(peer_count, block_rows, half),
            grad_half[token_of].reshape(peer_count, block_rows, half),
        ],
        axis=1,
    )
    weight_recv = lax.all_to_all(
        weight_send, ("expert", "seq"), split_axis=0, concat_axis=0, tiled=True
    )

    def join_halves(mine):
        both = jnp.broadcast_to(mine[None], (2,) + mine.shape)
        return lax.all_to_all(both, "core", split_axis=0, concat_axis=0, tiled=True)

    def by_expert(values):
        shaped = values.reshape((peer_count, local_count, per_peer) + values.shape[2:])
        return jnp.swapaxes(shaped, 0, 1).reshape(
            (local_count, peer_count * per_peer) + values.shape[2:]
        )

    def by_peer(values):
        shaped = values.reshape((local_count, peer_count, per_peer) + values.shape[2:])
        return jnp.swapaxes(shaped, 0, 1).reshape((peer_count, block_rows) + values.shape[2:])

    rows_both = exchange_rows(rows_send, seq_count)
    in_rows = jax.vmap(by_expert)(rows_both[:, :, 0])
    out_rows = jax.vmap(by_expert)(rows_both[:, :, 1])
    prob = by_expert(weight_recv).astype(jnp.float32)[:, :, None]
    weights = lax.all_gather(
        jnp.stack([gate_weight, up_weight, down_weight]), "seq", axis=2, tiled=True
    )
    gate_full, up_full, down_full = weights[0], weights[1], weights[2]
    hidden_count = gate_full.shape[2]
    gate_h, up_h, down_h = (
        w.reshape(local_count, 2, half, hidden_count) for w in (gate_full, up_full, down_full)
    )
    pre_gate = jnp.einsum("cemd,ecdf->emf", in_rows, gate_h, preferred_element_type=jnp.float32)
    pre_up = jnp.einsum("cemd,ecdf->emf", in_rows, up_h, preferred_element_type=jnp.float32)
    sigmoid_gate = jax.nn.sigmoid(pre_gate)
    silu_gate = pre_gate * sigmoid_gate
    hidden = silu_gate * pre_up
    hidden_low = hidden.astype(jnp.bfloat16)
    back_proj = jnp.einsum("cemd,ecdf->emf", out_rows, down_h, preferred_element_type=jnp.float32)
    partial_scores = jnp.sum(hidden * back_proj, axis=2)
    scaled = (prob[None] * out_rows.astype(jnp.float32)).astype(jnp.bfloat16)
    hidden_grad = prob * back_proj
    up_grad = (hidden_grad * silu_gate).astype(jnp.bfloat16)
    gate_grad = (
        hidden_grad * pre_up * sigmoid_gate * (1.0 + pre_gate * (1.0 - sigmoid_gate))
    ).astype(jnp.bfloat16)
    gate_part = jnp.einsum("cemd,emf->ecdf", in_rows, gate_grad, preferred_element_type=jnp.float32)
    up_part = jnp.einsum("cemd,emf->ecdf", in_rows, up_grad, preferred_element_type=jnp.float32)
    down_part = jnp.einsum("cemd,emf->ecdf", scaled, hidden_low, preferred_element_type=jnp.float32)
    parts = jnp.stack([gate_part, up_part, down_part]).reshape(
        3, local_count, model_width, hidden_count
    ).astype(jnp.bfloat16)
    parts, gate_grad, up_grad = lax.optimization_barrier((parts, gate_grad, up_grad))
    reduced_parts = lax.psum_scatter(parts, "seq", scatter_dimension=2, tiled=True).astype(jnp.float32)
    grad_gate, grad_up, grad_down = reduced_parts[0], reduced_parts[1], reduced_parts[2]
    input_terms = jnp.einsum(
        "emf,ecdf->ecdm", gate_grad, gate_h, preferred_element_type=jnp.float32
    )
    input_terms = input_terms + jnp.einsum(
        "emf,ecdf->ecdm", up_grad, up_h, preferred_element_type=jnp.float32
    )
    rows_here = local_count * slot_count
    input_terms = jnp.swapaxes(
        input_terms.reshape(local_count, tensor_count, part_width, slot_count), 0, 1
    ).reshape(tensor_count, part_width, rows_here)
    score_pad = 16
    score_rows = jnp.zeros((tensor_count, score_pad, rows_here), jnp.float32)
    score_rows = score_rows.at[:, 0, :].set(partial_scores.reshape(1, rows_here))
    stacked = jnp.concatenate([input_terms, score_rows], axis=1).astype(jnp.bfloat16)
    tx_count = lax.axis_size("tx")
    stacked = stacked.reshape(tx_count, 2, part_width + score_pad, rows_here)
    pair = lax.all_to_all(stacked, "core", split_axis=1, concat_axis=1, tiled=True)
    pair = jnp.sum(pair.astype(jnp.float32), axis=1).astype(jnp.bfloat16)
    ring = lax.all_to_all(pair, "tx", split_axis=0, concat_axis=0, tiled=True)
    reduced = jnp.sum(ring.astype(jnp.float32), axis=0).astype(jnp.bfloat16)
    back_send = by_peer(
        jnp.swapaxes(reduced, 0, 1).reshape(local_count, slot_count, part_width + score_pad)
    )
    back_all = lax.all_to_all(
        back_send, ("expert", "seq"), split_axis=0, concat_axis=0, tiled=True
    ).astype(jnp.float32)
    back_all = back_all.reshape(slot_count, part_width + score_pad)[target]
    route_rows = back_all[:, :part_width].reshape(tok_rows, 2, part_width)
    grad_tokens = jnp.sum(route_rows, axis=1).astype(jnp.bfloat16)
    grad_route = back_all[:, part_width].reshape(tok_rows, 2)
    return (grad_tokens, grad_route, grad_gate, grad_up, grad_down)


def solution(mesh):
    shape = mesh.devices.shape
    mesh = jax.sharding.Mesh(
        mesh.devices.reshape(shape[0], shape[1], shape[2] // 2, 2), ("expert", "seq", "tx", "core")
    )
    tensor = ("tx", "core")
    placed = (
        P(("expert", "seq"), None),
        P(("expert", "seq"), None),
        P(("expert", "seq"), None),
        P(("expert", "seq"), None),
        P("expert", "seq", tensor),
        P("expert", "seq", tensor),
        P("expert", "seq", tensor),
    )
    return jax.shard_map(
        shards,
        mesh=mesh,
        in_specs=placed,
        out_specs=(
            P(("expert", "seq"), tensor),
            P(("expert", "seq"), None),
            P("expert", "seq", tensor),
            P("expert", "seq", tensor),
            P("expert", "seq", tensor),
        ),
        check_vma=False,
    )
```

```python
import functools

import jax
import jax.numpy as jnp
from jax import lax
from jax.experimental import pallas as pl
from jax.experimental.pallas import tpu as pltpu
from jax.sharding import PartitionSpec as P

MESH = pl.DeviceIdType.MESH


def exchange_kernel(n_seq, n_tx, peers, send_ref, out_ref, send_sem, recv_sem, local_sem):
    e = lax.axis_index("expert")
    s = lax.axis_index("seq")
    x = lax.axis_index("tx")
    c = lax.axis_index("core")
    me = e * n_seq + s
    other = 1 - c
    x_left = lax.rem(x + n_tx - 1, n_tx)
    x_right = lax.rem(x + 1, n_tx)
    x_far = lax.rem(x + 2, n_tx)
    own = x * 2 + c
    from_left = x_left * 2 + c
    from_right = x_right * 2 + c
    from_far = x_far * 2 + c
    left = (e, s, x_left, c)
    right = (e, s, x_right, c)
    partner = (e, s, x, other)

    def peer(k):
        q = lax.rem(me + k, peers)
        return q, (q // n_seq, q % n_seq, x, c)

    barrier = pltpu.get_barrier_semaphore()
    for k in range(1, peers):
        pl.semaphore_signal(barrier, inc=1, device_id=peer(k)[1], device_id_type=MESH)
    for where in (left, right, partner):
        pl.semaphore_signal(barrier, inc=1, device_id=where, device_id_type=MESH)
    pl.semaphore_wait(barrier, peers + 2)

    def remote(src, dst, slot, recv, where):
        return pltpu.make_async_remote_copy(
            src_ref=src,
            dst_ref=dst,
            send_sem=send_sem.at[slot],
            recv_sem=recv_sem.at[recv],
            device_id=where,
            device_id_type=MESH,
        )

    local = pltpu.make_async_copy(send_ref.at[me], out_ref.at[own, me], local_sem.at[0])
    local.start()
    for k in range(1, peers):
        q, where = peer(k)
        remote(send_ref.at[q], out_ref.at[own, me], q, own * peers + me, where).start()

    def arrived(chunk, p):
        block = out_ref.at[chunk, p]
        remote(block, block, 0, chunk * peers + p, partner).wait_recv()

    def forward(chunk, p, slot, where):
        block = out_ref.at[chunk, p]
        remote(block, block, slot, chunk * peers + p, where).start()

    local.wait()
    for k in range(peers):
        p = peer(k)[0]
        if k > 0:
            arrived(own, p)
        forward(own, p, peers + p, right)
        forward(own, p, 2 * peers + p, left)
        forward(own, p, 3 * peers + p, partner)

    def relay(chunk, onward, base):
        def body(p, carry):
            arrived(chunk, p)
            if onward is not None:
                forward(chunk, p, base + peers + p, onward)
            forward(chunk, p, base + p, partner)
            return carry

        lax.fori_loop(0, peers, body, 0)

    relay(from_left, right, 4 * peers)
    relay(from_right, None, 6 * peers)
    relay(from_far, None, 7 * peers)

    def partner_chunks(p, carry):
        for column in range(n_tx):
            arrived(column * 2 + other, p)
        return carry

    lax.fori_loop(0, peers, partner_chunks, 0)

    def drain(slot, carry):
        block = out_ref.at[own, 0]
        remote(block, block, slot, 0, partner).wait_send()
        return carry

    for k in range(1, peers):
        q = peer(k)[0]
        drain(q, 0)
    lax.fori_loop(peers, 6 * peers, drain, 0)
    lax.fori_loop(7 * peers, 8 * peers, drain, 0)
    lax.fori_loop(6 * peers, 7 * peers, drain, 0)


def exchange_rows(rows_send, n_seq, n_tx):
    peers = rows_send.shape[0]
    chunks = 2 * n_tx
    return pl.pallas_call(
        functools.partial(exchange_kernel, n_seq, n_tx, peers),
        out_shape=jax.ShapeDtypeStruct((chunks,) + rows_send.shape, rows_send.dtype),
        in_specs=[pl.BlockSpec(memory_space=pl.ANY)],
        out_specs=pl.BlockSpec(memory_space=pl.ANY),
        scratch_shapes=[
            pltpu.SemaphoreType.DMA((8 * peers,)),
            pltpu.SemaphoreType.DMA((chunks * peers,)),
            pltpu.SemaphoreType.DMA((1,)),
        ],
        compiler_params=pltpu.CompilerParams(collective_id=0, has_side_effects=True),
    )(rows_send)


def shards(tokens, grad_out, expert_ids, route_weights, gate_weight, up_weight, down_weight):
    expert_count = lax.axis_size("expert")
    seq_count = lax.axis_size("seq")
    tensor_count = lax.axis_size("tx") * lax.axis_size("core")
    core = lax.axis_index("core")
    local_count = gate_weight.shape[0]
    tok_rows = tokens.shape[0]
    model_width = tokens.shape[1]
    part_width = model_width // tensor_count
    per_peer = tok_rows // 6
    peer_count = expert_count * seq_count
    block_rows = local_count * per_peer
    slot_count = peer_count * block_rows
    flat_ids = expert_ids.reshape(-1)
    route_count = flat_ids.shape[0]
    onehot = (
        flat_ids[:, None] == jnp.arange(local_count * expert_count, dtype=jnp.int32)[None, :]
    ).astype(jnp.int32)
    before = jnp.cumsum(onehot, axis=0) - onehot
    ranking = jnp.sum(before * onehot, axis=1)
    local_expert = flat_ids % local_count
    dest_peer = flat_ids // local_count * seq_count + ranking % seq_count
    target = (dest_peer * local_count + local_expert) * per_peer + ranking // seq_count
    source = (
        jnp.full((slot_count,), -1, jnp.int32)
        .at[target]
        .set(jnp.arange(route_count, dtype=jnp.int32))
    )
    filled = source >= 0
    safe_source = jnp.maximum(source, 0)
    token_of = safe_source // 2
    weight_send = (
        route_weights.reshape(-1)[safe_source] * filled.astype(route_weights.dtype)
    ).reshape(peer_count, block_rows)
    own_part = lax.axis_index("tx") * 2 + core
    half = part_width
    tokens_half = lax.dynamic_slice_in_dim(tokens, own_part * half, half, axis=1)
    grad_half = lax.dynamic_slice_in_dim(grad_out, own_part * half, half, axis=1)
    rows_send = jnp.stack(
        [
            tokens_half[token_of].reshape(peer_count, block_rows, half),
            grad_half[token_of].reshape(peer_count, block_rows, half),
        ],
        axis=1,
    )
    weight_recv = lax.all_to_all(
        weight_send, ("expert", "seq"), split_axis=0, concat_axis=0, tiled=True
    )

    def join_halves(mine):
        both = jnp.broadcast_to(mine[None], (2,) + mine.shape)
        return lax.all_to_all(both, "core", split_axis=0, concat_axis=0, tiled=True)

    def by_expert(values):
        shaped = values.reshape((peer_count, local_count, per_peer) + values.shape[2:])
        return jnp.swapaxes(shaped, 0, 1).reshape(
            (local_count, peer_count * per_peer) + values.shape[2:]
        )

    def by_peer(values):
        shaped = values.reshape((local_count, peer_count, per_peer) + values.shape[2:])
        return jnp.swapaxes(shaped, 0, 1).reshape((peer_count, block_rows) + values.shape[2:])

    rows_both = exchange_rows(rows_send, seq_count, lax.axis_size("tx"))
    in_rows = jax.vmap(by_expert)(rows_both[:, :, 0])
    out_rows = jax.vmap(by_expert)(rows_both[:, :, 1])
    prob = by_expert(weight_recv).astype(jnp.float32)[:, :, None]
    weights = lax.all_gather(
        jnp.stack([gate_weight, up_weight, down_weight]), "seq", axis=2, tiled=True
    )
    gate_full, up_full, down_full = weights[0], weights[1], weights[2]
    hidden_count = gate_full.shape[2]
    gate_h, up_h, down_h = (
        w.reshape(local_count, tensor_count, half, hidden_count)
        for w in (gate_full, up_full, down_full)
    )
    pre_gate = jnp.einsum("cemd,ecdf->emf", in_rows, gate_h, preferred_element_type=jnp.float32)
    pre_up = jnp.einsum("cemd,ecdf->emf", in_rows, up_h, preferred_element_type=jnp.float32)
    sigmoid_gate = jax.nn.sigmoid(pre_gate)
    silu_gate = pre_gate * sigmoid_gate
    hidden = silu_gate * pre_up
    hidden_low = hidden.astype(jnp.bfloat16)
    back_proj = jnp.einsum("cemd,ecdf->emf", out_rows, down_h, preferred_element_type=jnp.float32)
    partial_scores = jnp.sum(hidden * back_proj, axis=2)
    scaled = (prob[None] * out_rows.astype(jnp.float32)).astype(jnp.bfloat16)
    hidden_grad = prob * back_proj
    up_grad = (hidden_grad * silu_gate).astype(jnp.bfloat16)
    gate_grad = (
        hidden_grad * pre_up * sigmoid_gate * (1.0 + pre_gate * (1.0 - sigmoid_gate))
    ).astype(jnp.bfloat16)
    gate_part = jnp.einsum("cemd,emf->ecdf", in_rows, gate_grad, preferred_element_type=jnp.float32)
    up_part = jnp.einsum("cemd,emf->ecdf", in_rows, up_grad, preferred_element_type=jnp.float32)
    down_part = jnp.einsum("cemd,emf->ecdf", scaled, hidden_low, preferred_element_type=jnp.float32)
    parts = jnp.stack([gate_part, up_part, down_part]).reshape(
        3, local_count, model_width, hidden_count
    ).astype(jnp.bfloat16)
    parts, gate_grad, up_grad = lax.optimization_barrier((parts, gate_grad, up_grad))
    reduced_parts = lax.psum_scatter(parts, "seq", scatter_dimension=2, tiled=True).astype(jnp.float32)
    grad_gate, grad_up, grad_down = reduced_parts[0], reduced_parts[1], reduced_parts[2]
    input_terms = jnp.einsum(
        "emf,ecdf->ecdm", gate_grad, gate_h, preferred_element_type=jnp.float32
    )
    input_terms = input_terms + jnp.einsum(
        "emf,ecdf->ecdm", up_grad, up_h, preferred_element_type=jnp.float32
    )
    rows_here = local_count * slot_count
    input_terms = jnp.swapaxes(
        input_terms.reshape(local_count, tensor_count, part_width, slot_count), 0, 1
    ).reshape(tensor_count, part_width, rows_here)
    score_pad = 16
    score_rows = jnp.zeros((tensor_count, score_pad, rows_here), jnp.float32)
    score_rows = score_rows.at[:, 0, :].set(partial_scores.reshape(1, rows_here))
    stacked = jnp.concatenate([input_terms, score_rows], axis=1).astype(jnp.bfloat16)
    tx_count = lax.axis_size("tx")
    stacked = stacked.reshape(tx_count, 2, part_width + score_pad, rows_here)
    pair = lax.all_to_all(stacked, "core", split_axis=1, concat_axis=1, tiled=True)
    pair = jnp.sum(pair.astype(jnp.float32), axis=1).astype(jnp.bfloat16)
    ring = lax.all_to_all(pair, "tx", split_axis=0, concat_axis=0, tiled=True)
    reduced = jnp.sum(ring.astype(jnp.float32), axis=0).astype(jnp.bfloat16)
    back_send = by_peer(
        jnp.swapaxes(reduced, 0, 1).reshape(local_count, slot_count, part_width + score_pad)
    )
    back_all = lax.all_to_all(
        back_send, ("expert", "seq"), split_axis=0, concat_axis=0, tiled=True
    ).astype(jnp.float32)
    back_all = back_all.reshape(slot_count, part_width + score_pad)[target]
    route_rows = back_all[:, :part_width].reshape(tok_rows, 2, part_width)
    grad_tokens = jnp.sum(route_rows, axis=1).astype(jnp.bfloat16)
    grad_route = back_all[:, part_width].reshape(tok_rows, 2)
    return (grad_tokens, grad_route, grad_gate, grad_up, grad_down)


def solution(mesh):
    shape = mesh.devices.shape
    mesh = jax.sharding.Mesh(
        mesh.devices.reshape(shape[0], shape[1], shape[2] // 2, 2), ("expert", "seq", "tx", "core")
    )
    tensor = ("tx", "core")
    placed = (
        P(("expert", "seq"), None),
        P(("expert", "seq"), None),
        P(("expert", "seq"), None),
        P(("expert", "seq"), None),
        P("expert", "seq", tensor),
        P("expert", "seq", tensor),
        P("expert", "seq", tensor),
    )
    return jax.shard_map(
        shards,
        mesh=mesh,
        in_specs=placed,
        out_specs=(
            P(("expert", "seq"), tensor),
            P(("expert", "seq"), None),
            P("expert", "seq", tensor),
            P("expert", "seq", tensor),
            P("expert", "seq", tensor),
        ),
        check_vma=False,
    )
```

```python
import functools

import jax
import jax.numpy as jnp
from jax import lax
from jax.experimental import pallas as pl
from jax.experimental.pallas import tpu as pltpu
from jax.sharding import PartitionSpec as P

MESH = pl.DeviceIdType.MESH


def exchange_kernel(n_seq, n_tx, peers, send_ref, out_ref, send_sem, recv_sem, local_sem):
    e = lax.axis_index("expert")
    s = lax.axis_index("seq")
    x = lax.axis_index("tx")
    c = lax.axis_index("core")
    me = e * n_seq + s
    other = 1 - c
    x_left = lax.rem(x + n_tx - 1, n_tx)
    x_right = lax.rem(x + 1, n_tx)
    x_far = lax.rem(x + 2, n_tx)
    own = x * 2 + c
    from_left = x_left * 2 + c
    from_right = x_right * 2 + c
    from_far = x_far * 2 + c
    left = (e, s, x_left, c)
    right = (e, s, x_right, c)
    partner = (e, s, x, other)

    def peer(k):
        q = lax.rem(me + k, peers)
        return q, (q // n_seq, q % n_seq, x, c)

    barrier = pltpu.get_barrier_semaphore()
    for k in range(1, peers):
        pl.semaphore_signal(barrier, inc=1, device_id=peer(k)[1], device_id_type=MESH)
    for where in (left, right, partner):
        pl.semaphore_signal(barrier, inc=1, device_id=where, device_id_type=MESH)
    pl.semaphore_wait(barrier, peers + 2)

    def remote(src, dst, slot, recv, where):
        return pltpu.make_async_remote_copy(
            src_ref=src,
            dst_ref=dst,
            send_sem=send_sem.at[slot],
            recv_sem=recv_sem.at[recv],
            device_id=where,
            device_id_type=MESH,
        )

    local = pltpu.make_async_copy(send_ref.at[me], out_ref.at[own, me], local_sem.at[0])
    local.start()
    for k in range(1, peers):
        q, where = peer(k)
        remote(send_ref.at[q], out_ref.at[own, me], q, own * peers + me, where).start()

    def arrived(chunk, p):
        block = out_ref.at[chunk, p]
        remote(block, block, 0, chunk * peers + p, partner).wait_recv()

    def forward(chunk, p, slot, where):
        block = out_ref.at[chunk, p]
        remote(block, block, slot, chunk * peers + p, where).start()

    local.wait()
    for k in range(peers):
        p = peer(k)[0]
        if k > 0:
            arrived(own, p)
        forward(own, p, peers + p, right)
        forward(own, p, 2 * peers + p, left)
        forward(own, p, 3 * peers + p, partner)

    def relay(chunk, onward, onward_parity, base):
        def body(i, carry):
            for parity in (0, 1):
                p = 2 * i + parity
                arrived(chunk, p)
                if onward is not None and parity == onward_parity:
                    forward(chunk, p, base + peers + p, onward)
                forward(chunk, p, base + p, partner)
            return carry

        lax.fori_loop(0, peers // 2, body, 0)

    relay(from_left, right, 0, 4 * peers)
    relay(from_right, left, 1, 6 * peers)
    relay(from_far, None, 0, 8 * peers)

    def partner_chunks(p, carry):
        for column in range(n_tx):
            arrived(column * 2 + other, p)
        return carry

    lax.fori_loop(0, peers, partner_chunks, 0)

    def drain(slot, carry):
        block = out_ref.at[own, 0]
        remote(block, block, slot, 0, partner).wait_send()
        return carry

    def drain_pairs(first, parity):
        def body(i, carry):
            return drain(first + 2 * i + parity, carry)

        lax.fori_loop(0, peers // 2, body, 0)

    for k in range(1, peers):
        drain(peer(k)[0], 0)
    lax.fori_loop(peers, 5 * peers, drain, 0)
    drain_pairs(5 * peers, 0)
    lax.fori_loop(6 * peers, 7 * peers, drain, 0)
    drain_pairs(7 * peers, 1)
    lax.fori_loop(8 * peers, 9 * peers, drain, 0)


def exchange_rows(rows_send, n_seq, n_tx):
    peers = rows_send.shape[0]
    chunks = 2 * n_tx
    return pl.pallas_call(
        functools.partial(exchange_kernel, n_seq, n_tx, peers),
        out_shape=jax.ShapeDtypeStruct((chunks,) + rows_send.shape, rows_send.dtype),
        in_specs=[pl.BlockSpec(memory_space=pl.ANY)],
        out_specs=pl.BlockSpec(memory_space=pl.ANY),
        scratch_shapes=[
            pltpu.SemaphoreType.DMA((9 * peers,)),
            pltpu.SemaphoreType.DMA((chunks * peers,)),
            pltpu.SemaphoreType.DMA((1,)),
        ],
        compiler_params=pltpu.CompilerParams(collective_id=0, has_side_effects=True),
    )(rows_send)


def shards(tokens, grad_out, expert_ids, route_weights, gate_weight, up_weight, down_weight):
    expert_count = lax.axis_size("expert")
    seq_count = lax.axis_size("seq")
    tensor_count = lax.axis_size("tx") * lax.axis_size("core")
    core = lax.axis_index("core")
    local_count = gate_weight.shape[0]
    tok_rows = tokens.shape[0]
    model_width = tokens.shape[1]
    part_width = model_width // tensor_count
    per_peer = tok_rows // 6
    peer_count = expert_count * seq_count
    block_rows = local_count * per_peer
    slot_count = peer_count * block_rows
    flat_ids = expert_ids.reshape(-1)
    route_count = flat_ids.shape[0]
    onehot = (
        flat_ids[:, None] == jnp.arange(local_count * expert_count, dtype=jnp.int32)[None, :]
    ).astype(jnp.int32)
    before = jnp.cumsum(onehot, axis=0) - onehot
    ranking = jnp.sum(before * onehot, axis=1)
    local_expert = flat_ids % local_count
    dest_peer = flat_ids // local_count * seq_count + ranking % seq_count
    target = (dest_peer * local_count + local_expert) * per_peer + ranking // seq_count
    source = (
        jnp.full((slot_count,), -1, jnp.int32)
        .at[target]
        .set(jnp.arange(route_count, dtype=jnp.int32))
    )
    filled = source >= 0
    safe_source = jnp.maximum(source, 0)
    token_of = safe_source // 2
    weight_send = (
        route_weights.reshape(-1)[safe_source] * filled.astype(route_weights.dtype)
    ).reshape(peer_count, block_rows)
    own_part = lax.axis_index("tx") * 2 + core
    half = part_width
    tokens_half = lax.dynamic_slice_in_dim(tokens, own_part * half, half, axis=1)
    grad_half = lax.dynamic_slice_in_dim(grad_out, own_part * half, half, axis=1)
    rows_send = jnp.stack(
        [
            tokens_half[token_of].reshape(peer_count, block_rows, half),
            grad_half[token_of].reshape(peer_count, block_rows, half),
        ],
        axis=1,
    )
    weight_recv = lax.all_to_all(
        weight_send, ("expert", "seq"), split_axis=0, concat_axis=0, tiled=True
    )

    def join_halves(mine):
        both = jnp.broadcast_to(mine[None], (2,) + mine.shape)
        return lax.all_to_all(both, "core", split_axis=0, concat_axis=0, tiled=True)

    def by_expert(values):
        shaped = values.reshape((peer_count, local_count, per_peer) + values.shape[2:])
        return jnp.swapaxes(shaped, 0, 1).reshape(
            (local_count, peer_count * per_peer) + values.shape[2:]
        )

    def by_peer(values):
        shaped = values.reshape((local_count, peer_count, per_peer) + values.shape[2:])
        return jnp.swapaxes(shaped, 0, 1).reshape((peer_count, block_rows) + values.shape[2:])

    rows_both = exchange_rows(rows_send, seq_count, lax.axis_size("tx"))
    in_rows = jax.vmap(by_expert)(rows_both[:, :, 0])
    out_rows = jax.vmap(by_expert)(rows_both[:, :, 1])
    prob = by_expert(weight_recv).astype(jnp.float32)[:, :, None]
    weights = lax.all_gather(
        jnp.stack([gate_weight, up_weight, down_weight]), "seq", axis=2, tiled=True
    )
    gate_full, up_full, down_full = weights[0], weights[1], weights[2]
    hidden_count = gate_full.shape[2]
    gate_h, up_h, down_h = (
        w.reshape(local_count, tensor_count, half, hidden_count)
        for w in (gate_full, up_full, down_full)
    )
    pre_gate = jnp.einsum("cemd,ecdf->emf", in_rows, gate_h, preferred_element_type=jnp.float32)
    pre_up = jnp.einsum("cemd,ecdf->emf", in_rows, up_h, preferred_element_type=jnp.float32)
    sigmoid_gate = jax.nn.sigmoid(pre_gate)
    silu_gate = pre_gate * sigmoid_gate
    hidden = silu_gate * pre_up
    hidden_low = hidden.astype(jnp.bfloat16)
    back_proj = jnp.einsum("cemd,ecdf->emf", out_rows, down_h, preferred_element_type=jnp.float32)
    partial_scores = jnp.sum(hidden * back_proj, axis=2)
    scaled = (prob[None] * out_rows.astype(jnp.float32)).astype(jnp.bfloat16)
    hidden_grad = prob * back_proj
    up_grad = (hidden_grad * silu_gate).astype(jnp.bfloat16)
    gate_grad = (
        hidden_grad * pre_up * sigmoid_gate * (1.0 + pre_gate * (1.0 - sigmoid_gate))
    ).astype(jnp.bfloat16)
    gate_part = jnp.einsum("cemd,emf->ecdf", in_rows, gate_grad, preferred_element_type=jnp.float32)
    up_part = jnp.einsum("cemd,emf->ecdf", in_rows, up_grad, preferred_element_type=jnp.float32)
    down_part = jnp.einsum("cemd,emf->ecdf", scaled, hidden_low, preferred_element_type=jnp.float32)
    parts = jnp.stack([gate_part, up_part, down_part]).reshape(
        3, local_count, model_width, hidden_count
    ).astype(jnp.bfloat16)
    parts, gate_grad, up_grad = lax.optimization_barrier((parts, gate_grad, up_grad))
    reduced_parts = lax.psum_scatter(parts, "seq", scatter_dimension=2, tiled=True).astype(jnp.float32)
    grad_gate, grad_up, grad_down = reduced_parts[0], reduced_parts[1], reduced_parts[2]
    input_terms = jnp.einsum(
        "emf,ecdf->ecdm", gate_grad, gate_h, preferred_element_type=jnp.float32
    )
    input_terms = input_terms + jnp.einsum(
        "emf,ecdf->ecdm", up_grad, up_h, preferred_element_type=jnp.float32
    )
    rows_here = local_count * slot_count
    input_terms = jnp.swapaxes(
        input_terms.reshape(local_count, tensor_count, part_width, slot_count), 0, 1
    ).reshape(tensor_count, part_width, rows_here)
    score_pad = 16
    score_rows = jnp.zeros((tensor_count, score_pad, rows_here), jnp.float32)
    score_rows = score_rows.at[:, 0, :].set(partial_scores.reshape(1, rows_here))
    stacked = jnp.concatenate([input_terms, score_rows], axis=1).astype(jnp.bfloat16)
    tx_count = lax.axis_size("tx")
    stacked = stacked.reshape(tx_count, 2, part_width + score_pad, rows_here)
    pair = lax.all_to_all(stacked, "core", split_axis=1, concat_axis=1, tiled=True)
    pair = jnp.sum(pair.astype(jnp.float32), axis=1).astype(jnp.bfloat16)
    ring = lax.all_to_all(pair, "tx", split_axis=0, concat_axis=0, tiled=True)
    reduced = jnp.sum(ring.astype(jnp.float32), axis=0).astype(jnp.bfloat16)
    back_send = by_peer(
        jnp.swapaxes(reduced, 0, 1).reshape(local_count, slot_count, part_width + score_pad)
    )
    back_all = lax.all_to_all(
        back_send, ("expert", "seq"), split_axis=0, concat_axis=0, tiled=True
    ).astype(jnp.float32)
    back_all = back_all.reshape(slot_count, part_width + score_pad)[target]
    route_rows = back_all[:, :part_width].reshape(tok_rows, 2, part_width)
    grad_tokens = jnp.sum(route_rows, axis=1).astype(jnp.bfloat16)
    grad_route = back_all[:, part_width].reshape(tok_rows, 2)
    return (grad_tokens, grad_route, grad_gate, grad_up, grad_down)


def solution(mesh):
    shape = mesh.devices.shape
    mesh = jax.sharding.Mesh(
        mesh.devices.reshape(shape[0], shape[1], shape[2] // 2, 2), ("expert", "seq", "tx", "core")
    )
    tensor = ("tx", "core")
    placed = (
        P(("expert", "seq"), None),
        P(("expert", "seq"), None),
        P(("expert", "seq"), None),
        P(("expert", "seq"), None),
        P("expert", "seq", tensor),
        P("expert", "seq", tensor),
        P("expert", "seq", tensor),
    )
    return jax.shard_map(
        shards,
        mesh=mesh,
        in_specs=placed,
        out_specs=(
            P(("expert", "seq"), tensor),
            P(("expert", "seq"), None),
            P("expert", "seq", tensor),
            P("expert", "seq", tensor),
            P("expert", "seq", tensor),
        ),
        check_vma=False,
    )
```

```python
import functools

import jax
import jax.numpy as jnp
from jax import lax
from jax.experimental import pallas as pl
from jax.experimental.pallas import tpu as pltpu
from jax.sharding import PartitionSpec as P

MESH = pl.DeviceIdType.MESH


def exchange_kernel(
    n_seq, n_tx, peers, send_ref, weight_ref, out_ref, weight_out, send_sem, recv_sem, local_sem, w_send, w_recv
):
    e = lax.axis_index("expert")
    s = lax.axis_index("seq")
    x = lax.axis_index("tx")
    c = lax.axis_index("core")
    me = e * n_seq + s
    other = 1 - c
    x_left = lax.rem(x + n_tx - 1, n_tx)
    x_right = lax.rem(x + 1, n_tx)
    x_far = lax.rem(x + 2, n_tx)
    own = x * 2 + c
    from_left = x_left * 2 + c
    from_right = x_right * 2 + c
    from_far = x_far * 2 + c
    left = (e, s, x_left, c)
    right = (e, s, x_right, c)
    partner = (e, s, x, other)

    def peer(k):
        q = lax.rem(me + k, peers)
        return q, (q // n_seq, q % n_seq, x, c)

    barrier = pltpu.get_barrier_semaphore()
    for k in range(1, peers):
        pl.semaphore_signal(barrier, inc=1, device_id=peer(k)[1], device_id_type=MESH)
    for where in (left, right, partner):
        pl.semaphore_signal(barrier, inc=1, device_id=where, device_id_type=MESH)
    pl.semaphore_wait(barrier, peers + 2)

    def remote(src, dst, slot, recv, where):
        return pltpu.make_async_remote_copy(
            src_ref=src,
            dst_ref=dst,
            send_sem=send_sem.at[slot],
            recv_sem=recv_sem.at[recv],
            device_id=where,
            device_id_type=MESH,
        )

    s_left = lax.rem(s + n_seq - 1, n_seq)
    s_right = lax.rem(s + 1, n_seq)
    s_far = lax.rem(s + 2, n_seq)
    up_ring = (e, s_right, x, c)
    down_ring = (e, s_left, x, c)
    rows = weight_ref.shape[1] // 2

    def w_piece(ref, origin, piece):
        return ref.at[:, pl.ds(piece * rows, rows)] if origin is None else ref.at[:, origin, pl.ds(piece * rows, rows)]

    def w_copy(origin, piece, slot, where, src=None):
        return pltpu.make_async_remote_copy(
            src_ref=w_piece(weight_ref, None, piece) if src is None else src,
            dst_ref=w_piece(weight_out, origin, piece),
            send_sem=w_send.at[slot],
            recv_sem=w_recv.at[origin * 2 + piece],
            device_id=where,
            device_id_type=MESH,
        )

    w_local = pltpu.make_async_copy(weight_ref, weight_out.at[:, s], local_sem.at[1])
    w_local.start()
    for piece in range(2):
        w_copy(s, piece, piece, up_ring).start()
        w_copy(s, piece, 2 + piece, down_ring).start()

    local = pltpu.make_async_copy(send_ref.at[me], out_ref.at[own, me], local_sem.at[0])
    local.start()
    for k in range(1, peers):
        q, where = peer(k)
        remote(send_ref.at[q], out_ref.at[own, me], q, own * peers + me, where).start()

    def arrived(chunk, p):
        block = out_ref.at[chunk, p]
        remote(block, block, 0, chunk * peers + p, partner).wait_recv()

    def forward(chunk, p, slot, where):
        block = out_ref.at[chunk, p]
        remote(block, block, slot, chunk * peers + p, where).start()

    local.wait()
    for k in range(peers):
        p = peer(k)[0]
        if k > 0:
            arrived(own, p)
        forward(own, p, peers + p, right)
        forward(own, p, 2 * peers + p, left)
        forward(own, p, 3 * peers + p, partner)

    def relay(chunk, onward, onward_parity, base):
        def body(i, carry):
            for parity in (0, 1):
                p = 2 * i + parity
                arrived(chunk, p)
                if onward is not None and parity == onward_parity:
                    forward(chunk, p, base + peers + p, onward)
                forward(chunk, p, base + p, partner)
            return carry

        lax.fori_loop(0, peers // 2, body, 0)

    w_copy(s_left, 0, 0, up_ring).wait_recv()
    block = w_piece(weight_out, s_left, 0)
    w_copy(s_left, 0, 4, up_ring, src=block).start()
    w_copy(s_right, 1, 0, down_ring).wait_recv()
    block = w_piece(weight_out, s_right, 1)
    w_copy(s_right, 1, 5, down_ring, src=block).start()
    w_copy(s_left, 1, 0, up_ring).wait_recv()
    w_copy(s_right, 0, 0, up_ring).wait_recv()
    for piece in range(2):
        w_copy(s_far, piece, 0, up_ring).wait_recv()
    w_local.wait()

    relay(from_left, right, 0, 4 * peers)
    relay(from_right, left, 1, 6 * peers)
    relay(from_far, None, 0, 8 * peers)

    def partner_chunks(p, carry):
        for column in range(n_tx):
            arrived(column * 2 + other, p)
        return carry

    lax.fori_loop(0, peers, partner_chunks, 0)

    def drain(slot, carry):
        block = out_ref.at[own, 0]
        remote(block, block, slot, 0, partner).wait_send()
        return carry

    def drain_pairs(first, parity):
        def body(i, carry):
            return drain(first + 2 * i + parity, carry)

        lax.fori_loop(0, peers // 2, body, 0)

    for k in range(1, peers):
        drain(peer(k)[0], 0)
    lax.fori_loop(peers, 5 * peers, drain, 0)
    drain_pairs(5 * peers, 0)
    lax.fori_loop(6 * peers, 7 * peers, drain, 0)
    drain_pairs(7 * peers, 1)
    lax.fori_loop(8 * peers, 9 * peers, drain, 0)
    for slot in range(6):
        w_copy(s, slot % 2, slot, up_ring).wait_send()


def exchange_rows(rows_send, weights, n_seq, n_tx):
    peers = rows_send.shape[0]
    chunks = 2 * n_tx
    w_shape = (weights.shape[0], n_seq) + weights.shape[1:]
    return pl.pallas_call(
        functools.partial(exchange_kernel, n_seq, n_tx, peers),
        out_shape=(
            jax.ShapeDtypeStruct((chunks,) + rows_send.shape, rows_send.dtype),
            jax.ShapeDtypeStruct(w_shape, weights.dtype),
        ),
        in_specs=[pl.BlockSpec(memory_space=pl.ANY)] * 2,
        out_specs=(pl.BlockSpec(memory_space=pl.ANY), pl.BlockSpec(memory_space=pl.ANY)),
        scratch_shapes=[
            pltpu.SemaphoreType.DMA((9 * peers,)),
            pltpu.SemaphoreType.DMA((chunks * peers,)),
            pltpu.SemaphoreType.DMA((2,)),
            pltpu.SemaphoreType.DMA((6,)),
            pltpu.SemaphoreType.DMA((2 * n_seq,)),
        ],
        compiler_params=pltpu.CompilerParams(collective_id=0, has_side_effects=True),
    )(rows_send, weights)


def shards(tokens, grad_out, expert_ids, route_weights, gate_weight, up_weight, down_weight):
    expert_count = lax.axis_size("expert")
    seq_count = lax.axis_size("seq")
    tensor_count = lax.axis_size("tx") * lax.axis_size("core")
    core = lax.axis_index("core")
    local_count = gate_weight.shape[0]
    tok_rows = tokens.shape[0]
    model_width = tokens.shape[1]
    part_width = model_width // tensor_count
    per_peer = tok_rows // 6
    peer_count = expert_count * seq_count
    block_rows = local_count * per_peer
    slot_count = peer_count * block_rows
    flat_ids = expert_ids.reshape(-1)
    route_count = flat_ids.shape[0]
    onehot = (
        flat_ids[:, None] == jnp.arange(local_count * expert_count, dtype=jnp.int32)[None, :]
    ).astype(jnp.int32)
    before = jnp.cumsum(onehot, axis=0) - onehot
    ranking = jnp.sum(before * onehot, axis=1)
    local_expert = flat_ids % local_count
    dest_peer = flat_ids // local_count * seq_count + ranking % seq_count
    target = (dest_peer * local_count + local_expert) * per_peer + ranking // seq_count
    source = (
        jnp.full((slot_count,), -1, jnp.int32)
        .at[target]
        .set(jnp.arange(route_count, dtype=jnp.int32))
    )
    filled = source >= 0
    safe_source = jnp.maximum(source, 0)
    token_of = safe_source // 2
    weight_send = (
        route_weights.reshape(-1)[safe_source] * filled.astype(route_weights.dtype)
    ).reshape(peer_count, block_rows)
    own_part = lax.axis_index("tx") * 2 + core
    half = part_width
    tokens_half = lax.dynamic_slice_in_dim(tokens, own_part * half, half, axis=1)
    grad_half = lax.dynamic_slice_in_dim(grad_out, own_part * half, half, axis=1)
    rows_send = jnp.stack(
        [
            tokens_half[token_of].reshape(peer_count, block_rows, half),
            grad_half[token_of].reshape(peer_count, block_rows, half),
        ],
        axis=1,
    )
    weight_recv = lax.all_to_all(
        weight_send, ("expert", "seq"), split_axis=0, concat_axis=0, tiled=True
    )

    def join_halves(mine):
        both = jnp.broadcast_to(mine[None], (2,) + mine.shape)
        return lax.all_to_all(both, "core", split_axis=0, concat_axis=0, tiled=True)

    def by_expert(values):
        shaped = values.reshape((peer_count, local_count, per_peer) + values.shape[2:])
        return jnp.swapaxes(shaped, 0, 1).reshape(
            (local_count, peer_count * per_peer) + values.shape[2:]
        )

    def by_peer(values):
        shaped = values.reshape((local_count, peer_count, per_peer) + values.shape[2:])
        return jnp.swapaxes(shaped, 0, 1).reshape((peer_count, block_rows) + values.shape[2:])

    local_rows = gate_weight.shape[1]
    hidden_count = gate_weight.shape[2]
    rows_both, weights = exchange_rows(
        rows_send,
        jnp.stack([gate_weight, up_weight, down_weight]).reshape(
            3 * local_count, local_rows, hidden_count
        ),
        seq_count,
        lax.axis_size("tx"),
    )
    weights = weights.reshape(3, local_count, seq_count * local_rows, hidden_count)
    in_rows = jax.vmap(by_expert)(rows_both[:, :, 0])
    out_rows = jax.vmap(by_expert)(rows_both[:, :, 1])
    prob = by_expert(weight_recv).astype(jnp.float32)[:, :, None]
    gate_full, up_full, down_full = weights[0], weights[1], weights[2]
    hidden_count = gate_full.shape[2]
    gate_h, up_h, down_h = (
        w.reshape(local_count, tensor_count, half, hidden_count)
        for w in (gate_full, up_full, down_full)
    )
    pre_gate = jnp.einsum("cemd,ecdf->emf", in_rows, gate_h, preferred_element_type=jnp.float32)
    pre_up = jnp.einsum("cemd,ecdf->emf", in_rows, up_h, preferred_element_type=jnp.float32)
    sigmoid_gate = jax.nn.sigmoid(pre_gate)
    silu_gate = pre_gate * sigmoid_gate
    hidden = silu_gate * pre_up
    hidden_low = hidden.astype(jnp.bfloat16)
    back_proj = jnp.einsum("cemd,ecdf->emf", out_rows, down_h, preferred_element_type=jnp.float32)
    partial_scores = jnp.sum(hidden * back_proj, axis=2)
    scaled = (prob[None] * out_rows.astype(jnp.float32)).astype(jnp.bfloat16)
    hidden_grad = prob * back_proj
    up_grad = (hidden_grad * silu_gate).astype(jnp.bfloat16)
    gate_grad = (
        hidden_grad * pre_up * sigmoid_gate * (1.0 + pre_gate * (1.0 - sigmoid_gate))
    ).astype(jnp.bfloat16)
    gate_part = jnp.einsum("cemd,emf->ecdf", in_rows, gate_grad, preferred_element_type=jnp.float32)
    up_part = jnp.einsum("cemd,emf->ecdf", in_rows, up_grad, preferred_element_type=jnp.float32)
    down_part = jnp.einsum("cemd,emf->ecdf", scaled, hidden_low, preferred_element_type=jnp.float32)
    parts = jnp.stack([gate_part, up_part, down_part]).reshape(
        3, local_count, model_width, hidden_count
    ).astype(jnp.bfloat16)
    parts, gate_grad, up_grad = lax.optimization_barrier((parts, gate_grad, up_grad))
    reduced_parts = lax.psum_scatter(parts, "seq", scatter_dimension=2, tiled=True).astype(jnp.float32)
    grad_gate, grad_up, grad_down = reduced_parts[0], reduced_parts[1], reduced_parts[2]
    input_terms = jnp.einsum(
        "emf,ecdf->ecdm", gate_grad, gate_h, preferred_element_type=jnp.float32
    )
    input_terms = input_terms + jnp.einsum(
        "emf,ecdf->ecdm", up_grad, up_h, preferred_element_type=jnp.float32
    )
    rows_here = local_count * slot_count
    input_terms = jnp.swapaxes(
        input_terms.reshape(local_count, tensor_count, part_width, slot_count), 0, 1
    ).reshape(tensor_count, part_width, rows_here)
    score_pad = 16
    score_rows = jnp.zeros((tensor_count, score_pad, rows_here), jnp.float32)
    score_rows = score_rows.at[:, 0, :].set(partial_scores.reshape(1, rows_here))
    stacked = jnp.concatenate([input_terms, score_rows], axis=1).astype(jnp.bfloat16)
    tx_count = lax.axis_size("tx")
    stacked = stacked.reshape(tx_count, 2, part_width + score_pad, rows_here)
    pair = lax.all_to_all(stacked, "core", split_axis=1, concat_axis=1, tiled=True)
    pair = jnp.sum(pair.astype(jnp.float32), axis=1).astype(jnp.bfloat16)
    ring = lax.all_to_all(pair, "tx", split_axis=0, concat_axis=0, tiled=True)
    reduced = jnp.sum(ring.astype(jnp.float32), axis=0).astype(jnp.bfloat16)
    back_send = by_peer(
        jnp.swapaxes(reduced, 0, 1).reshape(local_count, slot_count, part_width + score_pad)
    )
    back_all = lax.all_to_all(
        back_send, ("expert", "seq"), split_axis=0, concat_axis=0, tiled=True
    ).astype(jnp.float32)
    back_all = back_all.reshape(slot_count, part_width + score_pad)[target]
    route_rows = back_all[:, :part_width].reshape(tok_rows, 2, part_width)
    grad_tokens = jnp.sum(route_rows, axis=1).astype(jnp.bfloat16)
    grad_route = back_all[:, part_width].reshape(tok_rows, 2)
    return (grad_tokens, grad_route, grad_gate, grad_up, grad_down)


def solution(mesh):
    shape = mesh.devices.shape
    mesh = jax.sharding.Mesh(
        mesh.devices.reshape(shape[0], shape[1], shape[2] // 2, 2), ("expert", "seq", "tx", "core")
    )
    tensor = ("tx", "core")
    placed = (
        P(("expert", "seq"), None),
        P(("expert", "seq"), None),
        P(("expert", "seq"), None),
        P(("expert", "seq"), None),
        P("expert", "seq", tensor),
        P("expert", "seq", tensor),
        P("expert", "seq", tensor),
    )
    return jax.shard_map(
        shards,
        mesh=mesh,
        in_specs=placed,
        out_specs=(
            P(("expert", "seq"), tensor),
            P(("expert", "seq"), None),
            P("expert", "seq", tensor),
            P("expert", "seq", tensor),
            P("expert", "seq", tensor),
        ),
        check_vma=False,
    )
```

```python
import functools

import jax
import jax.numpy as jnp
from jax import lax
from jax.experimental import pallas as pl
from jax.experimental.pallas import tpu as pltpu
from jax.sharding import PartitionSpec as P

MESH = pl.DeviceIdType.MESH


def exchange_kernel(n_seq, n_tx, peers, send_ref, out_ref, send_sem, recv_sem, local_sem):
    e = lax.axis_index("expert")
    s = lax.axis_index("seq")
    x = lax.axis_index("tx")
    c = lax.axis_index("core")
    me = e * n_seq + s
    other = 1 - c
    x_left = lax.rem(x + n_tx - 1, n_tx)
    x_right = lax.rem(x + 1, n_tx)
    x_far = lax.rem(x + 2, n_tx)
    own = x * 2 + c
    from_left = x_left * 2 + c
    from_right = x_right * 2 + c
    from_far = x_far * 2 + c
    left = (e, s, x_left, c)
    right = (e, s, x_right, c)
    partner = (e, s, x, other)

    def peer(k):
        q = lax.rem(me + k, peers)
        return q, (q // n_seq, q % n_seq, x, c)

    barrier = pltpu.get_barrier_semaphore()
    for k in range(1, peers):
        pl.semaphore_signal(barrier, inc=1, device_id=peer(k)[1], device_id_type=MESH)
    for where in (left, right, partner):
        pl.semaphore_signal(barrier, inc=1, device_id=where, device_id_type=MESH)
    pl.semaphore_wait(barrier, peers + 2)

    def remote(src, dst, slot, recv, where):
        return pltpu.make_async_remote_copy(
            src_ref=src,
            dst_ref=dst,
            send_sem=send_sem.at[slot],
            recv_sem=recv_sem.at[recv],
            device_id=where,
            device_id_type=MESH,
        )

    local = pltpu.make_async_copy(send_ref.at[:, me], out_ref.at[:, own, me], local_sem.at[0])
    local.start()
    for k in range(1, peers):
        q, where = peer(k)
        remote(send_ref.at[:, q], out_ref.at[:, own, me], q, own * peers + me, where).start()

    def arrived(chunk, p):
        block = out_ref.at[:, chunk, p]
        remote(block, block, 0, chunk * peers + p, partner).wait_recv()

    def forward(chunk, p, slot, where):
        block = out_ref.at[:, chunk, p]
        remote(block, block, slot, chunk * peers + p, where).start()

    local.wait()
    for k in range(peers):
        p = peer(k)[0]
        if k > 0:
            arrived(own, p)
        forward(own, p, peers + p, right)
        forward(own, p, 2 * peers + p, left)
        forward(own, p, 3 * peers + p, partner)

    def relay(chunk, onward, onward_parity, base):
        def body(i, carry):
            for parity in (0, 1):
                p = 2 * i + parity
                arrived(chunk, p)
                if onward is not None and parity == onward_parity:
                    forward(chunk, p, base + peers + p, onward)
                forward(chunk, p, base + p, partner)
            return carry

        lax.fori_loop(0, peers // 2, body, 0)

    relay(from_left, right, 0, 4 * peers)
    relay(from_right, left, 1, 6 * peers)
    relay(from_far, None, 0, 8 * peers)

    def partner_chunks(p, carry):
        for column in range(n_tx):
            arrived(column * 2 + other, p)
        return carry

    lax.fori_loop(0, peers, partner_chunks, 0)

    def drain(slot, carry):
        block = out_ref.at[:, own, 0]
        remote(block, block, slot, 0, partner).wait_send()
        return carry

    def drain_pairs(first, parity):
        def body(i, carry):
            return drain(first + 2 * i + parity, carry)

        lax.fori_loop(0, peers // 2, body, 0)

    for k in range(1, peers):
        drain(peer(k)[0], 0)
    lax.fori_loop(peers, 5 * peers, drain, 0)
    drain_pairs(5 * peers, 0)
    lax.fori_loop(6 * peers, 7 * peers, drain, 0)
    drain_pairs(7 * peers, 1)
    lax.fori_loop(8 * peers, 9 * peers, drain, 0)


def exchange_rows(rows_send, n_seq, n_tx):
    peers = rows_send.shape[1]
    chunks = 2 * n_tx
    return pl.pallas_call(
        functools.partial(exchange_kernel, n_seq, n_tx, peers),
        out_shape=jax.ShapeDtypeStruct(
            (rows_send.shape[0], chunks) + rows_send.shape[1:], rows_send.dtype
        ),
        in_specs=[pl.BlockSpec(memory_space=pl.ANY)],
        out_specs=pl.BlockSpec(memory_space=pl.ANY),
        scratch_shapes=[
            pltpu.SemaphoreType.DMA((9 * peers,)),
            pltpu.SemaphoreType.DMA((chunks * peers,)),
            pltpu.SemaphoreType.DMA((1,)),
        ],
        compiler_params=pltpu.CompilerParams(collective_id=0, has_side_effects=True),
    )(rows_send)


def shards(tokens, grad_out, expert_ids, route_weights, gate_weight, up_weight, down_weight):
    expert_count = lax.axis_size("expert")
    seq_count = lax.axis_size("seq")
    tensor_count = lax.axis_size("tx") * lax.axis_size("core")
    core = lax.axis_index("core")
    local_count = gate_weight.shape[0]
    tok_rows = tokens.shape[0]
    model_width = tokens.shape[1]
    part_width = model_width // tensor_count
    per_peer = tok_rows // 6
    peer_count = expert_count * seq_count
    block_rows = local_count * per_peer
    slot_count = peer_count * block_rows
    flat_ids = expert_ids.reshape(-1)
    route_count = flat_ids.shape[0]
    onehot = (
        flat_ids[:, None] == jnp.arange(local_count * expert_count, dtype=jnp.int32)[None, :]
    ).astype(jnp.int32)
    before = jnp.cumsum(onehot, axis=0) - onehot
    ranking = jnp.sum(before * onehot, axis=1)
    local_expert = flat_ids % local_count
    dest_peer = flat_ids // local_count * seq_count + ranking % seq_count
    target = (dest_peer * local_count + local_expert) * per_peer + ranking // seq_count
    source = (
        jnp.full((slot_count,), -1, jnp.int32)
        .at[target]
        .set(jnp.arange(route_count, dtype=jnp.int32))
    )
    filled = source >= 0
    safe_source = jnp.maximum(source, 0)
    token_of = safe_source // 2
    weight_send = (
        route_weights.reshape(-1)[safe_source] * filled.astype(route_weights.dtype)
    ).reshape(peer_count, block_rows)
    own_part = lax.axis_index("tx") * 2 + core
    half = part_width
    tokens_half = lax.dynamic_slice_in_dim(tokens, own_part * half, half, axis=1)
    grad_half = lax.dynamic_slice_in_dim(grad_out, own_part * half, half, axis=1)
    rows_send = jnp.stack(
        [
            tokens_half[token_of].reshape(peer_count, block_rows, half),
            grad_half[token_of].reshape(peer_count, block_rows, half),
        ],
        axis=0,
    )
    weight_recv = lax.all_to_all(
        weight_send, ("expert", "seq"), split_axis=0, concat_axis=0, tiled=True
    )

    def join_halves(mine):
        both = jnp.broadcast_to(mine[None], (2,) + mine.shape)
        return lax.all_to_all(both, "core", split_axis=0, concat_axis=0, tiled=True)

    def by_expert(values):
        shaped = values.reshape((peer_count, local_count, per_peer) + values.shape[2:])
        return jnp.swapaxes(shaped, 0, 1).reshape(
            (local_count, peer_count * per_peer) + values.shape[2:]
        )

    def by_peer(values):
        shaped = values.reshape((local_count, peer_count, per_peer) + values.shape[2:])
        return jnp.swapaxes(shaped, 0, 1).reshape((peer_count, block_rows) + values.shape[2:])

    rows_both = exchange_rows(rows_send, seq_count, lax.axis_size("tx"))
    in_rows = jax.vmap(by_expert)(rows_both[0])
    out_rows = jax.vmap(by_expert)(rows_both[1])
    prob = by_expert(weight_recv).astype(jnp.float32)[:, :, None]
    weights = lax.all_gather(
        jnp.stack([gate_weight, up_weight, down_weight]), "seq", axis=2, tiled=True
    )
    gate_full, up_full, down_full = weights[0], weights[1], weights[2]
    hidden_count = gate_full.shape[2]
    gate_h, up_h, down_h = (
        w.reshape(local_count, tensor_count, half, hidden_count)
        for w in (gate_full, up_full, down_full)
    )
    pre_gate = jnp.einsum("cemd,ecdf->emf", in_rows, gate_h, preferred_element_type=jnp.float32)
    pre_up = jnp.einsum("cemd,ecdf->emf", in_rows, up_h, preferred_element_type=jnp.float32)
    sigmoid_gate = jax.nn.sigmoid(pre_gate)
    silu_gate = pre_gate * sigmoid_gate
    hidden = silu_gate * pre_up
    hidden_low = hidden.astype(jnp.bfloat16)
    back_proj = jnp.einsum("cemd,ecdf->emf", out_rows, down_h, preferred_element_type=jnp.float32)
    partial_scores = jnp.sum(hidden * back_proj, axis=2)
    scaled = (prob[None] * out_rows.astype(jnp.float32)).astype(jnp.bfloat16)
    hidden_grad = prob * back_proj
    up_grad = (hidden_grad * silu_gate).astype(jnp.bfloat16)
    gate_grad = (
        hidden_grad * pre_up * sigmoid_gate * (1.0 + pre_gate * (1.0 - sigmoid_gate))
    ).astype(jnp.bfloat16)
    gate_part = jnp.einsum("cemd,emf->ecdf", in_rows, gate_grad, preferred_element_type=jnp.float32)
    up_part = jnp.einsum("cemd,emf->ecdf", in_rows, up_grad, preferred_element_type=jnp.float32)
    down_part = jnp.einsum("cemd,emf->ecdf", scaled, hidden_low, preferred_element_type=jnp.float32)
    parts = jnp.stack([gate_part, up_part, down_part]).reshape(
        3, local_count, model_width, hidden_count
    ).astype(jnp.bfloat16)
    parts, gate_grad, up_grad = lax.optimization_barrier((parts, gate_grad, up_grad))
    reduced_parts = lax.psum_scatter(parts, "seq", scatter_dimension=2, tiled=True).astype(jnp.float32)
    grad_gate, grad_up, grad_down = reduced_parts[0], reduced_parts[1], reduced_parts[2]
    input_terms = jnp.einsum(
        "emf,ecdf->ecdm", gate_grad, gate_h, preferred_element_type=jnp.float32
    )
    input_terms = input_terms + jnp.einsum(
        "emf,ecdf->ecdm", up_grad, up_h, preferred_element_type=jnp.float32
    )
    rows_here = local_count * slot_count
    input_terms = jnp.swapaxes(
        input_terms.reshape(local_count, tensor_count, part_width, slot_count), 0, 1
    ).reshape(tensor_count, part_width, rows_here)
    score_pad = 16
    score_rows = jnp.zeros((tensor_count, score_pad, rows_here), jnp.float32)
    score_rows = score_rows.at[:, 0, :].set(partial_scores.reshape(1, rows_here))
    stacked = jnp.concatenate([input_terms, score_rows], axis=1).astype(jnp.bfloat16)
    tx_count = lax.axis_size("tx")
    stacked = stacked.reshape(tx_count, 2, part_width + score_pad, rows_here)
    pair = lax.all_to_all(stacked, "core", split_axis=1, concat_axis=1, tiled=True)
    pair = jnp.sum(pair.astype(jnp.float32), axis=1).astype(jnp.bfloat16)
    ring = lax.all_to_all(pair, "tx", split_axis=0, concat_axis=0, tiled=True)
    reduced = jnp.sum(ring.astype(jnp.float32), axis=0).astype(jnp.bfloat16)
    back_send = by_peer(
        jnp.swapaxes(reduced, 0, 1).reshape(local_count, slot_count, part_width + score_pad)
    )
    back_all = lax.all_to_all(
        back_send, ("expert", "seq"), split_axis=0, concat_axis=0, tiled=True
    ).astype(jnp.float32)
    back_all = back_all.reshape(slot_count, part_width + score_pad)[target]
    route_rows = back_all[:, :part_width].reshape(tok_rows, 2, part_width)
    grad_tokens = jnp.sum(route_rows, axis=1).astype(jnp.bfloat16)
    grad_route = back_all[:, part_width].reshape(tok_rows, 2)
    return (grad_tokens, grad_route, grad_gate, grad_up, grad_down)


def solution(mesh):
    shape = mesh.devices.shape
    mesh = jax.sharding.Mesh(
        mesh.devices.reshape(shape[0], shape[1], shape[2] // 2, 2), ("expert", "seq", "tx", "core")
    )
    tensor = ("tx", "core")
    placed = (
        P(("expert", "seq"), None),
        P(("expert", "seq"), None),
        P(("expert", "seq"), None),
        P(("expert", "seq"), None),
        P("expert", "seq", tensor),
        P("expert", "seq", tensor),
        P("expert", "seq", tensor),
    )
    return jax.shard_map(
        shards,
        mesh=mesh,
        in_specs=placed,
        out_specs=(
            P(("expert", "seq"), tensor),
            P(("expert", "seq"), None),
            P("expert", "seq", tensor),
            P("expert", "seq", tensor),
            P("expert", "seq", tensor),
        ),
        check_vma=False,
    )
```

```python
import functools

import jax
import jax.numpy as jnp
from jax import lax
from jax.experimental import pallas as pl
from jax.experimental.pallas import tpu as pltpu
from jax.sharding import PartitionSpec as P

MESH = pl.DeviceIdType.MESH


def exchange_kernel(
    n_seq, n_tx, peers, tok_send, grad_send, tok_out, grad_out, send_sem, recv_sem, local_sem
):
    sends = (tok_send, grad_send)
    outs = (tok_out, grad_out)
    e = lax.axis_index("expert")
    s = lax.axis_index("seq")
    x = lax.axis_index("tx")
    c = lax.axis_index("core")
    me = e * n_seq + s
    other = 1 - c
    x_left = lax.rem(x + n_tx - 1, n_tx)
    x_right = lax.rem(x + 1, n_tx)
    x_far = lax.rem(x + 2, n_tx)
    own = x * 2 + c
    from_left = x_left * 2 + c
    from_right = x_right * 2 + c
    from_far = x_far * 2 + c
    left = (e, s, x_left, c)
    right = (e, s, x_right, c)
    partner = (e, s, x, other)

    def peer(k):
        q = lax.rem(me + k, peers)
        return q, (q // n_seq, q % n_seq, x, c)

    barrier = pltpu.get_barrier_semaphore()
    for k in range(1, peers):
        pl.semaphore_signal(barrier, inc=1, device_id=peer(k)[1], device_id_type=MESH)
    for where in (left, right, partner):
        pl.semaphore_signal(barrier, inc=1, device_id=where, device_id_type=MESH)
    pl.semaphore_wait(barrier, peers + 2)

    def remote(kind, src, dst, slot, recv, where):
        return pltpu.make_async_remote_copy(
            src_ref=src,
            dst_ref=dst,
            send_sem=send_sem.at[kind, slot],
            recv_sem=recv_sem.at[kind, recv],
            device_id=where,
            device_id_type=MESH,
        )

    locals_ = [
        pltpu.make_async_copy(sends[kind].at[me], outs[kind].at[own, me], local_sem.at[kind])
        for kind in range(2)
    ]
    for copy in locals_:
        copy.start()
    for k in range(1, peers):
        q, where = peer(k)
        for kind in range(2):
            remote(
                kind, sends[kind].at[q], outs[kind].at[own, me], q, own * peers + me, where
            ).start()

    def arrived(chunk, p):
        for kind in range(2):
            block = outs[kind].at[chunk, p]
            remote(kind, block, block, 0, chunk * peers + p, partner).wait_recv()

    def forward(chunk, p, slot, where):
        for kind in range(2):
            block = outs[kind].at[chunk, p]
            remote(kind, block, block, slot, chunk * peers + p, where).start()

    for copy in locals_:
        copy.wait()
    for k in range(peers):
        p = peer(k)[0]
        if k > 0:
            arrived(own, p)
        forward(own, p, peers + p, right)
        forward(own, p, 2 * peers + p, left)
        forward(own, p, 3 * peers + p, partner)

    def relay(chunk, onward, onward_parity, base):
        def body(i, carry):
            for parity in (0, 1):
                p = 2 * i + parity
                arrived(chunk, p)
                if onward is not None and parity == onward_parity:
                    forward(chunk, p, base + peers + p, onward)
                forward(chunk, p, base + p, partner)
            return carry

        lax.fori_loop(0, peers // 2, body, 0)

    relay(from_left, right, 0, 4 * peers)
    relay(from_right, left, 1, 6 * peers)
    relay(from_far, None, 0, 8 * peers)

    def partner_chunks(p, carry):
        for column in range(n_tx):
            arrived(column * 2 + other, p)
        return carry

    lax.fori_loop(0, peers, partner_chunks, 0)

    def drain(slot, carry):
        for kind in range(2):
            block = outs[kind].at[own, 0]
            remote(kind, block, block, slot, 0, partner).wait_send()
        return carry

    def drain_pairs(first, parity):
        def body(i, carry):
            return drain(first + 2 * i + parity, carry)

        lax.fori_loop(0, peers // 2, body, 0)

    for k in range(1, peers):
        drain(peer(k)[0], 0)
    lax.fori_loop(peers, 5 * peers, drain, 0)
    drain_pairs(5 * peers, 0)
    lax.fori_loop(6 * peers, 7 * peers, drain, 0)
    drain_pairs(7 * peers, 1)
    lax.fori_loop(8 * peers, 9 * peers, drain, 0)


def exchange_rows(tok_send, grad_send, n_seq, n_tx):
    peers = tok_send.shape[0]
    chunks = 2 * n_tx
    shape = jax.ShapeDtypeStruct((chunks,) + tok_send.shape, tok_send.dtype)
    return pl.pallas_call(
        functools.partial(exchange_kernel, n_seq, n_tx, peers),
        out_shape=(shape, shape),
        in_specs=[pl.BlockSpec(memory_space=pl.ANY)] * 2,
        out_specs=(pl.BlockSpec(memory_space=pl.ANY), pl.BlockSpec(memory_space=pl.ANY)),
        scratch_shapes=[
            pltpu.SemaphoreType.DMA((2, 9 * peers)),
            pltpu.SemaphoreType.DMA((2, chunks * peers)),
            pltpu.SemaphoreType.DMA((2,)),
        ],
        compiler_params=pltpu.CompilerParams(collective_id=0, has_side_effects=True),
    )(tok_send, grad_send)


def shards(tokens, grad_out, expert_ids, route_weights, gate_weight, up_weight, down_weight):
    expert_count = lax.axis_size("expert")
    seq_count = lax.axis_size("seq")
    tensor_count = lax.axis_size("tx") * lax.axis_size("core")
    core = lax.axis_index("core")
    local_count = gate_weight.shape[0]
    tok_rows = tokens.shape[0]
    model_width = tokens.shape[1]
    part_width = model_width // tensor_count
    per_peer = tok_rows // 6
    peer_count = expert_count * seq_count
    block_rows = local_count * per_peer
    slot_count = peer_count * block_rows
    flat_ids = expert_ids.reshape(-1)
    route_count = flat_ids.shape[0]
    onehot = (
        flat_ids[:, None] == jnp.arange(local_count * expert_count, dtype=jnp.int32)[None, :]
    ).astype(jnp.int32)
    before = jnp.cumsum(onehot, axis=0) - onehot
    ranking = jnp.sum(before * onehot, axis=1)
    local_expert = flat_ids % local_count
    dest_peer = flat_ids // local_count * seq_count + ranking % seq_count
    target = (dest_peer * local_count + local_expert) * per_peer + ranking // seq_count
    source = (
        jnp.full((slot_count,), -1, jnp.int32)
        .at[target]
        .set(jnp.arange(route_count, dtype=jnp.int32))
    )
    filled = source >= 0
    safe_source = jnp.maximum(source, 0)
    token_of = safe_source // 2
    weight_send = (
        route_weights.reshape(-1)[safe_source] * filled.astype(route_weights.dtype)
    ).reshape(peer_count, block_rows)
    own_part = lax.axis_index("tx") * 2 + core
    half = part_width
    tokens_half = lax.dynamic_slice_in_dim(tokens, own_part * half, half, axis=1)
    grad_half = lax.dynamic_slice_in_dim(grad_out, own_part * half, half, axis=1)
    tok_send = tokens_half[token_of].reshape(peer_count, block_rows, half)
    grad_send = grad_half[token_of].reshape(peer_count, block_rows, half)
    weight_recv = lax.all_to_all(
        weight_send, ("expert", "seq"), split_axis=0, concat_axis=0, tiled=True
    )

    def join_halves(mine):
        both = jnp.broadcast_to(mine[None], (2,) + mine.shape)
        return lax.all_to_all(both, "core", split_axis=0, concat_axis=0, tiled=True)

    def by_expert(values):
        shaped = values.reshape((peer_count, local_count, per_peer) + values.shape[2:])
        return jnp.swapaxes(shaped, 0, 1).reshape(
            (local_count, peer_count * per_peer) + values.shape[2:]
        )

    def by_peer(values):
        shaped = values.reshape((local_count, peer_count, per_peer) + values.shape[2:])
        return jnp.swapaxes(shaped, 0, 1).reshape((peer_count, block_rows) + values.shape[2:])

    tok_recv, grad_recv = exchange_rows(tok_send, grad_send, seq_count, lax.axis_size("tx"))
    in_rows = jax.vmap(by_expert)(tok_recv)
    out_rows = jax.vmap(by_expert)(grad_recv)
    prob = by_expert(weight_recv).astype(jnp.float32)[:, :, None]
    weights = lax.all_gather(
        jnp.stack([gate_weight, up_weight, down_weight]), "seq", axis=2, tiled=True
    )
    gate_full, up_full, down_full = weights[0], weights[1], weights[2]
    hidden_count = gate_full.shape[2]
    gate_h, up_h, down_h = (
        w.reshape(local_count, tensor_count, half, hidden_count)
        for w in (gate_full, up_full, down_full)
    )
    pre_gate = jnp.einsum("cemd,ecdf->emf", in_rows, gate_h, preferred_element_type=jnp.float32)
    pre_up = jnp.einsum("cemd,ecdf->emf", in_rows, up_h, preferred_element_type=jnp.float32)
    sigmoid_gate = jax.nn.sigmoid(pre_gate)
    silu_gate = pre_gate * sigmoid_gate
    hidden = silu_gate * pre_up
    hidden_low = hidden.astype(jnp.bfloat16)
    back_proj = jnp.einsum("cemd,ecdf->emf", out_rows, down_h, preferred_element_type=jnp.float32)
    partial_scores = jnp.sum(hidden * back_proj, axis=2)
    scaled = (prob[None] * out_rows.astype(jnp.float32)).astype(jnp.bfloat16)
    hidden_grad = prob * back_proj
    up_grad = (hidden_grad * silu_gate).astype(jnp.bfloat16)
    gate_grad = (
        hidden_grad * pre_up * sigmoid_gate * (1.0 + pre_gate * (1.0 - sigmoid_gate))
    ).astype(jnp.bfloat16)
    gate_part = jnp.einsum("cemd,emf->ecdf", in_rows, gate_grad, preferred_element_type=jnp.float32)
    up_part = jnp.einsum("cemd,emf->ecdf", in_rows, up_grad, preferred_element_type=jnp.float32)
    down_part = jnp.einsum("cemd,emf->ecdf", scaled, hidden_low, preferred_element_type=jnp.float32)
    parts = jnp.stack([gate_part, up_part, down_part]).reshape(
        3, local_count, model_width, hidden_count
    ).astype(jnp.bfloat16)
    parts, gate_grad, up_grad = lax.optimization_barrier((parts, gate_grad, up_grad))
    reduced_parts = lax.psum_scatter(parts, "seq", scatter_dimension=2, tiled=True).astype(jnp.float32)
    grad_gate, grad_up, grad_down = reduced_parts[0], reduced_parts[1], reduced_parts[2]
    input_terms = jnp.einsum(
        "emf,ecdf->ecdm", gate_grad, gate_h, preferred_element_type=jnp.float32
    )
    input_terms = input_terms + jnp.einsum(
        "emf,ecdf->ecdm", up_grad, up_h, preferred_element_type=jnp.float32
    )
    rows_here = local_count * slot_count
    input_terms = jnp.swapaxes(
        input_terms.reshape(local_count, tensor_count, part_width, slot_count), 0, 1
    ).reshape(tensor_count, part_width, rows_here)
    score_pad = 16
    score_rows = jnp.zeros((tensor_count, score_pad, rows_here), jnp.float32)
    score_rows = score_rows.at[:, 0, :].set(partial_scores.reshape(1, rows_here))
    stacked = jnp.concatenate([input_terms, score_rows], axis=1).astype(jnp.bfloat16)
    tx_count = lax.axis_size("tx")
    stacked = stacked.reshape(tx_count, 2, part_width + score_pad, rows_here)
    pair = lax.all_to_all(stacked, "core", split_axis=1, concat_axis=1, tiled=True)
    pair = jnp.sum(pair.astype(jnp.float32), axis=1).astype(jnp.bfloat16)
    ring = lax.all_to_all(pair, "tx", split_axis=0, concat_axis=0, tiled=True)
    reduced = jnp.sum(ring.astype(jnp.float32), axis=0).astype(jnp.bfloat16)
    back_send = by_peer(
        jnp.swapaxes(reduced, 0, 1).reshape(local_count, slot_count, part_width + score_pad)
    )
    back_all = lax.all_to_all(
        back_send, ("expert", "seq"), split_axis=0, concat_axis=0, tiled=True
    ).astype(jnp.float32)
    back_all = back_all.reshape(slot_count, part_width + score_pad)[target]
    route_rows = back_all[:, :part_width].reshape(tok_rows, 2, part_width)
    grad_tokens = jnp.sum(route_rows, axis=1).astype(jnp.bfloat16)
    grad_route = back_all[:, part_width].reshape(tok_rows, 2)
    return (grad_tokens, grad_route, grad_gate, grad_up, grad_down)


def solution(mesh):
    shape = mesh.devices.shape
    mesh = jax.sharding.Mesh(
        mesh.devices.reshape(shape[0], shape[1], shape[2] // 2, 2), ("expert", "seq", "tx", "core")
    )
    tensor = ("tx", "core")
    placed = (
        P(("expert", "seq"), None),
        P(("expert", "seq"), None),
        P(("expert", "seq"), None),
        P(("expert", "seq"), None),
        P("expert", "seq", tensor),
        P("expert", "seq", tensor),
        P("expert", "seq", tensor),
    )
    return jax.shard_map(
        shards,
        mesh=mesh,
        in_specs=placed,
        out_specs=(
            P(("expert", "seq"), tensor),
            P(("expert", "seq"), None),
            P("expert", "seq", tensor),
            P("expert", "seq", tensor),
            P("expert", "seq", tensor),
        ),
        check_vma=False,
    )
```

```python
import functools

import jax
import jax.numpy as jnp
from jax import lax
from jax.experimental import pallas as pl
from jax.experimental.pallas import tpu as pltpu
from jax.sharding import PartitionSpec as P

MESH = pl.DeviceIdType.MESH


def exchange_kernel(
    n_seq, n_tx, peers, tok_send, grad_send, tok_out, grad_out, send_sem, recv_sem, local_sem
):
    sends = (tok_send, grad_send)
    outs = (tok_out, grad_out)
    e = lax.axis_index("expert")
    s = lax.axis_index("seq")
    x = lax.axis_index("tx")
    c = lax.axis_index("core")
    me = e * n_seq + s
    other = 1 - c
    x_left = lax.rem(x + n_tx - 1, n_tx)
    x_right = lax.rem(x + 1, n_tx)
    x_far = lax.rem(x + 2, n_tx)
    own = x * 2 + c
    from_left = x_left * 2 + c
    from_right = x_right * 2 + c
    from_far = x_far * 2 + c
    left = (e, s, x_left, c)
    right = (e, s, x_right, c)
    partner = (e, s, x, other)

    def peer(k):
        q = lax.rem(me + k, peers)
        return q, (q // n_seq, q % n_seq, x, c)

    barrier = pltpu.get_barrier_semaphore()
    for k in range(1, peers):
        pl.semaphore_signal(barrier, inc=1, device_id=peer(k)[1], device_id_type=MESH)
    for where in (left, right, partner):
        pl.semaphore_signal(barrier, inc=1, device_id=where, device_id_type=MESH)
    pl.semaphore_wait(barrier, peers + 2)

    def remote(kind, src, dst, slot, recv, where):
        return pltpu.make_async_remote_copy(
            src_ref=src,
            dst_ref=dst,
            send_sem=send_sem.at[kind, slot],
            recv_sem=recv_sem.at[kind, recv],
            device_id=where,
            device_id_type=MESH,
        )

    locals_ = [
        pltpu.make_async_copy(sends[kind].at[me], outs[kind].at[own, me], local_sem.at[kind])
        for kind in range(2)
    ]
    for copy in locals_:
        copy.start()
    for k in range(1, peers):
        q, where = peer(k)
        for kind in range(2):
            remote(
                kind, sends[kind].at[q], outs[kind].at[own, me], q, own * peers + me, where
            ).start()

    def arrived(chunk, p):
        for kind in range(2):
            block = outs[kind].at[chunk, p]
            remote(kind, block, block, 0, chunk * peers + p, partner).wait_recv()

    def forward(chunk, p, slot, where):
        for kind in range(2):
            block = outs[kind].at[chunk, p]
            remote(kind, block, block, slot, chunk * peers + p, where).start()

    for copy in locals_:
        copy.wait()
    for k in range(peers):
        p = peer(k)[0]
        if k > 0:
            arrived(own, p)
        forward(own, p, peers + p, right)
        forward(own, p, 2 * peers + p, left)
        forward(own, p, 3 * peers + p, partner)

    def relay(chunk, onward, onward_parity, base):
        def body(i, carry):
            for parity in (0, 1):
                p = 2 * i + parity
                arrived(chunk, p)
                if onward is not None and parity == onward_parity:
                    forward(chunk, p, base + peers + p, onward)
                forward(chunk, p, base + p, partner)
            return carry

        lax.fori_loop(0, peers // 2, body, 0)

    relay(from_left, right, 0, 4 * peers)
    relay(from_right, left, 1, 6 * peers)
    relay(from_far, None, 0, 8 * peers)

    def partner_chunks(p, carry):
        for column in range(n_tx):
            arrived(column * 2 + other, p)
        return carry

    lax.fori_loop(0, peers, partner_chunks, 0)

    def drain(slot, carry):
        for kind in range(2):
            block = outs[kind].at[own, 0]
            remote(kind, block, block, slot, 0, partner).wait_send()
        return carry

    def drain_pairs(first, parity):
        def body(i, carry):
            return drain(first + 2 * i + parity, carry)

        lax.fori_loop(0, peers // 2, body, 0)

    for k in range(1, peers):
        drain(peer(k)[0], 0)
    lax.fori_loop(peers, 5 * peers, drain, 0)
    drain_pairs(5 * peers, 0)
    lax.fori_loop(6 * peers, 7 * peers, drain, 0)
    drain_pairs(7 * peers, 1)
    lax.fori_loop(8 * peers, 9 * peers, drain, 0)


def exchange_rows(tok_send, grad_send, n_seq, n_tx):
    peers = tok_send.shape[0]
    chunks = 2 * n_tx
    shape = jax.ShapeDtypeStruct((chunks,) + tok_send.shape, tok_send.dtype)
    return pl.pallas_call(
        functools.partial(exchange_kernel, n_seq, n_tx, peers),
        out_shape=(shape, shape),
        in_specs=[pl.BlockSpec(memory_space=pl.ANY)] * 2,
        out_specs=(pl.BlockSpec(memory_space=pl.ANY), pl.BlockSpec(memory_space=pl.ANY)),
        scratch_shapes=[
            pltpu.SemaphoreType.DMA((2, 9 * peers)),
            pltpu.SemaphoreType.DMA((2, chunks * peers)),
            pltpu.SemaphoreType.DMA((2,)),
        ],
        compiler_params=pltpu.CompilerParams(collective_id=0, has_side_effects=True),
    )(tok_send, grad_send)


def shards(tokens, grad_out, expert_ids, route_weights, gate_weight, up_weight, down_weight):
    expert_count = lax.axis_size("expert")
    seq_count = lax.axis_size("seq")
    tensor_count = lax.axis_size("tx") * lax.axis_size("core")
    core = lax.axis_index("core")
    local_count = gate_weight.shape[0]
    tok_rows = tokens.shape[0]
    model_width = tokens.shape[1]
    part_width = model_width // tensor_count
    per_peer = tok_rows // 6
    peer_count = expert_count * seq_count
    block_rows = local_count * per_peer
    slot_count = peer_count * block_rows
    flat_ids = expert_ids.reshape(-1)
    route_count = flat_ids.shape[0]
    onehot = (
        flat_ids[:, None] == jnp.arange(local_count * expert_count, dtype=jnp.int32)[None, :]
    ).astype(jnp.int32)
    before = jnp.cumsum(onehot, axis=0) - onehot
    ranking = jnp.sum(before * onehot, axis=1)
    local_expert = flat_ids % local_count
    dest_peer = flat_ids // local_count * seq_count + ranking % seq_count
    target = (dest_peer * local_count + local_expert) * per_peer + ranking // seq_count
    source = (
        jnp.full((slot_count,), -1, jnp.int32)
        .at[target]
        .set(jnp.arange(route_count, dtype=jnp.int32))
    )
    filled = source >= 0
    safe_source = jnp.maximum(source, 0)
    token_of = safe_source // 2
    weight_send = (
        route_weights.reshape(-1)[safe_source] * filled.astype(route_weights.dtype)
    ).reshape(peer_count, block_rows)
    own_part = lax.axis_index("tx") * 2 + core
    half = part_width
    tokens_half = lax.dynamic_slice_in_dim(tokens, own_part * half, half, axis=1)
    grad_half = lax.dynamic_slice_in_dim(grad_out, own_part * half, half, axis=1)
    tok_send = tokens_half[token_of].reshape(peer_count, block_rows, half)
    grad_send = grad_half[token_of].reshape(peer_count, block_rows, half)

    def join_halves(mine):
        both = jnp.broadcast_to(mine[None], (2,) + mine.shape)
        return lax.all_to_all(both, "core", split_axis=0, concat_axis=0, tiled=True)

    def by_expert(values):
        shaped = values.reshape((peer_count, local_count, per_peer) + values.shape[2:])
        return jnp.swapaxes(shaped, 0, 1).reshape(
            (local_count, peer_count * per_peer) + values.shape[2:]
        )

    def by_peer(values):
        shaped = values.reshape((local_count, peer_count, per_peer) + values.shape[2:])
        return jnp.swapaxes(shaped, 0, 1).reshape((peer_count, block_rows) + values.shape[2:])

    tok_recv, grad_recv = exchange_rows(tok_send, grad_send, seq_count, lax.axis_size("tx"))
    weight_send, tok_recv = lax.optimization_barrier((weight_send, tok_recv))
    weight_recv = lax.all_to_all(
        weight_send, ("expert", "seq"), split_axis=0, concat_axis=0, tiled=True
    )
    in_rows = jax.vmap(by_expert)(tok_recv)
    out_rows = jax.vmap(by_expert)(grad_recv)
    prob = by_expert(weight_recv).astype(jnp.float32)[:, :, None]
    weights = lax.all_gather(
        jnp.stack([gate_weight, up_weight, down_weight]), "seq", axis=2, tiled=True
    )
    gate_full, up_full, down_full = weights[0], weights[1], weights[2]
    hidden_count = gate_full.shape[2]
    gate_h, up_h, down_h = (
        w.reshape(local_count, tensor_count, half, hidden_count)
        for w in (gate_full, up_full, down_full)
    )
    pre_gate = jnp.einsum("cemd,ecdf->emf", in_rows, gate_h, preferred_element_type=jnp.float32)
    pre_up = jnp.einsum("cemd,ecdf->emf", in_rows, up_h, preferred_element_type=jnp.float32)
    sigmoid_gate = jax.nn.sigmoid(pre_gate)
    silu_gate = pre_gate * sigmoid_gate
    hidden = silu_gate * pre_up
    hidden_low = hidden.astype(jnp.bfloat16)
    back_proj = jnp.einsum("cemd,ecdf->emf", out_rows, down_h, preferred_element_type=jnp.float32)
    partial_scores = jnp.sum(hidden * back_proj, axis=2)
    scaled = (prob[None] * out_rows.astype(jnp.float32)).astype(jnp.bfloat16)
    hidden_grad = prob * back_proj
    up_grad = (hidden_grad * silu_gate).astype(jnp.bfloat16)
    gate_grad = (
        hidden_grad * pre_up * sigmoid_gate * (1.0 + pre_gate * (1.0 - sigmoid_gate))
    ).astype(jnp.bfloat16)
    gate_part = jnp.einsum("cemd,emf->ecdf", in_rows, gate_grad, preferred_element_type=jnp.float32)
    up_part = jnp.einsum("cemd,emf->ecdf", in_rows, up_grad, preferred_element_type=jnp.float32)
    down_part = jnp.einsum("cemd,emf->ecdf", scaled, hidden_low, preferred_element_type=jnp.float32)
    parts = jnp.stack([gate_part, up_part, down_part]).reshape(
        3, local_count, model_width, hidden_count
    ).astype(jnp.bfloat16)
    parts, gate_grad, up_grad = lax.optimization_barrier((parts, gate_grad, up_grad))
    reduced_parts = lax.psum_scatter(parts, "seq", scatter_dimension=2, tiled=True).astype(jnp.float32)
    grad_gate, grad_up, grad_down = reduced_parts[0], reduced_parts[1], reduced_parts[2]
    input_terms = jnp.einsum(
        "emf,ecdf->ecdm", gate_grad, gate_h, preferred_element_type=jnp.float32
    )
    input_terms = input_terms + jnp.einsum(
        "emf,ecdf->ecdm", up_grad, up_h, preferred_element_type=jnp.float32
    )
    rows_here = local_count * slot_count
    input_terms = jnp.swapaxes(
        input_terms.reshape(local_count, tensor_count, part_width, slot_count), 0, 1
    ).reshape(tensor_count, part_width, rows_here)
    score_pad = 16
    score_rows = jnp.zeros((tensor_count, score_pad, rows_here), jnp.float32)
    score_rows = score_rows.at[:, 0, :].set(partial_scores.reshape(1, rows_here))
    stacked = jnp.concatenate([input_terms, score_rows], axis=1).astype(jnp.bfloat16)
    tx_count = lax.axis_size("tx")
    stacked = stacked.reshape(tx_count, 2, part_width + score_pad, rows_here)
    pair = lax.all_to_all(stacked, "core", split_axis=1, concat_axis=1, tiled=True)
    pair = jnp.sum(pair.astype(jnp.float32), axis=1).astype(jnp.bfloat16)
    ring = lax.all_to_all(pair, "tx", split_axis=0, concat_axis=0, tiled=True)
    reduced = jnp.sum(ring.astype(jnp.float32), axis=0).astype(jnp.bfloat16)
    back_send = by_peer(
        jnp.swapaxes(reduced, 0, 1).reshape(local_count, slot_count, part_width + score_pad)
    )
    back_all = lax.all_to_all(
        back_send, ("expert", "seq"), split_axis=0, concat_axis=0, tiled=True
    ).astype(jnp.float32)
    back_all = back_all.reshape(slot_count, part_width + score_pad)[target]
    route_rows = back_all[:, :part_width].reshape(tok_rows, 2, part_width)
    grad_tokens = jnp.sum(route_rows, axis=1).astype(jnp.bfloat16)
    grad_route = back_all[:, part_width].reshape(tok_rows, 2)
    return (grad_tokens, grad_route, grad_gate, grad_up, grad_down)


def solution(mesh):
    shape = mesh.devices.shape
    mesh = jax.sharding.Mesh(
        mesh.devices.reshape(shape[0], shape[1], shape[2] // 2, 2), ("expert", "seq", "tx", "core")
    )
    tensor = ("tx", "core")
    placed = (
        P(("expert", "seq"), None),
        P(("expert", "seq"), None),
        P(("expert", "seq"), None),
        P(("expert", "seq"), None),
        P("expert", "seq", tensor),
        P("expert", "seq", tensor),
        P("expert", "seq", tensor),
    )
    return jax.shard_map(
        shards,
        mesh=mesh,
        in_specs=placed,
        out_specs=(
            P(("expert", "seq"), tensor),
            P(("expert", "seq"), None),
            P("expert", "seq", tensor),
            P("expert", "seq", tensor),
            P("expert", "seq", tensor),
        ),
        check_vma=False,
    )
```

```python
import functools

import jax
import jax.numpy as jnp
from jax import lax
from jax.experimental import pallas as pl
from jax.experimental.pallas import tpu as pltpu
from jax.sharding import PartitionSpec as P

MESH = pl.DeviceIdType.MESH


def exchange_kernel(
    n_seq, n_tx, peers, tok_send, grad_send, tok_out, grad_out, send_sem, recv_sem, local_sem
):
    sends = (tok_send, grad_send)
    outs = (tok_out, grad_out)
    e = lax.axis_index("expert")
    s = lax.axis_index("seq")
    x = lax.axis_index("tx")
    c = lax.axis_index("core")
    me = e * n_seq + s
    other = 1 - c
    x_left = lax.rem(x + n_tx - 1, n_tx)
    x_right = lax.rem(x + 1, n_tx)
    x_far = lax.rem(x + 2, n_tx)
    own = x * 2 + c
    from_left = x_left * 2 + c
    from_right = x_right * 2 + c
    from_far = x_far * 2 + c
    left = (e, s, x_left, c)
    right = (e, s, x_right, c)
    partner = (e, s, x, other)

    def peer(k):
        q = lax.rem(me + k, peers)
        return q, (q // n_seq, q % n_seq, x, c)

    barrier = pltpu.get_barrier_semaphore()
    for k in range(1, peers):
        pl.semaphore_signal(barrier, inc=1, device_id=peer(k)[1], device_id_type=MESH)
    for where in (left, right, partner):
        pl.semaphore_signal(barrier, inc=1, device_id=where, device_id_type=MESH)
    pl.semaphore_wait(barrier, peers + 2)

    def remote(kind, src, dst, slot, recv, where):
        return pltpu.make_async_remote_copy(
            src_ref=src,
            dst_ref=dst,
            send_sem=send_sem.at[kind, slot],
            recv_sem=recv_sem.at[kind, recv],
            device_id=where,
            device_id_type=MESH,
        )

    locals_ = [
        pltpu.make_async_copy(sends[kind].at[me], outs[kind].at[own, me], local_sem.at[kind])
        for kind in range(2)
    ]
    for copy in locals_:
        copy.start()
    for k in range(1, peers):
        q, where = peer(k)
        for kind in range(2):
            remote(
                kind, sends[kind].at[q], outs[kind].at[own, me], q, own * peers + me, where
            ).start()

    def arrived(chunk, p):
        for kind in range(2):
            block = outs[kind].at[chunk, p]
            remote(kind, block, block, 0, chunk * peers + p, partner).wait_recv()

    def forward(chunk, p, slot, where):
        for kind in range(2):
            block = outs[kind].at[chunk, p]
            remote(kind, block, block, slot, chunk * peers + p, where).start()

    for copy in locals_:
        copy.wait()
    for k in range(peers):
        p = peer(k)[0]
        if k > 0:
            arrived(own, p)
        forward(own, p, peers + p, right)
        forward(own, p, 2 * peers + p, left)
        forward(own, p, 3 * peers + p, partner)

    def relay(chunk, onward, onward_parity, base):
        def body(i, carry):
            for parity in (0, 1):
                p = 2 * i + parity
                arrived(chunk, p)
                if onward is not None and parity == onward_parity:
                    forward(chunk, p, base + peers + p, onward)
                forward(chunk, p, base + p, partner)
            return carry

        lax.fori_loop(0, peers // 2, body, 0)

    relay(from_left, right, 0, 4 * peers)
    relay(from_right, left, 1, 6 * peers)
    relay(from_far, None, 0, 8 * peers)

    def partner_chunks(p, carry):
        for column in range(n_tx):
            arrived(column * 2 + other, p)
        return carry

    lax.fori_loop(0, peers, partner_chunks, 0)

    def drain(slot, carry):
        for kind in range(2):
            block = outs[kind].at[own, 0]
            remote(kind, block, block, slot, 0, partner).wait_send()
        return carry

    def drain_pairs(first, parity):
        def body(i, carry):
            return drain(first + 2 * i + parity, carry)

        lax.fori_loop(0, peers // 2, body, 0)

    for k in range(1, peers):
        drain(peer(k)[0], 0)
    lax.fori_loop(peers, 5 * peers, drain, 0)
    drain_pairs(5 * peers, 0)
    lax.fori_loop(6 * peers, 7 * peers, drain, 0)
    drain_pairs(7 * peers, 1)
    lax.fori_loop(8 * peers, 9 * peers, drain, 0)


def exchange_rows(tok_send, grad_send, n_seq, n_tx):
    peers = tok_send.shape[0]
    chunks = 2 * n_tx
    shape = jax.ShapeDtypeStruct((chunks,) + tok_send.shape, tok_send.dtype)
    return pl.pallas_call(
        functools.partial(exchange_kernel, n_seq, n_tx, peers),
        out_shape=(shape, shape),
        in_specs=[pl.BlockSpec(memory_space=pl.ANY)] * 2,
        out_specs=(pl.BlockSpec(memory_space=pl.ANY), pl.BlockSpec(memory_space=pl.ANY)),
        scratch_shapes=[
            pltpu.SemaphoreType.DMA((2, 9 * peers)),
            pltpu.SemaphoreType.DMA((2, chunks * peers)),
            pltpu.SemaphoreType.DMA((2,)),
        ],
        compiler_params=pltpu.CompilerParams(collective_id=0, has_side_effects=True),
    )(tok_send, grad_send)


def shards(tokens, grad_out, expert_ids, route_weights, gate_weight, up_weight, down_weight):
    expert_count = lax.axis_size("expert")
    seq_count = lax.axis_size("seq")
    tensor_count = lax.axis_size("tx") * lax.axis_size("core")
    core = lax.axis_index("core")
    local_count = gate_weight.shape[0]
    tok_rows = tokens.shape[0]
    model_width = tokens.shape[1]
    part_width = model_width // tensor_count
    per_peer = tok_rows // 6
    peer_count = expert_count * seq_count
    block_rows = local_count * per_peer
    slot_count = peer_count * block_rows
    flat_ids = expert_ids.reshape(-1)
    route_count = flat_ids.shape[0]
    onehot = (
        flat_ids[:, None] == jnp.arange(local_count * expert_count, dtype=jnp.int32)[None, :]
    ).astype(jnp.int32)
    before = jnp.cumsum(onehot, axis=0) - onehot
    ranking = jnp.sum(before * onehot, axis=1)
    local_expert = flat_ids % local_count
    dest_peer = flat_ids // local_count * seq_count + ranking % seq_count
    target = (dest_peer * local_count + local_expert) * per_peer + ranking // seq_count
    source = (
        jnp.full((slot_count,), -1, jnp.int32)
        .at[target]
        .set(jnp.arange(route_count, dtype=jnp.int32))
    )
    filled = source >= 0
    safe_source = jnp.maximum(source, 0)
    token_of = safe_source // 2
    weight_send = (
        route_weights.reshape(-1)[safe_source] * filled.astype(route_weights.dtype)
    ).reshape(peer_count, block_rows)
    own_part = lax.axis_index("tx") * 2 + core
    half = part_width
    tokens_half = lax.dynamic_slice_in_dim(tokens, own_part * half, half, axis=1)
    grad_half = lax.dynamic_slice_in_dim(grad_out, own_part * half, half, axis=1)
    tok_send = tokens_half[token_of].reshape(peer_count, block_rows, half)
    grad_send = grad_half[token_of].reshape(peer_count, block_rows, half)

    def join_halves(mine):
        both = jnp.broadcast_to(mine[None], (2,) + mine.shape)
        return lax.all_to_all(both, "core", split_axis=0, concat_axis=0, tiled=True)

    def by_expert(values):
        shaped = values.reshape((peer_count, local_count, per_peer) + values.shape[2:])
        return jnp.swapaxes(shaped, 0, 1).reshape(
            (local_count, peer_count * per_peer) + values.shape[2:]
        )

    def by_peer(values):
        shaped = values.reshape((local_count, peer_count, per_peer) + values.shape[2:])
        return jnp.swapaxes(shaped, 0, 1).reshape((peer_count, block_rows) + values.shape[2:])

    tok_recv, grad_recv = exchange_rows(tok_send, grad_send, seq_count, lax.axis_size("tx"))
    weight_send, tok_recv = lax.optimization_barrier((weight_send, tok_recv))
    weight_recv = lax.all_to_all(
        weight_send, ("expert", "seq"), split_axis=0, concat_axis=0, tiled=True
    )
    in_rows = jax.vmap(by_expert)(tok_recv)
    out_rows = jax.vmap(by_expert)(grad_recv)
    prob = by_expert(weight_recv).astype(jnp.float32)[:, :, None]
    gate_full, up_full, down_full = (
        lax.all_gather(w, "seq", axis=1, tiled=True) for w in (gate_weight, up_weight, down_weight)
    )
    hidden_count = gate_full.shape[2]
    gate_h, up_h, down_h = (
        w.reshape(local_count, tensor_count, half, hidden_count)
        for w in (gate_full, up_full, down_full)
    )
    pre_gate = jnp.einsum("cemd,ecdf->emf", in_rows, gate_h, preferred_element_type=jnp.float32)
    pre_up = jnp.einsum("cemd,ecdf->emf", in_rows, up_h, preferred_element_type=jnp.float32)
    sigmoid_gate = jax.nn.sigmoid(pre_gate)
    silu_gate = pre_gate * sigmoid_gate
    hidden = silu_gate * pre_up
    hidden_low = hidden.astype(jnp.bfloat16)
    back_proj = jnp.einsum("cemd,ecdf->emf", out_rows, down_h, preferred_element_type=jnp.float32)
    partial_scores = jnp.sum(hidden * back_proj, axis=2)
    scaled = (prob[None] * out_rows.astype(jnp.float32)).astype(jnp.bfloat16)
    hidden_grad = prob * back_proj
    up_grad = (hidden_grad * silu_gate).astype(jnp.bfloat16)
    gate_grad = (
        hidden_grad * pre_up * sigmoid_gate * (1.0 + pre_gate * (1.0 - sigmoid_gate))
    ).astype(jnp.bfloat16)
    gate_part = jnp.einsum("cemd,emf->ecdf", in_rows, gate_grad, preferred_element_type=jnp.float32)
    up_part = jnp.einsum("cemd,emf->ecdf", in_rows, up_grad, preferred_element_type=jnp.float32)
    down_part = jnp.einsum("cemd,emf->ecdf", scaled, hidden_low, preferred_element_type=jnp.float32)
    parts = jnp.stack([gate_part, up_part, down_part]).reshape(
        3, local_count, model_width, hidden_count
    ).astype(jnp.bfloat16)
    parts, gate_grad, up_grad = lax.optimization_barrier((parts, gate_grad, up_grad))
    reduced_parts = lax.psum_scatter(parts, "seq", scatter_dimension=2, tiled=True).astype(jnp.float32)
    grad_gate, grad_up, grad_down = reduced_parts[0], reduced_parts[1], reduced_parts[2]
    input_terms = jnp.einsum(
        "emf,ecdf->ecdm", gate_grad, gate_h, preferred_element_type=jnp.float32
    )
    input_terms = input_terms + jnp.einsum(
        "emf,ecdf->ecdm", up_grad, up_h, preferred_element_type=jnp.float32
    )
    rows_here = local_count * slot_count
    input_terms = jnp.swapaxes(
        input_terms.reshape(local_count, tensor_count, part_width, slot_count), 0, 1
    ).reshape(tensor_count, part_width, rows_here)
    score_pad = 16
    score_rows = jnp.zeros((tensor_count, score_pad, rows_here), jnp.float32)
    score_rows = score_rows.at[:, 0, :].set(partial_scores.reshape(1, rows_here))
    stacked = jnp.concatenate([input_terms, score_rows], axis=1).astype(jnp.bfloat16)
    tx_count = lax.axis_size("tx")
    stacked = stacked.reshape(tx_count, 2, part_width + score_pad, rows_here)
    pair = lax.all_to_all(stacked, "core", split_axis=1, concat_axis=1, tiled=True)
    pair = jnp.sum(pair.astype(jnp.float32), axis=1).astype(jnp.bfloat16)
    ring = lax.all_to_all(pair, "tx", split_axis=0, concat_axis=0, tiled=True)
    reduced = jnp.sum(ring.astype(jnp.float32), axis=0).astype(jnp.bfloat16)
    back_send = by_peer(
        jnp.swapaxes(reduced, 0, 1).reshape(local_count, slot_count, part_width + score_pad)
    )
    back_all = lax.all_to_all(
        back_send, ("expert", "seq"), split_axis=0, concat_axis=0, tiled=True
    ).astype(jnp.float32)
    back_all = back_all.reshape(slot_count, part_width + score_pad)[target]
    route_rows = back_all[:, :part_width].reshape(tok_rows, 2, part_width)
    grad_tokens = jnp.sum(route_rows, axis=1).astype(jnp.bfloat16)
    grad_route = back_all[:, part_width].reshape(tok_rows, 2)
    return (grad_tokens, grad_route, grad_gate, grad_up, grad_down)


def solution(mesh):
    shape = mesh.devices.shape
    mesh = jax.sharding.Mesh(
        mesh.devices.reshape(shape[0], shape[1], shape[2] // 2, 2), ("expert", "seq", "tx", "core")
    )
    tensor = ("tx", "core")
    placed = (
        P(("expert", "seq"), None),
        P(("expert", "seq"), None),
        P(("expert", "seq"), None),
        P(("expert", "seq"), None),
        P("expert", "seq", tensor),
        P("expert", "seq", tensor),
        P("expert", "seq", tensor),
    )
    return jax.shard_map(
        shards,
        mesh=mesh,
        in_specs=placed,
        out_specs=(
            P(("expert", "seq"), tensor),
            P(("expert", "seq"), None),
            P("expert", "seq", tensor),
            P("expert", "seq", tensor),
            P("expert", "seq", tensor),
        ),
        check_vma=False,
    )
```

```python
import functools

import jax
import jax.numpy as jnp
from jax import lax
from jax.experimental import pallas as pl
from jax.experimental.pallas import tpu as pltpu
from jax.sharding import PartitionSpec as P

MESH = pl.DeviceIdType.MESH


def exchange_kernel(
    n_seq, n_tx, peers, tok_send, grad_send, tok_out, grad_out, send_sem, recv_sem, local_sem
):
    sends = (tok_send, grad_send)
    outs = (tok_out, grad_out)
    e = lax.axis_index("expert")
    s = lax.axis_index("seq")
    x = lax.axis_index("tx")
    c = lax.axis_index("core")
    me = e * n_seq + s
    other = 1 - c
    x_left = lax.rem(x + n_tx - 1, n_tx)
    x_right = lax.rem(x + 1, n_tx)
    x_far = lax.rem(x + 2, n_tx)
    own = x * 2 + c
    from_left = x_left * 2 + c
    from_right = x_right * 2 + c
    from_far = x_far * 2 + c
    left = (e, s, x_left, c)
    right = (e, s, x_right, c)
    partner = (e, s, x, other)

    def peer(k):
        q = lax.rem(me + k, peers)
        return q, (q // n_seq, q % n_seq, x, c)

    barrier = pltpu.get_barrier_semaphore()
    for k in range(1, peers):
        pl.semaphore_signal(barrier, inc=1, device_id=peer(k)[1], device_id_type=MESH)
    for where in (left, right, partner):
        pl.semaphore_signal(barrier, inc=1, device_id=where, device_id_type=MESH)
    pl.semaphore_wait(barrier, peers + 2)

    def remote(kind, src, dst, slot, recv, where):
        return pltpu.make_async_remote_copy(
            src_ref=src,
            dst_ref=dst,
            send_sem=send_sem.at[kind, slot],
            recv_sem=recv_sem.at[kind, recv],
            device_id=where,
            device_id_type=MESH,
        )

    locals_ = [
        pltpu.make_async_copy(sends[kind].at[me], outs[kind].at[own, me], local_sem.at[kind])
        for kind in range(2)
    ]
    for copy in locals_:
        copy.start()
    for k in range(1, peers):
        q, where = peer(k)
        for kind in range(2):
            remote(
                kind, sends[kind].at[q], outs[kind].at[own, me], q, own * peers + me, where
            ).start()

    def arrived(chunk, p):
        for kind in range(2):
            block = outs[kind].at[chunk, p]
            remote(kind, block, block, 0, chunk * peers + p, partner).wait_recv()

    def forward(chunk, p, slot, where):
        for kind in range(2):
            block = outs[kind].at[chunk, p]
            remote(kind, block, block, slot, chunk * peers + p, where).start()

    for copy in locals_:
        copy.wait()
    for k in range(peers):
        p = peer(k)[0]
        if k > 0:
            arrived(own, p)
        forward(own, p, peers + p, right)
        forward(own, p, 2 * peers + p, left)
        forward(own, p, 3 * peers + p, partner)

    def relay(chunk, onward, onward_parity, base):
        def body(i, carry):
            for parity in (0, 1):
                p = 2 * i + parity
                arrived(chunk, p)
                if onward is not None and parity == onward_parity:
                    forward(chunk, p, base + peers + p, onward)
                forward(chunk, p, base + p, partner)
            return carry

        lax.fori_loop(0, peers // 2, body, 0)

    relay(from_left, right, 0, 4 * peers)
    relay(from_right, left, 1, 6 * peers)
    relay(from_far, None, 0, 8 * peers)

    def partner_chunks(p, carry):
        for column in range(n_tx):
            arrived(column * 2 + other, p)
        return carry

    lax.fori_loop(0, peers, partner_chunks, 0)

    def drain(slot, carry):
        for kind in range(2):
            block = outs[kind].at[own, 0]
            remote(kind, block, block, slot, 0, partner).wait_send()
        return carry

    def drain_pairs(first, parity):
        def body(i, carry):
            return drain(first + 2 * i + parity, carry)

        lax.fori_loop(0, peers // 2, body, 0)

    for k in range(1, peers):
        drain(peer(k)[0], 0)
    lax.fori_loop(peers, 5 * peers, drain, 0)
    drain_pairs(5 * peers, 0)
    lax.fori_loop(6 * peers, 7 * peers, drain, 0)
    drain_pairs(7 * peers, 1)
    lax.fori_loop(8 * peers, 9 * peers, drain, 0)


def exchange_rows(tok_send, grad_send, n_seq, n_tx):
    peers = tok_send.shape[0]
    chunks = 2 * n_tx
    shape = jax.ShapeDtypeStruct((chunks,) + tok_send.shape, tok_send.dtype)
    return pl.pallas_call(
        functools.partial(exchange_kernel, n_seq, n_tx, peers),
        out_shape=(shape, shape),
        in_specs=[pl.BlockSpec(memory_space=pl.ANY)] * 2,
        out_specs=(pl.BlockSpec(memory_space=pl.ANY), pl.BlockSpec(memory_space=pl.ANY)),
        scratch_shapes=[
            pltpu.SemaphoreType.DMA((2, 9 * peers)),
            pltpu.SemaphoreType.DMA((2, chunks * peers)),
            pltpu.SemaphoreType.DMA((2,)),
        ],
        compiler_params=pltpu.CompilerParams(collective_id=0, has_side_effects=True),
    )(tok_send, grad_send)


def shards(tokens, grad_out, expert_ids, route_weights, gate_weight, up_weight, down_weight):
    expert_count = lax.axis_size("expert")
    seq_count = lax.axis_size("seq")
    tensor_count = lax.axis_size("tx") * lax.axis_size("core")
    core = lax.axis_index("core")
    local_count = gate_weight.shape[0]
    tok_rows = tokens.shape[0]
    model_width = tokens.shape[1]
    part_width = model_width // tensor_count
    per_peer = tok_rows // 6
    peer_count = expert_count * seq_count
    block_rows = local_count * per_peer
    slot_count = peer_count * block_rows
    flat_ids = expert_ids.reshape(-1)
    route_count = flat_ids.shape[0]
    onehot = (
        flat_ids[:, None] == jnp.arange(local_count * expert_count, dtype=jnp.int32)[None, :]
    ).astype(jnp.int32)
    before = jnp.cumsum(onehot, axis=0) - onehot
    ranking = jnp.sum(before * onehot, axis=1)
    local_expert = flat_ids % local_count
    dest_peer = flat_ids // local_count * seq_count + ranking % seq_count
    target = (dest_peer * local_count + local_expert) * per_peer + ranking // seq_count
    source = (
        jnp.full((slot_count,), -1, jnp.int32)
        .at[target]
        .set(jnp.arange(route_count, dtype=jnp.int32))
    )
    filled = source >= 0
    safe_source = jnp.maximum(source, 0)
    token_of = safe_source // 2
    weight_send = (
        route_weights.reshape(-1)[safe_source] * filled.astype(route_weights.dtype)
    ).reshape(peer_count, block_rows)
    own_part = lax.axis_index("tx") * 2 + core
    half = part_width
    tokens_half = lax.dynamic_slice_in_dim(tokens, own_part * half, half, axis=1)
    grad_half = lax.dynamic_slice_in_dim(grad_out, own_part * half, half, axis=1)
    tok_send = tokens_half[token_of].reshape(peer_count, block_rows, half)
    grad_send = grad_half[token_of].reshape(peer_count, block_rows, half)

    def join_halves(mine):
        both = jnp.broadcast_to(mine[None], (2,) + mine.shape)
        return lax.all_to_all(both, "core", split_axis=0, concat_axis=0, tiled=True)

    def by_expert(values):
        shaped = values.reshape((peer_count, local_count, per_peer) + values.shape[2:])
        return jnp.swapaxes(shaped, 0, 1).reshape(
            (local_count, peer_count * per_peer) + values.shape[2:]
        )

    def by_peer(values):
        shaped = values.reshape((local_count, peer_count, per_peer) + values.shape[2:])
        return jnp.swapaxes(shaped, 0, 1).reshape((peer_count, block_rows) + values.shape[2:])

    tok_recv, grad_recv = exchange_rows(tok_send, grad_send, seq_count, lax.axis_size("tx"))
    weight_send, tok_recv = lax.optimization_barrier((weight_send, tok_recv))
    weight_recv = lax.all_to_all(
        weight_send, ("expert", "seq"), split_axis=0, concat_axis=0, tiled=True
    )
    in_rows = jax.vmap(by_expert)(tok_recv)
    out_rows = jax.vmap(by_expert)(grad_recv)
    prob = by_expert(weight_recv).astype(jnp.float32)[:, :, None]
    weights = lax.all_gather(
        jnp.stack([gate_weight, up_weight, down_weight], axis=2), "seq", axis=1, tiled=True
    )
    hidden_count = weights.shape[3]
    gate_up_h = weights[:, :, 0:2, :].reshape(local_count, tensor_count, half, 2 * hidden_count)
    down_h = weights[:, :, 2, :].reshape(local_count, tensor_count, half, hidden_count)
    pre = jnp.einsum("cemd,ecdg->emg", in_rows, gate_up_h, preferred_element_type=jnp.float32)
    pre_gate = pre[:, :, :hidden_count]
    pre_up = pre[:, :, hidden_count:]
    sigmoid_gate = jax.nn.sigmoid(pre_gate)
    silu_gate = pre_gate * sigmoid_gate
    hidden = silu_gate * pre_up
    hidden_low = hidden.astype(jnp.bfloat16)
    back_proj = jnp.einsum("cemd,ecdf->emf", out_rows, down_h, preferred_element_type=jnp.float32)
    partial_scores = jnp.sum(hidden * back_proj, axis=2)
    scaled = (prob[None] * out_rows.astype(jnp.float32)).astype(jnp.bfloat16)
    hidden_grad = prob * back_proj
    up_grad = (hidden_grad * silu_gate).astype(jnp.bfloat16)
    gate_grad = (
        hidden_grad * pre_up * sigmoid_gate * (1.0 + pre_gate * (1.0 - sigmoid_gate))
    ).astype(jnp.bfloat16)
    gate_up_grad = jnp.concatenate([gate_grad, up_grad], axis=2)
    gate_up_part = jnp.einsum(
        "cemd,emg->ecdg", in_rows, gate_up_grad, preferred_element_type=jnp.float32
    )
    down_part = jnp.einsum("cemd,emf->ecdf", scaled, hidden_low, preferred_element_type=jnp.float32)
    parts = jnp.concatenate(
        [
            gate_up_part.reshape(local_count, model_width, 2, hidden_count),
            down_part.reshape(local_count, model_width, 1, hidden_count),
        ],
        axis=2,
    ).astype(jnp.bfloat16)
    parts, gate_up_grad = lax.optimization_barrier((parts, gate_up_grad))
    reduced_parts = lax.psum_scatter(parts, "seq", scatter_dimension=1, tiled=True).astype(jnp.float32)
    grad_gate, grad_up, grad_down = (reduced_parts[:, :, w, :] for w in range(3))
    input_terms = jnp.einsum(
        "emg,ecdg->ecdm", gate_up_grad, gate_up_h, preferred_element_type=jnp.float32
    )
    rows_here = local_count * slot_count
    input_terms = jnp.swapaxes(
        input_terms.reshape(local_count, tensor_count, part_width, slot_count), 0, 1
    ).reshape(tensor_count, part_width, rows_here)
    score_pad = 16
    score_rows = jnp.zeros((tensor_count, score_pad, rows_here), jnp.float32)
    score_rows = score_rows.at[:, 0, :].set(partial_scores.reshape(1, rows_here))
    stacked = jnp.concatenate([input_terms, score_rows], axis=1).astype(jnp.bfloat16)
    tx_count = lax.axis_size("tx")
    stacked = stacked.reshape(tx_count, 2, part_width + score_pad, rows_here)
    pair = lax.all_to_all(stacked, "core", split_axis=1, concat_axis=1, tiled=True)
    pair = jnp.sum(pair.astype(jnp.float32), axis=1).astype(jnp.bfloat16)
    ring = lax.all_to_all(pair, "tx", split_axis=0, concat_axis=0, tiled=True)
    reduced = jnp.sum(ring.astype(jnp.float32), axis=0).astype(jnp.bfloat16)
    back_send = by_peer(
        jnp.swapaxes(reduced, 0, 1).reshape(local_count, slot_count, part_width + score_pad)
    )
    back_all = lax.all_to_all(
        back_send, ("expert", "seq"), split_axis=0, concat_axis=0, tiled=True
    ).astype(jnp.float32)
    back_all = back_all.reshape(slot_count, part_width + score_pad)[target]
    route_rows = back_all[:, :part_width].reshape(tok_rows, 2, part_width)
    grad_tokens = jnp.sum(route_rows, axis=1).astype(jnp.bfloat16)
    grad_route = back_all[:, part_width].reshape(tok_rows, 2)
    return (grad_tokens, grad_route, grad_gate, grad_up, grad_down)


def solution(mesh):
    shape = mesh.devices.shape
    mesh = jax.sharding.Mesh(
        mesh.devices.reshape(shape[0], shape[1], shape[2] // 2, 2), ("expert", "seq", "tx", "core")
    )
    tensor = ("tx", "core")
    placed = (
        P(("expert", "seq"), None),
        P(("expert", "seq"), None),
        P(("expert", "seq"), None),
        P(("expert", "seq"), None),
        P("expert", "seq", tensor),
        P("expert", "seq", tensor),
        P("expert", "seq", tensor),
    )
    return jax.shard_map(
        shards,
        mesh=mesh,
        in_specs=placed,
        out_specs=(
            P(("expert", "seq"), tensor),
            P(("expert", "seq"), None),
            P("expert", "seq", tensor),
            P("expert", "seq", tensor),
            P("expert", "seq", tensor),
        ),
        check_vma=False,
    )
```

```python
import functools

import jax
import jax.numpy as jnp
from jax import lax
from jax.experimental import pallas as pl
from jax.experimental.pallas import tpu as pltpu
from jax.sharding import PartitionSpec as P

MESH = pl.DeviceIdType.MESH


def exchange_kernel(
    n_seq, n_tx, peers, tok_send, grad_send, tok_out, grad_out, send_sem, recv_sem, local_sem
):
    sends = (tok_send, grad_send)
    outs = (tok_out, grad_out)
    e = lax.axis_index("expert")
    s = lax.axis_index("seq")
    x = lax.axis_index("tx")
    c = lax.axis_index("core")
    me = e * n_seq + s
    other = 1 - c
    x_left = lax.rem(x + n_tx - 1, n_tx)
    x_right = lax.rem(x + 1, n_tx)
    x_far = lax.rem(x + 2, n_tx)
    own = x * 2 + c
    from_left = x_left * 2 + c
    from_right = x_right * 2 + c
    from_far = x_far * 2 + c
    left = (e, s, x_left, c)
    right = (e, s, x_right, c)
    partner = (e, s, x, other)

    def peer(k):
        q = lax.rem(me + k, peers)
        return q, (q // n_seq, q % n_seq, x, c)

    barrier = pltpu.get_barrier_semaphore()
    for k in range(1, peers):
        pl.semaphore_signal(barrier, inc=1, device_id=peer(k)[1], device_id_type=MESH)
    for where in (left, right, partner):
        pl.semaphore_signal(barrier, inc=1, device_id=where, device_id_type=MESH)
    pl.semaphore_wait(barrier, peers + 2)

    def remote(kind, src, dst, slot, recv, where):
        return pltpu.make_async_remote_copy(
            src_ref=src,
            dst_ref=dst,
            send_sem=send_sem.at[kind, slot],
            recv_sem=recv_sem.at[kind, recv],
            device_id=where,
            device_id_type=MESH,
        )

    locals_ = [
        pltpu.make_async_copy(sends[kind].at[me], outs[kind].at[own, me], local_sem.at[kind])
        for kind in range(2)
    ]
    for copy in locals_:
        copy.start()
    for k in range(1, peers):
        q, where = peer(k)
        for kind in range(2):
            remote(
                kind, sends[kind].at[q], outs[kind].at[own, me], q, own * peers + me, where
            ).start()

    def arrived(chunk, p):
        for kind in range(2):
            block = outs[kind].at[chunk, p]
            remote(kind, block, block, 0, chunk * peers + p, partner).wait_recv()

    def forward(chunk, p, slot, where):
        for kind in range(2):
            block = outs[kind].at[chunk, p]
            remote(kind, block, block, slot, chunk * peers + p, where).start()

    for copy in locals_:
        copy.wait()
    for k in range(peers):
        p = peer(k)[0]
        if k > 0:
            arrived(own, p)
        forward(own, p, peers + p, right)
        forward(own, p, 2 * peers + p, left)
        forward(own, p, 3 * peers + p, partner)

    def relay(chunk, onward, onward_parity, base):
        def body(i, carry):
            for parity in (0, 1):
                p = 2 * i + parity
                arrived(chunk, p)
                if onward is not None and parity == onward_parity:
                    forward(chunk, p, base + peers + p, onward)
                forward(chunk, p, base + p, partner)
            return carry

        lax.fori_loop(0, peers // 2, body, 0)

    relay(from_left, right, 0, 4 * peers)
    relay(from_right, left, 1, 6 * peers)
    relay(from_far, None, 0, 8 * peers)

    def partner_chunks(p, carry):
        for column in range(n_tx):
            arrived(column * 2 + other, p)
        return carry

    lax.fori_loop(0, peers, partner_chunks, 0)

    def drain(slot, carry):
        for kind in range(2):
            block = outs[kind].at[own, 0]
            remote(kind, block, block, slot, 0, partner).wait_send()
        return carry

    def drain_pairs(first, parity):
        def body(i, carry):
            return drain(first + 2 * i + parity, carry)

        lax.fori_loop(0, peers // 2, body, 0)

    for k in range(1, peers):
        drain(peer(k)[0], 0)
    lax.fori_loop(peers, 5 * peers, drain, 0)
    drain_pairs(5 * peers, 0)
    lax.fori_loop(6 * peers, 7 * peers, drain, 0)
    drain_pairs(7 * peers, 1)
    lax.fori_loop(8 * peers, 9 * peers, drain, 0)


def exchange_rows(tok_send, grad_send, n_seq, n_tx):
    peers = tok_send.shape[0]
    chunks = 2 * n_tx
    shape = jax.ShapeDtypeStruct((chunks,) + tok_send.shape, tok_send.dtype)
    return pl.pallas_call(
        functools.partial(exchange_kernel, n_seq, n_tx, peers),
        out_shape=(shape, shape),
        in_specs=[pl.BlockSpec(memory_space=pl.ANY)] * 2,
        out_specs=(pl.BlockSpec(memory_space=pl.ANY), pl.BlockSpec(memory_space=pl.ANY)),
        scratch_shapes=[
            pltpu.SemaphoreType.DMA((2, 9 * peers)),
            pltpu.SemaphoreType.DMA((2, chunks * peers)),
            pltpu.SemaphoreType.DMA((2,)),
        ],
        compiler_params=pltpu.CompilerParams(collective_id=0, has_side_effects=True),
    )(tok_send, grad_send)


def shards(tokens, grad_out, expert_ids, route_weights, gate_weight, up_weight, down_weight):
    expert_count = lax.axis_size("expert")
    seq_count = lax.axis_size("seq")
    tensor_count = lax.axis_size("tx") * lax.axis_size("core")
    core = lax.axis_index("core")
    local_count = gate_weight.shape[0]
    tok_rows = tokens.shape[0]
    model_width = tokens.shape[1]
    part_width = model_width // tensor_count
    per_peer = tok_rows // 6
    peer_count = expert_count * seq_count
    block_rows = local_count * per_peer
    slot_count = peer_count * block_rows
    flat_ids = expert_ids.reshape(-1)
    route_count = flat_ids.shape[0]
    onehot = (
        flat_ids[:, None] == jnp.arange(local_count * expert_count, dtype=jnp.int32)[None, :]
    ).astype(jnp.int32)
    before = jnp.cumsum(onehot, axis=0) - onehot
    ranking = jnp.sum(before * onehot, axis=1)
    local_expert = flat_ids % local_count
    dest_peer = flat_ids // local_count * seq_count + ranking % seq_count
    target = (dest_peer * local_count + local_expert) * per_peer + ranking // seq_count
    source = (
        jnp.full((slot_count,), -1, jnp.int32)
        .at[target]
        .set(jnp.arange(route_count, dtype=jnp.int32))
    )
    filled = source >= 0
    safe_source = jnp.maximum(source, 0)
    token_of = safe_source // 2
    weight_send = (
        route_weights.reshape(-1)[safe_source] * filled.astype(route_weights.dtype)
    ).reshape(peer_count, block_rows)
    own_part = lax.axis_index("tx") * 2 + core
    half = part_width
    tokens_half = lax.dynamic_slice_in_dim(tokens, own_part * half, half, axis=1)
    grad_half = lax.dynamic_slice_in_dim(grad_out, own_part * half, half, axis=1)
    tok_send = tokens_half[token_of].reshape(peer_count, block_rows, half)
    grad_send = grad_half[token_of].reshape(peer_count, block_rows, half)

    def join_halves(mine):
        both = jnp.broadcast_to(mine[None], (2,) + mine.shape)
        return lax.all_to_all(both, "core", split_axis=0, concat_axis=0, tiled=True)

    def by_expert(values):
        shaped = values.reshape((peer_count, local_count, per_peer) + values.shape[2:])
        return jnp.swapaxes(shaped, 0, 1).reshape(
            (local_count, peer_count * per_peer) + values.shape[2:]
        )

    def by_peer(values):
        shaped = values.reshape((local_count, peer_count, per_peer) + values.shape[2:])
        return jnp.swapaxes(shaped, 0, 1).reshape((peer_count, block_rows) + values.shape[2:])

    tok_recv, grad_recv = exchange_rows(tok_send, grad_send, seq_count, lax.axis_size("tx"))
    weight_send, tok_recv = lax.optimization_barrier((weight_send, tok_recv))
    weight_recv = lax.all_to_all(
        weight_send, ("expert", "seq"), split_axis=0, concat_axis=0, tiled=True
    )
    in_rows = jax.vmap(by_expert)(tok_recv)
    out_rows = jax.vmap(by_expert)(grad_recv)
    prob = by_expert(weight_recv).astype(jnp.float32)[:, :, None]
    weights = lax.all_gather(
        jnp.stack([gate_weight, up_weight, down_weight]), "seq", axis=2, tiled=True
    )
    gate_full, up_full, down_full = weights[0], weights[1], weights[2]
    hidden_count = gate_full.shape[2]
    gate_h, up_h, down_h = (
        w.reshape(local_count, tensor_count, half, hidden_count)
        for w in (gate_full, up_full, down_full)
    )
    pre_gate = jnp.einsum("cemd,ecdf->emf", in_rows, gate_h, preferred_element_type=jnp.float32)
    pre_up = jnp.einsum("cemd,ecdf->emf", in_rows, up_h, preferred_element_type=jnp.float32)
    sigmoid_gate = jax.nn.sigmoid(pre_gate)
    silu_gate = pre_gate * sigmoid_gate
    hidden = silu_gate * pre_up
    hidden_low = hidden.astype(jnp.bfloat16)
    back_proj = jnp.einsum("cemd,ecdf->emf", out_rows, down_h, preferred_element_type=jnp.float32)
    partial_scores = jnp.sum(hidden * back_proj, axis=2)
    scaled = (prob[None] * out_rows.astype(jnp.float32)).astype(jnp.bfloat16)
    hidden_grad = prob * back_proj
    up_grad = (hidden_grad * silu_gate).astype(jnp.bfloat16)
    gate_grad = (
        hidden_grad * pre_up * sigmoid_gate * (1.0 + pre_gate * (1.0 - sigmoid_gate))
    ).astype(jnp.bfloat16)
    gate_part = jnp.einsum("cemd,emf->ecdf", in_rows, gate_grad, preferred_element_type=jnp.float32)
    up_part = jnp.einsum("cemd,emf->ecdf", in_rows, up_grad, preferred_element_type=jnp.float32)
    down_part = jnp.einsum("cemd,emf->ecdf", scaled, hidden_low, preferred_element_type=jnp.float32)
    parts = jnp.stack([gate_part, up_part, down_part]).reshape(
        3, local_count, model_width, hidden_count
    ).astype(jnp.bfloat16)
    parts, gate_grad, up_grad = lax.optimization_barrier((parts, gate_grad, up_grad))
    reduced_parts = lax.psum_scatter(parts, "seq", scatter_dimension=2, tiled=True).astype(jnp.float32)
    grad_gate, grad_up, grad_down = reduced_parts[0], reduced_parts[1], reduced_parts[2]
    score_pad = 16
    gate_p, up_p = (
        jnp.pad(w, ((0, 0), (0, 0), (0, score_pad), (0, 0))) for w in (gate_h, up_h)
    )
    input_terms = jnp.einsum(
        "emf,ecdf->ecdm", gate_grad, gate_p, preferred_element_type=jnp.float32
    )
    input_terms = input_terms + jnp.einsum(
        "emf,ecdf->ecdm", up_grad, up_p, preferred_element_type=jnp.float32
    )
    input_terms = input_terms.at[:, :, part_width, :].set(partial_scores[:, None, :])
    rows_here = local_count * slot_count
    stacked = jnp.swapaxes(
        input_terms.reshape(local_count, tensor_count, part_width + score_pad, slot_count), 0, 1
    ).reshape(tensor_count, part_width + score_pad, rows_here).astype(jnp.bfloat16)
    tx_count = lax.axis_size("tx")
    stacked = stacked.reshape(tx_count, 2, part_width + score_pad, rows_here)
    pair = lax.all_to_all(stacked, "core", split_axis=1, concat_axis=1, tiled=True)
    pair = jnp.sum(pair.astype(jnp.float32), axis=1).astype(jnp.bfloat16)
    ring = lax.all_to_all(pair, "tx", split_axis=0, concat_axis=0, tiled=True)
    reduced = jnp.sum(ring.astype(jnp.float32), axis=0).astype(jnp.bfloat16)
    back_send = by_peer(
        jnp.swapaxes(reduced, 0, 1).reshape(local_count, slot_count, part_width + score_pad)
    )
    back_all = lax.all_to_all(
        back_send, ("expert", "seq"), split_axis=0, concat_axis=0, tiled=True
    ).astype(jnp.float32)
    back_all = back_all.reshape(slot_count, part_width + score_pad)[target]
    route_rows = back_all[:, :part_width].reshape(tok_rows, 2, part_width)
    grad_tokens = jnp.sum(route_rows, axis=1).astype(jnp.bfloat16)
    grad_route = back_all[:, part_width].reshape(tok_rows, 2)
    return (grad_tokens, grad_route, grad_gate, grad_up, grad_down)


def solution(mesh):
    shape = mesh.devices.shape
    mesh = jax.sharding.Mesh(
        mesh.devices.reshape(shape[0], shape[1], shape[2] // 2, 2), ("expert", "seq", "tx", "core")
    )
    tensor = ("tx", "core")
    placed = (
        P(("expert", "seq"), None),
        P(("expert", "seq"), None),
        P(("expert", "seq"), None),
        P(("expert", "seq"), None),
        P("expert", "seq", tensor),
        P("expert", "seq", tensor),
        P("expert", "seq", tensor),
    )
    return jax.shard_map(
        shards,
        mesh=mesh,
        in_specs=placed,
        out_specs=(
            P(("expert", "seq"), tensor),
            P(("expert", "seq"), None),
            P("expert", "seq", tensor),
            P("expert", "seq", tensor),
            P("expert", "seq", tensor),
        ),
        check_vma=False,
    )
```

```python
import functools

import jax
import jax.numpy as jnp
from jax import lax
from jax.experimental import pallas as pl
from jax.experimental.pallas import tpu as pltpu
from jax.sharding import PartitionSpec as P

MESH = pl.DeviceIdType.MESH


def exchange_kernel(
    n_seq, n_tx, peers, tok_send, grad_send, tok_out, grad_out, send_sem, recv_sem, local_sem
):
    sends = (tok_send, grad_send)
    outs = (tok_out, grad_out)
    e = lax.axis_index("expert")
    s = lax.axis_index("seq")
    x = lax.axis_index("tx")
    c = lax.axis_index("core")
    me = e * n_seq + s
    other = 1 - c
    x_left = lax.rem(x + n_tx - 1, n_tx)
    x_right = lax.rem(x + 1, n_tx)
    x_far = lax.rem(x + 2, n_tx)
    own = x * 2 + c
    from_left = x_left * 2 + c
    from_right = x_right * 2 + c
    from_far = x_far * 2 + c
    left = (e, s, x_left, c)
    right = (e, s, x_right, c)
    partner = (e, s, x, other)

    def peer(k):
        q = lax.rem(me + k, peers)
        return q, (q // n_seq, q % n_seq, x, c)

    barrier = pltpu.get_barrier_semaphore()
    for k in range(1, peers):
        pl.semaphore_signal(barrier, inc=1, device_id=peer(k)[1], device_id_type=MESH)
    for where in (left, right, partner):
        pl.semaphore_signal(barrier, inc=1, device_id=where, device_id_type=MESH)
    pl.semaphore_wait(barrier, peers + 2)

    def remote(kind, src, dst, slot, recv, where):
        return pltpu.make_async_remote_copy(
            src_ref=src,
            dst_ref=dst,
            send_sem=send_sem.at[kind, slot],
            recv_sem=recv_sem.at[kind, recv],
            device_id=where,
            device_id_type=MESH,
        )

    locals_ = [
        pltpu.make_async_copy(sends[kind].at[me], outs[kind].at[own, me], local_sem.at[kind])
        for kind in range(2)
    ]
    for copy in locals_:
        copy.start()
    for k in range(1, peers):
        q, where = peer(k)
        for kind in range(2):
            remote(
                kind, sends[kind].at[q], outs[kind].at[own, me], q, own * peers + me, where
            ).start()

    def arrived(chunk, p):
        for kind in range(2):
            block = outs[kind].at[chunk, p]
            remote(kind, block, block, 0, chunk * peers + p, partner).wait_recv()

    def forward(chunk, p, slot, where):
        for kind in range(2):
            block = outs[kind].at[chunk, p]
            remote(kind, block, block, slot, chunk * peers + p, where).start()

    for copy in locals_:
        copy.wait()
    for k in range(peers):
        p = peer(k)[0]
        if k > 0:
            arrived(own, p)
        forward(own, p, peers + p, right)
        forward(own, p, 2 * peers + p, left)
        forward(own, p, 3 * peers + p, partner)

    def relay(chunk, onward, onward_parity, base):
        def body(i, carry):
            for parity in (0, 1):
                p = 2 * i + parity
                arrived(chunk, p)
                if onward is not None and parity == onward_parity:
                    forward(chunk, p, base + peers + p, onward)
                forward(chunk, p, base + p, partner)
            return carry

        lax.fori_loop(0, peers // 2, body, 0)

    relay(from_left, right, 0, 4 * peers)
    relay(from_right, left, 1, 6 * peers)
    relay(from_far, None, 0, 8 * peers)

    def partner_chunks(p, carry):
        for column in range(n_tx):
            arrived(column * 2 + other, p)
        return carry

    lax.fori_loop(0, peers, partner_chunks, 0)

    def drain(slot, carry):
        for kind in range(2):
            block = outs[kind].at[own, 0]
            remote(kind, block, block, slot, 0, partner).wait_send()
        return carry

    def drain_pairs(first, parity):
        def body(i, carry):
            return drain(first + 2 * i + parity, carry)

        lax.fori_loop(0, peers // 2, body, 0)

    for k in range(1, peers):
        drain(peer(k)[0], 0)
    lax.fori_loop(peers, 5 * peers, drain, 0)
    drain_pairs(5 * peers, 0)
    lax.fori_loop(6 * peers, 7 * peers, drain, 0)
    drain_pairs(7 * peers, 1)
    lax.fori_loop(8 * peers, 9 * peers, drain, 0)


def exchange_rows(tok_send, grad_send, n_seq, n_tx):
    peers = tok_send.shape[0]
    chunks = 2 * n_tx
    shape = jax.ShapeDtypeStruct((chunks,) + tok_send.shape, tok_send.dtype)
    return pl.pallas_call(
        functools.partial(exchange_kernel, n_seq, n_tx, peers),
        out_shape=(shape, shape),
        in_specs=[pl.BlockSpec(memory_space=pl.ANY)] * 2,
        out_specs=(pl.BlockSpec(memory_space=pl.ANY), pl.BlockSpec(memory_space=pl.ANY)),
        scratch_shapes=[
            pltpu.SemaphoreType.DMA((2, 9 * peers)),
            pltpu.SemaphoreType.DMA((2, chunks * peers)),
            pltpu.SemaphoreType.DMA((2,)),
        ],
        compiler_params=pltpu.CompilerParams(collective_id=0, has_side_effects=True),
    )(tok_send, grad_send)


def shards(tokens, grad_out, expert_ids, route_weights, gate_weight, up_weight, down_weight):
    expert_count = lax.axis_size("expert")
    seq_count = lax.axis_size("seq")
    tensor_count = lax.axis_size("tx") * lax.axis_size("core")
    core = lax.axis_index("core")
    local_count = gate_weight.shape[0]
    tok_rows = tokens.shape[0]
    model_width = tokens.shape[1]
    part_width = model_width // tensor_count
    per_peer = tok_rows // 6
    peer_count = expert_count * seq_count
    block_rows = local_count * per_peer
    slot_count = peer_count * block_rows
    flat_ids = expert_ids.reshape(-1)
    route_count = flat_ids.shape[0]
    onehot = (
        flat_ids[:, None] == jnp.arange(local_count * expert_count, dtype=jnp.int32)[None, :]
    ).astype(jnp.int32)
    before = jnp.cumsum(onehot, axis=0) - onehot
    ranking = jnp.sum(before * onehot, axis=1)
    local_expert = flat_ids % local_count
    dest_peer = flat_ids // local_count * seq_count + ranking % seq_count
    target = (dest_peer * local_count + local_expert) * per_peer + ranking // seq_count
    source = (
        jnp.full((slot_count,), -1, jnp.int32)
        .at[target]
        .set(jnp.arange(route_count, dtype=jnp.int32))
    )
    filled = source >= 0
    safe_source = jnp.maximum(source, 0)
    token_of = safe_source // 2
    weight_send = (
        route_weights.reshape(-1)[safe_source] * filled.astype(route_weights.dtype)
    ).reshape(peer_count, block_rows)
    own_part = lax.axis_index("tx") * 2 + core
    half = part_width
    tokens_half = lax.dynamic_slice_in_dim(tokens, own_part * half, half, axis=1)
    grad_half = lax.dynamic_slice_in_dim(grad_out, own_part * half, half, axis=1)
    tok_send = tokens_half[token_of].reshape(peer_count, block_rows, half)
    grad_send = grad_half[token_of].reshape(peer_count, block_rows, half)

    def join_halves(mine):
        both = jnp.broadcast_to(mine[None], (2,) + mine.shape)
        return lax.all_to_all(both, "core", split_axis=0, concat_axis=0, tiled=True)

    def by_expert(values):
        shaped = values.reshape((peer_count, local_count, per_peer) + values.shape[2:])
        return jnp.swapaxes(shaped, 0, 1).reshape(
            (local_count, peer_count * per_peer) + values.shape[2:]
        )

    def by_peer(values):
        shaped = values.reshape((local_count, peer_count, per_peer) + values.shape[2:])
        return jnp.swapaxes(shaped, 0, 1).reshape((peer_count, block_rows) + values.shape[2:])

    tok_recv, grad_recv = exchange_rows(tok_send, grad_send, seq_count, lax.axis_size("tx"))
    weight_send, tok_recv = lax.optimization_barrier((weight_send, tok_recv))
    weight_recv = lax.all_to_all(
        weight_send, ("expert", "seq"), split_axis=0, concat_axis=0, tiled=True
    )
    in_rows = jax.vmap(by_expert)(tok_recv)
    out_rows = jax.vmap(by_expert)(grad_recv)
    prob = by_expert(weight_recv).astype(jnp.float32)[:, :, None]
    weights = lax.all_gather(
        jnp.stack([gate_weight, up_weight, down_weight]), "seq", axis=2, tiled=True
    )
    gate_full, up_full, down_full = weights[0], weights[1], weights[2]
    hidden_count = gate_full.shape[2]
    gate_h, up_h, down_h = (
        w.reshape(local_count, tensor_count, half, hidden_count)
        for w in (gate_full, up_full, down_full)
    )
    pre_gate = jnp.einsum("cemd,ecdf->emf", in_rows, gate_h, preferred_element_type=jnp.float32)
    pre_up = jnp.einsum("cemd,ecdf->emf", in_rows, up_h, preferred_element_type=jnp.float32)
    sigmoid_gate = jax.nn.sigmoid(pre_gate)
    silu_gate = pre_gate * sigmoid_gate
    hidden = silu_gate * pre_up
    hidden_low = hidden.astype(jnp.bfloat16)
    back_proj = jnp.einsum("cemd,ecdf->emf", out_rows, down_h, preferred_element_type=jnp.float32)
    partial_scores = jnp.sum(hidden * back_proj, axis=2)
    scaled = (prob[None] * out_rows.astype(jnp.float32)).astype(jnp.bfloat16)
    hidden_grad = prob * back_proj
    up_grad = (hidden_grad * silu_gate).astype(jnp.bfloat16)
    gate_grad = (
        hidden_grad * pre_up * sigmoid_gate * (1.0 + pre_gate * (1.0 - sigmoid_gate))
    ).astype(jnp.bfloat16)
    gate_part = jnp.einsum("cemd,emf->ecdf", in_rows, gate_grad, preferred_element_type=jnp.float32)
    up_part = jnp.einsum("cemd,emf->ecdf", in_rows, up_grad, preferred_element_type=jnp.float32)
    down_part = jnp.einsum("cemd,emf->ecdf", scaled, hidden_low, preferred_element_type=jnp.float32)
    parts = jnp.stack([gate_part, up_part, down_part]).reshape(
        3, local_count, model_width, hidden_count
    ).astype(jnp.bfloat16)
    parts, gate_grad, up_grad = lax.optimization_barrier((parts, gate_grad, up_grad))
    reduced_parts = lax.psum_scatter(parts, "seq", scatter_dimension=2, tiled=True)
    grad_gate, grad_up, grad_down = (reduced_parts[w].astype(jnp.float32) for w in range(3))
    score_pad = 16
    gate_p, up_p = (
        jnp.pad(w, ((0, 0), (0, 0), (0, score_pad), (0, 0))) for w in (gate_h, up_h)
    )
    input_terms = jnp.einsum(
        "emf,ecdf->ecdm", gate_grad, gate_p, preferred_element_type=jnp.float32
    )
    input_terms = input_terms + jnp.einsum(
        "emf,ecdf->ecdm", up_grad, up_p, preferred_element_type=jnp.float32
    )
    input_terms = input_terms.at[:, :, part_width, :].set(partial_scores[:, None, :])
    rows_here = local_count * slot_count
    stacked = jnp.swapaxes(
        input_terms.reshape(local_count, tensor_count, part_width + score_pad, slot_count), 0, 1
    ).reshape(tensor_count, part_width + score_pad, rows_here).astype(jnp.bfloat16)
    tx_count = lax.axis_size("tx")
    stacked = stacked.reshape(tx_count, 2, part_width + score_pad, rows_here)
    pair = lax.all_to_all(stacked, "core", split_axis=1, concat_axis=1, tiled=True)
    pair = jnp.sum(pair.astype(jnp.float32), axis=1).astype(jnp.bfloat16)
    ring = lax.all_to_all(pair, "tx", split_axis=0, concat_axis=0, tiled=True)
    reduced = jnp.sum(ring.astype(jnp.float32), axis=0).astype(jnp.bfloat16)
    back_send = by_peer(
        jnp.swapaxes(reduced, 0, 1).reshape(local_count, slot_count, part_width + score_pad)
    )
    back_all = lax.all_to_all(
        back_send, ("expert", "seq"), split_axis=0, concat_axis=0, tiled=True
    ).astype(jnp.float32)
    back_all = back_all.reshape(slot_count, part_width + score_pad)[target]
    route_rows = back_all[:, :part_width].reshape(tok_rows, 2, part_width)
    grad_tokens = jnp.sum(route_rows, axis=1).astype(jnp.bfloat16)
    grad_route = back_all[:, part_width].reshape(tok_rows, 2)
    return (grad_tokens, grad_route, grad_gate, grad_up, grad_down)


def solution(mesh):
    shape = mesh.devices.shape
    mesh = jax.sharding.Mesh(
        mesh.devices.reshape(shape[0], shape[1], shape[2] // 2, 2), ("expert", "seq", "tx", "core")
    )
    tensor = ("tx", "core")
    placed = (
        P(("expert", "seq"), None),
        P(("expert", "seq"), None),
        P(("expert", "seq"), None),
        P(("expert", "seq"), None),
        P("expert", "seq", tensor),
        P("expert", "seq", tensor),
        P("expert", "seq", tensor),
    )
    return jax.shard_map(
        shards,
        mesh=mesh,
        in_specs=placed,
        out_specs=(
            P(("expert", "seq"), tensor),
            P(("expert", "seq"), None),
            P("expert", "seq", tensor),
            P("expert", "seq", tensor),
            P("expert", "seq", tensor),
        ),
        check_vma=False,
    )
```

```python
import functools

import jax
import jax.numpy as jnp
from jax import lax
from jax.experimental import pallas as pl
from jax.experimental.pallas import tpu as pltpu
from jax.sharding import PartitionSpec as P

MESH = pl.DeviceIdType.MESH


def exchange_kernel(
    n_seq, n_tx, peers, tok_send, grad_send, tok_out, grad_out, send_sem, recv_sem, local_sem
):
    sends = (tok_send, grad_send)
    outs = (tok_out, grad_out)
    e = lax.axis_index("expert")
    s = lax.axis_index("seq")
    x = lax.axis_index("tx")
    c = lax.axis_index("core")
    me = e * n_seq + s
    other = 1 - c
    x_left = lax.rem(x + n_tx - 1, n_tx)
    x_right = lax.rem(x + 1, n_tx)
    x_far = lax.rem(x + 2, n_tx)
    own = x * 2 + c
    from_left = x_left * 2 + c
    from_right = x_right * 2 + c
    from_far = x_far * 2 + c
    left = (e, s, x_left, c)
    right = (e, s, x_right, c)
    partner = (e, s, x, other)

    def peer(k):
        q = lax.rem(me + k, peers)
        return q, (q // n_seq, q % n_seq, x, c)

    barrier = pltpu.get_barrier_semaphore()
    for k in range(1, peers):
        pl.semaphore_signal(barrier, inc=1, device_id=peer(k)[1], device_id_type=MESH)
    for where in (left, right, partner):
        pl.semaphore_signal(barrier, inc=1, device_id=where, device_id_type=MESH)
    pl.semaphore_wait(barrier, peers + 2)

    def remote(kind, src, dst, slot, recv, where):
        return pltpu.make_async_remote_copy(
            src_ref=src,
            dst_ref=dst,
            send_sem=send_sem.at[kind, slot],
            recv_sem=recv_sem.at[kind, recv],
            device_id=where,
            device_id_type=MESH,
        )

    locals_ = [
        pltpu.make_async_copy(sends[kind].at[me], outs[kind].at[own, me], local_sem.at[kind])
        for kind in range(2)
    ]
    for copy in locals_:
        copy.start()
    for k in range(1, peers):
        q, where = peer(k)
        for kind in range(2):
            remote(
                kind, sends[kind].at[q], outs[kind].at[own, me], q, own * peers + me, where
            ).start()

    def arrived(chunk, p):
        for kind in range(2):
            block = outs[kind].at[chunk, p]
            remote(kind, block, block, 0, chunk * peers + p, partner).wait_recv()

    def forward(chunk, p, slot, where):
        for kind in range(2):
            block = outs[kind].at[chunk, p]
            remote(kind, block, block, slot, chunk * peers + p, where).start()

    for copy in locals_:
        copy.wait()
    for k in range(peers):
        p = peer(k)[0]
        if k > 0:
            arrived(own, p)
        forward(own, p, peers + p, right)
        forward(own, p, 2 * peers + p, left)
        forward(own, p, 3 * peers + p, partner)

    def relay(chunk, onward, onward_parity, base):
        def body(i, carry):
            for parity in (0, 1):
                p = 2 * i + parity
                arrived(chunk, p)
                if onward is not None and parity == onward_parity:
                    forward(chunk, p, base + peers + p, onward)
                forward(chunk, p, base + p, partner)
            return carry

        lax.fori_loop(0, peers // 2, body, 0)

    relay(from_left, right, 0, 4 * peers)
    relay(from_right, left, 1, 6 * peers)
    relay(from_far, None, 0, 8 * peers)

    def partner_chunks(p, carry):
        for column in range(n_tx):
            arrived(column * 2 + other, p)
        return carry

    lax.fori_loop(0, peers, partner_chunks, 0)

    def drain(slot, carry):
        for kind in range(2):
            block = outs[kind].at[own, 0]
            remote(kind, block, block, slot, 0, partner).wait_send()
        return carry

    def drain_pairs(first, parity):
        def body(i, carry):
            return drain(first + 2 * i + parity, carry)

        lax.fori_loop(0, peers // 2, body, 0)

    for k in range(1, peers):
        drain(peer(k)[0], 0)
    lax.fori_loop(peers, 5 * peers, drain, 0)
    drain_pairs(5 * peers, 0)
    lax.fori_loop(6 * peers, 7 * peers, drain, 0)
    drain_pairs(7 * peers, 1)
    lax.fori_loop(8 * peers, 9 * peers, drain, 0)


def exchange_rows(tok_send, grad_send, n_seq, n_tx):
    peers = tok_send.shape[0]
    chunks = 2 * n_tx
    shape = jax.ShapeDtypeStruct((chunks,) + tok_send.shape, tok_send.dtype)
    return pl.pallas_call(
        functools.partial(exchange_kernel, n_seq, n_tx, peers),
        out_shape=(shape, shape),
        in_specs=[pl.BlockSpec(memory_space=pl.ANY)] * 2,
        out_specs=(pl.BlockSpec(memory_space=pl.ANY), pl.BlockSpec(memory_space=pl.ANY)),
        scratch_shapes=[
            pltpu.SemaphoreType.DMA((2, 9 * peers)),
            pltpu.SemaphoreType.DMA((2, chunks * peers)),
            pltpu.SemaphoreType.DMA((2,)),
        ],
        compiler_params=pltpu.CompilerParams(collective_id=0, has_side_effects=True),
    )(tok_send, grad_send)


def shards(tokens, grad_out, expert_ids, route_weights, gate_weight, up_weight, down_weight):
    expert_count = lax.axis_size("expert")
    seq_count = lax.axis_size("seq")
    tensor_count = lax.axis_size("tx") * lax.axis_size("core")
    core = lax.axis_index("core")
    local_count = gate_weight.shape[0]
    tok_rows = tokens.shape[0]
    model_width = tokens.shape[1]
    part_width = model_width // tensor_count
    per_peer = tok_rows // 6
    peer_count = expert_count * seq_count
    block_rows = local_count * per_peer
    slot_count = peer_count * block_rows
    flat_ids = expert_ids.reshape(-1)
    route_count = flat_ids.shape[0]
    onehot = (
        flat_ids[:, None] == jnp.arange(local_count * expert_count, dtype=jnp.int32)[None, :]
    ).astype(jnp.int32)
    before = jnp.cumsum(onehot, axis=0) - onehot
    ranking = jnp.sum(before * onehot, axis=1)
    local_expert = flat_ids % local_count
    dest_peer = flat_ids // local_count * seq_count + ranking % seq_count
    target = (dest_peer * local_count + local_expert) * per_peer + ranking // seq_count
    source = (
        jnp.full((slot_count,), -1, jnp.int32)
        .at[target]
        .set(jnp.arange(route_count, dtype=jnp.int32))
    )
    filled = source >= 0
    safe_source = jnp.maximum(source, 0)
    token_of = safe_source // 2
    weight_send = (
        route_weights.reshape(-1)[safe_source] * filled.astype(route_weights.dtype)
    ).reshape(peer_count, block_rows)
    own_part = lax.axis_index("tx") * 2 + core
    half = part_width
    tokens_half = lax.dynamic_slice_in_dim(tokens, own_part * half, half, axis=1)
    grad_half = lax.dynamic_slice_in_dim(grad_out, own_part * half, half, axis=1)
    tok_send = tokens_half[token_of].reshape(peer_count, block_rows, half)
    grad_send = grad_half[token_of].reshape(peer_count, block_rows, half)

    def join_halves(mine):
        both = jnp.broadcast_to(mine[None], (2,) + mine.shape)
        return lax.all_to_all(both, "core", split_axis=0, concat_axis=0, tiled=True)

    def by_expert(values):
        shaped = values.reshape((peer_count, local_count, per_peer) + values.shape[2:])
        return jnp.swapaxes(shaped, 0, 1).reshape(
            (local_count, peer_count * per_peer) + values.shape[2:]
        )

    def by_peer(values):
        shaped = values.reshape((local_count, peer_count, per_peer) + values.shape[2:])
        return jnp.swapaxes(shaped, 0, 1).reshape((peer_count, block_rows) + values.shape[2:])

    tok_recv, grad_recv = exchange_rows(tok_send, grad_send, seq_count, lax.axis_size("tx"))
    weight_send, tok_recv = lax.optimization_barrier((weight_send, tok_recv))
    weight_recv = lax.all_to_all(
        weight_send, ("expert", "seq"), split_axis=0, concat_axis=0, tiled=True
    )
    in_rows = jax.vmap(by_expert)(tok_recv)
    out_rows = jax.vmap(by_expert)(grad_recv)
    prob = by_expert(weight_recv).astype(jnp.float32)[:, :, None]
    weights = lax.all_gather(
        jnp.stack([gate_weight, up_weight, down_weight]), "seq", axis=2, tiled=True
    )
    gate_full, up_full, down_full = weights[0], weights[1], weights[2]
    hidden_count = gate_full.shape[2]
    gate_h, up_h, down_h = (
        w.reshape(local_count, tensor_count, half, hidden_count)
        for w in (gate_full, up_full, down_full)
    )
    pre_gate = jnp.einsum("cemd,ecdf->emf", in_rows, gate_h, preferred_element_type=jnp.float32)
    pre_up = jnp.einsum("cemd,ecdf->emf", in_rows, up_h, preferred_element_type=jnp.float32)
    sigmoid_gate = jax.nn.sigmoid(pre_gate)
    silu_gate = pre_gate * sigmoid_gate
    hidden = silu_gate * pre_up
    hidden_low = hidden.astype(jnp.bfloat16)
    back_proj = jnp.einsum("cemd,ecdf->emf", out_rows, down_h, preferred_element_type=jnp.float32)
    partial_scores = jnp.sum(hidden * back_proj, axis=2)
    scaled = (prob[None] * out_rows.astype(jnp.float32)).astype(jnp.bfloat16)
    hidden_grad = prob * back_proj
    up_grad = (hidden_grad * silu_gate).astype(jnp.bfloat16)
    gate_grad = (
        hidden_grad * pre_up * sigmoid_gate * (1.0 + pre_gate * (1.0 - sigmoid_gate))
    ).astype(jnp.bfloat16)
    gate_part = jnp.einsum("cemd,emf->ecdf", in_rows, gate_grad, preferred_element_type=jnp.float32)
    up_part = jnp.einsum("cemd,emf->ecdf", in_rows, up_grad, preferred_element_type=jnp.float32)
    down_part = jnp.einsum("cemd,emf->ecdf", scaled, hidden_low, preferred_element_type=jnp.float32)
    parts = jnp.stack([gate_part, up_part, down_part]).reshape(
        3, local_count, model_width, hidden_count
    ).astype(jnp.bfloat16)
    parts, gate_grad, up_grad = lax.optimization_barrier((parts, gate_grad, up_grad))
    reduced_parts = lax.psum_scatter(parts, "seq", scatter_dimension=2, tiled=True).astype(jnp.float32)
    grad_gate, grad_up, grad_down = reduced_parts[0], reduced_parts[1], reduced_parts[2]
    score_pad = 16
    gate_p, up_p = (
        jnp.pad(w, ((0, 0), (0, 0), (0, score_pad), (0, 0))) for w in (gate_h, up_h)
    )
    input_terms = jnp.einsum(
        "emf,ecdf->ecdm", gate_grad, gate_p, preferred_element_type=jnp.float32
    )
    input_terms = input_terms + jnp.einsum(
        "emf,ecdf->ecdm", up_grad, up_p, preferred_element_type=jnp.float32
    )
    input_terms = input_terms.at[:, :, part_width, :].set(partial_scores[:, None, :])
    rows_here = local_count * slot_count
    stacked = jnp.swapaxes(
        input_terms.reshape(local_count, tensor_count, part_width + score_pad, slot_count), 0, 1
    ).reshape(tensor_count, part_width + score_pad, rows_here).astype(jnp.bfloat16)
    tx_count = lax.axis_size("tx")
    stacked = stacked.reshape(tx_count, 2, part_width + score_pad, rows_here)
    pair = lax.all_to_all(stacked, "core", split_axis=1, concat_axis=1, tiled=True)
    pair = jnp.sum(pair.astype(jnp.float32), axis=1).astype(jnp.bfloat16)
    ring = lax.all_to_all(pair, "tx", split_axis=0, concat_axis=0, tiled=True)
    reduced = jnp.sum(ring.astype(jnp.float32), axis=0).astype(jnp.bfloat16)
    back_send = by_peer(
        jnp.swapaxes(reduced, 0, 1).reshape(local_count, slot_count, part_width + score_pad)
    )
    back_all = lax.all_to_all(
        back_send, ("expert", "seq"), split_axis=0, concat_axis=0, tiled=True
    ).astype(jnp.float32)
    back_all = back_all.reshape(slot_count, part_width + score_pad)
    pair_target = target.reshape(tok_rows, 2)
    first, second = back_all[pair_target[:, 0]], back_all[pair_target[:, 1]]
    grad_tokens = (first[:, :part_width] + second[:, :part_width]).astype(jnp.bfloat16)
    grad_route = jnp.stack([first[:, part_width], second[:, part_width]], axis=1)
    return (grad_tokens, grad_route, grad_gate, grad_up, grad_down)


def solution(mesh):
    shape = mesh.devices.shape
    mesh = jax.sharding.Mesh(
        mesh.devices.reshape(shape[0], shape[1], shape[2] // 2, 2), ("expert", "seq", "tx", "core")
    )
    tensor = ("tx", "core")
    placed = (
        P(("expert", "seq"), None),
        P(("expert", "seq"), None),
        P(("expert", "seq"), None),
        P(("expert", "seq"), None),
        P("expert", "seq", tensor),
        P("expert", "seq", tensor),
        P("expert", "seq", tensor),
    )
    return jax.shard_map(
        shards,
        mesh=mesh,
        in_specs=placed,
        out_specs=(
            P(("expert", "seq"), tensor),
            P(("expert", "seq"), None),
            P("expert", "seq", tensor),
            P("expert", "seq", tensor),
            P("expert", "seq", tensor),
        ),
        check_vma=False,
    )
```

```python
import functools

import jax
import jax.numpy as jnp
from jax import lax
from jax.experimental import pallas as pl
from jax.experimental.pallas import tpu as pltpu
from jax.sharding import PartitionSpec as P

MESH = pl.DeviceIdType.MESH


def exchange_kernel(
    n_seq, n_tx, peers, tok_send, grad_send, tok_out, grad_out, send_sem, recv_sem, local_sem
):
    sends = (tok_send, grad_send)
    outs = (tok_out, grad_out)
    e = lax.axis_index("expert")
    s = lax.axis_index("seq")
    x = lax.axis_index("tx")
    c = lax.axis_index("core")
    me = e * n_seq + s
    other = 1 - c
    x_left = lax.rem(x + n_tx - 1, n_tx)
    x_right = lax.rem(x + 1, n_tx)
    x_far = lax.rem(x + 2, n_tx)
    own = x * 2 + c
    from_left = x_left * 2 + c
    from_right = x_right * 2 + c
    from_far = x_far * 2 + c
    left = (e, s, x_left, c)
    right = (e, s, x_right, c)
    partner = (e, s, x, other)

    def peer(k):
        q = lax.rem(me + k, peers)
        return q, (q // n_seq, q % n_seq, x, c)

    barrier = pltpu.get_barrier_semaphore()
    for k in range(1, peers):
        pl.semaphore_signal(barrier, inc=1, device_id=peer(k)[1], device_id_type=MESH)
    for where in (left, right, partner):
        pl.semaphore_signal(barrier, inc=1, device_id=where, device_id_type=MESH)
    pl.semaphore_wait(barrier, peers + 2)

    def remote(kind, src, dst, slot, recv, where):
        return pltpu.make_async_remote_copy(
            src_ref=src,
            dst_ref=dst,
            send_sem=send_sem.at[kind, slot],
            recv_sem=recv_sem.at[kind, recv],
            device_id=where,
            device_id_type=MESH,
        )

    locals_ = [
        pltpu.make_async_copy(sends[kind].at[me], outs[kind].at[own, me], local_sem.at[kind])
        for kind in range(2)
    ]
    for copy in locals_:
        copy.start()
    for k in range(1, peers):
        q, where = peer(k)
        for kind in range(2):
            remote(
                kind, sends[kind].at[q], outs[kind].at[own, me], q, own * peers + me, where
            ).start()

    def arrived(chunk, p):
        for kind in range(2):
            block = outs[kind].at[chunk, p]
            remote(kind, block, block, 0, chunk * peers + p, partner).wait_recv()

    def forward(chunk, p, slot, where):
        for kind in range(2):
            block = outs[kind].at[chunk, p]
            remote(kind, block, block, slot, chunk * peers + p, where).start()

    for copy in locals_:
        copy.wait()
    for k in range(peers):
        p = peer(k)[0]
        if k > 0:
            arrived(own, p)
        forward(own, p, peers + p, right)
        forward(own, p, 2 * peers + p, left)
        forward(own, p, 3 * peers + p, partner)

    def relay(chunk, onward, onward_parity, base):
        def body(i, carry):
            for parity in (0, 1):
                p = 2 * i + parity
                arrived(chunk, p)
                if onward is not None and parity == onward_parity:
                    forward(chunk, p, base + peers + p, onward)
                forward(chunk, p, base + p, partner)
            return carry

        lax.fori_loop(0, peers // 2, body, 0)

    relay(from_left, right, 0, 4 * peers)
    relay(from_right, left, 1, 6 * peers)
    relay(from_far, None, 0, 8 * peers)

    def partner_chunks(p, carry):
        for column in range(n_tx):
            arrived(column * 2 + other, p)
        return carry

    lax.fori_loop(0, peers, partner_chunks, 0)

    def drain(slot, carry):
        for kind in range(2):
            block = outs[kind].at[own, 0]
            remote(kind, block, block, slot, 0, partner).wait_send()
        return carry

    def drain_pairs(first, parity):
        def body(i, carry):
            return drain(first + 2 * i + parity, carry)

        lax.fori_loop(0, peers // 2, body, 0)

    for k in range(1, peers):
        drain(peer(k)[0], 0)
    lax.fori_loop(peers, 5 * peers, drain, 0)
    drain_pairs(5 * peers, 0)
    lax.fori_loop(6 * peers, 7 * peers, drain, 0)
    drain_pairs(7 * peers, 1)
    lax.fori_loop(8 * peers, 9 * peers, drain, 0)


def exchange_rows(tok_send, grad_send, n_seq, n_tx):
    peers = tok_send.shape[0]
    chunks = 2 * n_tx
    shape = jax.ShapeDtypeStruct((chunks,) + tok_send.shape, tok_send.dtype)
    return pl.pallas_call(
        functools.partial(exchange_kernel, n_seq, n_tx, peers),
        out_shape=(shape, shape),
        in_specs=[pl.BlockSpec(memory_space=pl.ANY)] * 2,
        out_specs=(pl.BlockSpec(memory_space=pl.ANY), pl.BlockSpec(memory_space=pl.ANY)),
        scratch_shapes=[
            pltpu.SemaphoreType.DMA((2, 9 * peers)),
            pltpu.SemaphoreType.DMA((2, chunks * peers)),
            pltpu.SemaphoreType.DMA((2,)),
        ],
        compiler_params=pltpu.CompilerParams(collective_id=0, has_side_effects=True),
    )(tok_send, grad_send)


def shards(tokens, grad_out, expert_ids, route_weights, gate_weight, up_weight, down_weight):
    expert_count = lax.axis_size("expert")
    seq_count = lax.axis_size("seq")
    tensor_count = lax.axis_size("tx") * lax.axis_size("core")
    core = lax.axis_index("core")
    local_count = gate_weight.shape[0]
    tok_rows = tokens.shape[0]
    model_width = tokens.shape[1]
    part_width = model_width // tensor_count
    per_peer = tok_rows // 6
    peer_count = expert_count * seq_count
    block_rows = local_count * per_peer
    slot_count = peer_count * block_rows
    flat_ids = expert_ids.reshape(-1)
    route_count = flat_ids.shape[0]
    onehot = (
        flat_ids[:, None] == jnp.arange(local_count * expert_count, dtype=jnp.int32)[None, :]
    ).astype(jnp.int32)
    before = jnp.cumsum(onehot, axis=0) - onehot
    ranking = jnp.sum(before * onehot, axis=1)
    local_expert = flat_ids % local_count
    dest_peer = flat_ids // local_count * seq_count + ranking % seq_count
    target = (dest_peer * local_count + local_expert) * per_peer + ranking // seq_count
    source = (
        jnp.full((slot_count,), -1, jnp.int32)
        .at[target]
        .set(jnp.arange(route_count, dtype=jnp.int32))
    )
    filled = source >= 0
    safe_source = jnp.maximum(source, 0)
    token_of = safe_source // 2
    weight_send = (
        route_weights.reshape(-1)[safe_source] * filled.astype(route_weights.dtype)
    ).reshape(peer_count, block_rows)
    own_part = lax.axis_index("tx") * 2 + core
    half = part_width
    tokens_half = lax.dynamic_slice_in_dim(tokens, own_part * half, half, axis=1)
    grad_half = lax.dynamic_slice_in_dim(grad_out, own_part * half, half, axis=1)
    tok_send = tokens_half[token_of].reshape(peer_count, block_rows, half)
    grad_send = grad_half[token_of].reshape(peer_count, block_rows, half)

    def join_halves(mine):
        both = jnp.broadcast_to(mine[None], (2,) + mine.shape)
        return lax.all_to_all(both, "core", split_axis=0, concat_axis=0, tiled=True)

    def by_expert(values):
        shaped = values.reshape((peer_count, local_count, per_peer) + values.shape[2:])
        return jnp.swapaxes(shaped, 0, 1).reshape(
            (local_count, peer_count * per_peer) + values.shape[2:]
        )

    def by_peer(values):
        shaped = values.reshape((local_count, peer_count, per_peer) + values.shape[2:])
        return jnp.swapaxes(shaped, 0, 1).reshape((peer_count, block_rows) + values.shape[2:])

    tok_recv, grad_recv = exchange_rows(tok_send, grad_send, seq_count, lax.axis_size("tx"))
    weight_send, tok_recv = lax.optimization_barrier((weight_send, tok_recv))
    weight_recv = lax.all_to_all(
        weight_send, ("expert", "seq"), split_axis=0, concat_axis=0, tiled=True
    )
    in_rows = jax.vmap(by_expert)(tok_recv)
    out_rows = jax.vmap(by_expert)(grad_recv)
    prob = by_expert(weight_recv).astype(jnp.float32)[:, :, None]
    weights = lax.all_gather(
        jnp.stack([gate_weight, up_weight, down_weight]), "seq", axis=2, tiled=True
    )
    gate_full, up_full, down_full = weights[0], weights[1], weights[2]
    hidden_count = gate_full.shape[2]
    gate_h, up_h, down_h = (
        w.reshape(local_count, tensor_count, half, hidden_count)
        for w in (gate_full, up_full, down_full)
    )
    pre_gate = jnp.einsum("cemd,ecdf->emf", in_rows, gate_h, preferred_element_type=jnp.float32)
    pre_up = jnp.einsum("cemd,ecdf->emf", in_rows, up_h, preferred_element_type=jnp.float32)
    sigmoid_gate = jax.nn.sigmoid(pre_gate)
    silu_gate = pre_gate * sigmoid_gate
    hidden = silu_gate * pre_up
    hidden_low = hidden.astype(jnp.bfloat16)
    back_proj = jnp.einsum("cemd,ecdf->emf", out_rows, down_h, preferred_element_type=jnp.float32)
    partial_scores = jnp.sum(hidden * back_proj, axis=2)
    scaled = (prob[None] * out_rows.astype(jnp.float32)).astype(jnp.bfloat16)
    hidden_grad = prob * back_proj
    up_grad = (hidden_grad * silu_gate).astype(jnp.bfloat16)
    gate_grad = (
        hidden_grad * pre_up * sigmoid_gate * (1.0 + pre_gate * (1.0 - sigmoid_gate))
    ).astype(jnp.bfloat16)
    gate_part = jnp.einsum("cemd,emf->ecdf", in_rows, gate_grad, preferred_element_type=jnp.float32)
    up_part = jnp.einsum("cemd,emf->ecdf", in_rows, up_grad, preferred_element_type=jnp.float32)
    down_part = jnp.einsum("cemd,emf->ecdf", scaled, hidden_low, preferred_element_type=jnp.float32)
    parts = jnp.stack([gate_part, up_part, down_part]).reshape(
        3, local_count, model_width, hidden_count
    ).astype(jnp.bfloat16)
    parts, gate_grad, up_grad = lax.optimization_barrier((parts, gate_grad, up_grad))
    reduced_parts = lax.psum_scatter(parts, "seq", scatter_dimension=2, tiled=True)
    grad_gate, grad_up, grad_down = (reduced_parts[w].astype(jnp.float32) for w in range(3))
    score_pad = 16
    gate_p, up_p = (
        jnp.pad(w, ((0, 0), (0, 0), (0, score_pad), (0, 0))) for w in (gate_h, up_h)
    )
    input_terms = jnp.einsum(
        "emf,ecdf->ecdm", gate_grad, gate_p, preferred_element_type=jnp.float32
    )
    input_terms = input_terms + jnp.einsum(
        "emf,ecdf->ecdm", up_grad, up_p, preferred_element_type=jnp.float32
    )
    input_terms = input_terms.at[:, :, part_width, :].set(partial_scores[:, None, :])
    rows_here = local_count * slot_count
    stacked = jnp.swapaxes(
        input_terms.reshape(local_count, tensor_count, part_width + score_pad, slot_count), 0, 1
    ).reshape(tensor_count, part_width + score_pad, rows_here).astype(jnp.bfloat16)
    tx_count = lax.axis_size("tx")
    stacked = stacked.reshape(tx_count, 2, part_width + score_pad, rows_here)
    pair = lax.all_to_all(stacked, "core", split_axis=1, concat_axis=1, tiled=True)
    pair = jnp.sum(pair.astype(jnp.float32), axis=1).astype(jnp.bfloat16)
    ring = lax.all_to_all(pair, "tx", split_axis=0, concat_axis=0, tiled=True)
    reduced = jnp.sum(ring.astype(jnp.float32), axis=0).astype(jnp.bfloat16)
    back_send = by_peer(
        jnp.swapaxes(reduced, 0, 1).reshape(local_count, slot_count, part_width + score_pad)
    )
    back_all = lax.all_to_all(
        back_send, ("expert", "seq"), split_axis=0, concat_axis=0, tiled=True
    ).astype(jnp.float32)
    back_all = back_all.reshape(slot_count, part_width + score_pad)
    pair_target = target.reshape(tok_rows, 2)
    first, second = back_all[pair_target[:, 0]], back_all[pair_target[:, 1]]
    grad_tokens = (first[:, :part_width] + second[:, :part_width]).astype(jnp.bfloat16)
    grad_route = jnp.stack([first[:, part_width], second[:, part_width]], axis=1)
    return (grad_tokens, grad_route, grad_gate, grad_up, grad_down)


def solution(mesh):
    shape = mesh.devices.shape
    mesh = jax.sharding.Mesh(
        mesh.devices.reshape(shape[0], shape[1], shape[2] // 2, 2), ("expert", "seq", "tx", "core")
    )
    tensor = ("tx", "core")
    placed = (
        P(("expert", "seq"), None),
        P(("expert", "seq"), None),
        P(("expert", "seq"), None),
        P(("expert", "seq"), None),
        P("expert", "seq", tensor),
        P("expert", "seq", tensor),
        P("expert", "seq", tensor),
    )
    return jax.shard_map(
        shards,
        mesh=mesh,
        in_specs=placed,
        out_specs=(
            P(("expert", "seq"), tensor),
            P(("expert", "seq"), None),
            P("expert", "seq", tensor),
            P("expert", "seq", tensor),
            P("expert", "seq", tensor),
        ),
        check_vma=False,
    )
```
